32 devices in a mesh: dp: 4 (over y, core), lat: 8 (over z, x).
Axes of the slice: x: 2, y: 2, z: 4, core: 2. Of those that a mesh axis runs over, the one named last changes fastest.
Arguments:
- inputs: bfloat16 [4, 96, 180, 768], P('dp', 'lat'), may hold values from -6 to 6
- cotangent: bfloat16 [4, 96, 180, 768], P('dp', 'lat'), may hold values from -6 to 6
- storm_weight: int32 [4], P('dp'), may hold values from 32 to 192
- norm_gain: float32 [768], replicated, may hold values from 0.5 to 1.5
- norm_shift: float32 [768], replicated, may hold values from -1 to 1
- inner_weight: bfloat16 [2, 8, 96, 96], replicated, may hold values from -0.4375 to 0.4375
- inner_bias: float32 [2, 8, 96], replicated, may hold values from -0.1 to 0.1
- outer_weight: bfloat16 [2, 8, 96, 96], replicated, may hold values from -0.4375 to 0.4375
- outer_bias: float32 [2, 8, 96], replicated, may hold values from -0.05 to 0.05
- post_gain: float32 [768], replicated, may hold values from 0.5 to 1.5
- post_shift: float32 [768], replicated, may hold values from -1 to 1
- expand_weight: bfloat16 [768, 3072], replicated, may hold values from -0.21875 to 0.21875
- expand_bias: float32 [3072], replicated, may hold values from -0.5 to 0.5
- reduce_weight: bfloat16 [3072, 768], replicated, may hold values from -0.109375 to 0.109375
- reduce_bias: float32 [768], replicated, may hold values from -0.5 to 0.5
Outputs:
- layer_out: bfloat16 [4, 96, 180, 768], P('dp', 'lat')
- input_grad: float32 [4, 96, 180, 768], P('dp', 'lat')
- norm_gain_grad: float32 [768], replicated
- norm_shift_grad: float32 [768], replicated
- inner_weight_grad: float32 [2, 8, 96, 96], replicated
- inner_bias_grad: float32 [2, 8, 96], replicated
- outer_weight_grad: float32 [2, 8, 96, 96], replicated
- outer_bias_grad: float32 [2, 8, 96], replicated
- post_gain_grad: float32 [768], replicated
- post_shift_grad: float32 [768], replicated
- expand_weight_grad: float32 [768, 3072], replicated
- expand_bias_grad: float32 [3072], replicated
- reduce_weight_grad: float32 [3072, 768], replicated
- reduce_bias_grad: float32 [768], replicated
The draws below stay inside these ranges and needn't reach their ends.
All inputs are finite; a program needn't handle non-finite values.
Results may differ from the reference program's by a relative error of at most 0.017.
The reference program's roundings to bfloat16 on the way count: a program that leaves them out, or rounds other values in their place, can miss the bound.
Values may be sent and summed in bfloat16 or wider, within the bound.
A program may use at most 320 MiB of HBM per device.

```python
import math
import jax
import jax.numpy as jnp
from jax import lax

C = 768
BLOCKS = 8
BLOCK = 96
FF = 3072
LAT = 90
LON = 180
LAT_PAD = 96
LON_PAD = 96
SAMPLES = 4


def plant(entries, rng, smallest, largest):
    longest = entries.shape.index(max(entries.shape))
    spots = []
    for shift in (0, 1):
        where = [jax.random.randint(jax.random.fold_in(rng, axis), (), 0, length) for axis, length in enumerate(entries.shape)]
        where[longest] = (where[longest] + shift) % entries.shape[longest]
        spots.append(tuple(where))
    return entries.at[spots[0]].set(smallest).at[spots[1]].set(largest)


def levels(rng, dims, pieces, low, largest):
    level, own = 1.0, jax.random.fold_in(rng, 6)
    for position, blocks in pieces:
        steps = jnp.exp(jax.random.uniform(jax.random.fold_in(own, position), (blocks,), jnp.float32, low / len(pieces), largest / len(pieces)))
        level = level * jnp.repeat(steps, dims[position] // blocks).reshape([-1 if axis == position else 1 for axis in range(len(dims))])
    return level


def centred(own_key, extent, scale, limit, split=(), held_as=jnp.bfloat16):
    level = levels(own_key, extent, split, -0.22, 0.18) if split else 1.0
    values = jax.random.normal(own_key, extent, jnp.float32) * scale * level
    return jnp.minimum(jnp.maximum(values, -limit), limit).astype(held_as)


def setup_inputs(seed: int = 0) -> dict:
    streams_of = jax.random.split(jax.random.key(seed), 16)
    inputs = centred(streams_of[0], (SAMPLES, LAT_PAD, LON, C), 1.0, 6.0, ((0, 4), (1, 8)))
    cotangent = centred(streams_of[1], (SAMPLES, LAT_PAD, LON, C), 1.0, 6.0, ((0, 4), (1, 8)))
    storm_weight = plant(jax.random.randint(streams_of[2], (SAMPLES,), 32, 193), jax.random.fold_in(streams_of[2], 1), 32, 192).astype(jnp.int32)
    norm_gain = jnp.clip(1.0 + 0.1 * jax.random.normal(streams_of[3], (C,), jnp.float32), 0.5, 1.5)
    norm_shift = centred(streams_of[4], (C,), 0.2, 1.0, (), jnp.float32)
    inner_weight = centred(streams_of[5], (2, BLOCKS, BLOCK, BLOCK), (2 * BLOCK) ** -0.5, 0.4375)
    inner_bias = centred(streams_of[6], (2, BLOCKS, BLOCK), 0.02, 0.1, (), jnp.float32)
    outer_weight = centred(streams_of[7], (2, BLOCKS, BLOCK, BLOCK), (2 * BLOCK) ** -0.5, 0.4375)
    outer_bias = centred(streams_of[8], (2, BLOCKS, BLOCK), 0.01, 0.05, (), jnp.float32)
    post_gain = jnp.clip(1.0 + 0.1 * jax.random.normal(streams_of[9], (C,), jnp.float32), 0.5, 1.5)
    post_shift = centred(streams_of[10], (C,), 0.2, 1.0, (), jnp.float32)
    expand_weight = centred(streams_of[11], (C, FF), C ** -0.5, 0.21875)
    expand_bias = centred(streams_of[12], (FF,), 0.1, 0.5, (), jnp.float32)
    reduce_weight = centred(streams_of[13], (FF, C), FF ** -0.5, 0.109375)
    reduce_bias = centred(streams_of[14], (C,), 0.1, 0.5, (), jnp.float32)
    return dict(inputs=inputs, cotangent=cotangent, storm_weight=storm_weight, norm_gain=norm_gain, norm_shift=norm_shift, inner_weight=inner_weight, inner_bias=inner_bias, outer_weight=outer_weight, outer_bias=outer_bias, post_gain=post_gain, post_shift=post_shift, expand_weight=expand_weight, expand_bias=expand_bias, reduce_weight=reduce_weight, reduce_bias=reduce_bias)


shrink_level = 0.01
epsilon = 1e-06

@jax.custom_vjp
def low(v):
    return lax.optimization_barrier(v.astype(jnp.bfloat16)).astype(jnp.float32)

@jax.custom_vjp
def low_back(v):
    return v

def low_keep(v):
    return (low(v), None)

def low_pass(kept, grad):
    return (grad,)

def back_keep(v):
    return (v, None)

def back_low(kept, grad):
    return (low(grad),)
low.defvjp(low_keep, low_pass)
low_back.defvjp(back_keep, back_low)

def spectral_tables():
    mode_ids = jnp.arange(LON_PAD, dtype=jnp.int32)
    columns = jnp.arange(LON, dtype=jnp.int32)
    phases = (columns[:, None] * mode_ids[None, :] % LON).astype(jnp.float32) * (2.0 * math.pi / LON)
    kept_modes = (mode_ids < LON // 2 + 1).astype(jnp.float32)
    factor = jnp.where((mode_ids == 0) | (mode_ids == LON // 2), 1.0, 2.0).astype(jnp.float32) * kept_modes
    scaling = 1.0 / math.sqrt(LON)
    forward_lon = jnp.stack([jnp.cos(phases) * kept_modes, -jnp.sin(phases) * kept_modes], axis=1) * scaling
    inverse_lon = jnp.stack([jnp.cos(phases) * factor, -jnp.sin(phases) * factor], axis=1) * scaling
    row_ids = jnp.arange(LAT_PAD, dtype=jnp.int32)
    angles = (row_ids[:, None] * row_ids[None, :] % LAT).astype(jnp.float32) * (2.0 * math.pi / LAT)
    inside = ((row_ids[:, None] < LAT) & (row_ids[None, :] < LAT)).astype(jnp.float32) / math.sqrt(LAT)
    cosine = jnp.cos(angles) * inside
    sine_part = jnp.sin(angles) * inside
    forward_lat = jnp.stack([jnp.stack([cosine, sine_part], axis=1), jnp.stack([-sine_part, cosine], axis=1)], axis=0)
    inverse_lat = jnp.stack([jnp.stack([cosine, -sine_part], axis=1), jnp.stack([sine_part, cosine], axis=1)], axis=0)
    return (forward_lon, inverse_lon, forward_lat, inverse_lat)

def layer_norm(values, gain, shift):
    center = lax.optimization_barrier(jnp.mean(values, axis=-1, keepdims=True))
    spread = lax.optimization_barrier(jnp.mean(jnp.square(values - center), axis=-1, keepdims=True))
    return (values - center) * lax.rsqrt(spread + epsilon) * gain + shift

def soft_shrink(values):
    return values - shrink_level * jnp.tanh(values / shrink_level)

def gelu_exact(values):
    return jax.nn.gelu(values, approximate=False)

def complex_mix(real, imag, weight, bias):
    highest = lax.Precision.HIGHEST

    def product(left, right):
        return jnp.einsum('kmbi,bio->kmbo', left, right, precision=highest)
    return (product(real, weight[0]) - product(imag, weight[1]) + bias[0], product(imag, weight[0]) + product(real, weight[1]) + bias[1])

def forward(sample, params, tables):
    norm_gain, norm_shift, inner_weight, inner_bias, outer_weight, outer_bias, post_gain, post_shift, expand_weight, expand_bias, reduce_weight, reduce_bias = params
    forward_lon, inverse_lon, forward_lat, inverse_lat = tables
    highest = lax.Precision.HIGHEST
    width = sample.shape[-1]
    row_keep = (jnp.arange(LAT_PAD, dtype=jnp.int32) < LAT).astype(jnp.float32)
    first = layer_norm(sample, norm_gain, norm_shift)
    lon_spec = low_back(low(jnp.einsum('rwc,wqm->rqmc', low(first), forward_lon, precision=highest)))
    freq = low_back(low(jnp.einsum('qkpr,rpmc->kqmc', forward_lat, lon_spec, precision=highest)))
    block_shape = (LAT_PAD, LON_PAD, BLOCKS, width // BLOCKS)
    freq_re = freq[:, 0].reshape(block_shape)
    freq_im = freq[:, 1].reshape(block_shape)
    inner_re, inner_im = complex_mix(freq_re, freq_im, inner_weight, inner_bias)
    hidden_re = low(gelu_exact(low_back(inner_re)))
    hidden_im = low(gelu_exact(low_back(inner_im)))
    outer_re, outer_im = complex_mix(hidden_re, hidden_im, outer_weight, outer_bias)
    shrunk = jnp.stack([low(soft_shrink(low_back(outer_re))).reshape(LAT_PAD, LON_PAD, width), low(soft_shrink(low_back(outer_im))).reshape(LAT_PAD, LON_PAD, width)], axis=1)
    back_spec = low_back(low(jnp.einsum('qrpk,kpmc->rqmc', inverse_lat, shrunk, precision=highest)))
    filtered = low_back(jnp.einsum('wqm,rqmc->rwc', inverse_lon, back_spec, precision=highest))
    mixed = filtered + first + sample
    second = low(layer_norm(mixed, post_gain, post_shift)).reshape(-1, width)
    pre_act = low_back(jnp.dot(second, expand_weight, precision=highest) + expand_bias)
    activ = low(gelu_exact(pre_act))
    branch = low_back(jnp.dot(activ, reduce_weight, precision=highest) + reduce_bias)
    return (mixed + branch.reshape(mixed.shape)) * row_keep[:, None, None]

def reference(inputs, cotangent, storm_weight, norm_gain, norm_shift, inner_weight, inner_bias, outer_weight, outer_bias, post_gain, post_shift, expand_weight, expand_bias, reduce_weight, reduce_bias):
    params = tuple((p.astype(jnp.float32) for p in (norm_gain, norm_shift, inner_weight, inner_bias, outer_weight, outer_bias, post_gain, post_shift, expand_weight, expand_bias, reduce_weight, reduce_bias)))
    tables = tuple((low(t) for t in spectral_tables()))

    def one_sample(totals, item):
        sample, cot_sample, weight_sample = item
        result, pull = jax.vjp(lambda s, p: forward(s, p, tables), sample.astype(jnp.float32), params)
        sample_grad, param_grads = pull(cot_sample.astype(jnp.float32) * (weight_sample.astype(jnp.float32) / 64.0))
        totals = jax.tree.map(lambda a, b: a + b, totals, param_grads)
        return (totals, (result.astype(jnp.bfloat16), sample_grad))
    zero_grads = tuple((jnp.zeros_like(p) for p in params))
    totals, (layer_out, input_grad) = lax.scan(one_sample, zero_grads, (inputs, cotangent, storm_weight))
    return (layer_out, input_grad, totals[0], totals[1], totals[2], totals[3], totals[4], totals[5], totals[6], totals[7], totals[8], totals[9], totals[10], totals[11])
```

```python
import functools
import math

import jax
import jax.numpy as jnp
import ml_dtypes
import numpy as np
from jax import lax
from jax.experimental import pallas as pl
from jax.experimental.pallas import tpu as pltpu
from jax.sharding import PartitionSpec as P

BLOCKS = 8
LAT = 90
LON = 180
LAT_PAD = 96
LON_PAD = 96
COLS = 192
GROUPS = 2
LANES = 128

SHRINK = 0.01
EPS = 1e-6
SQRT_HALF = 0.7071067811865476
PDF_SCALE = 0.3989422804014327

F32 = jnp.float32
BF16 = jnp.bfloat16
MESH = pl.DeviceIdType.MESH
VMEM_LIMIT = 62 * 2**20


def base_tables():
    f = np.float32
    modes = np.arange(LON_PAD)
    columns = np.arange(LON)
    phases = (columns[:, None] * modes[None, :] % LON).astype(f) * f(2.0 * math.pi / LON)
    kept = (modes < LON // 2 + 1).astype(f)
    factor = np.where((modes == 0) | (modes == LON // 2), f(1), f(2)) * kept
    scale = f(1.0 / math.sqrt(LON))
    forward_lon = np.stack([np.cos(phases) * kept, -np.sin(phases) * kept], axis=1) * scale
    inverse_lon = np.stack([np.cos(phases) * factor, -np.sin(phases) * factor], axis=1) * scale
    rows = np.arange(LAT_PAD)
    angles = (rows[:, None] * rows[None, :] % LAT).astype(f) * f(2.0 * math.pi / LAT)
    inside = ((rows[:, None] < LAT) & (rows[None, :] < LAT)).astype(f) / f(math.sqrt(LAT))
    cs = np.cos(angles) * inside
    sn = np.sin(angles) * inside
    forward_lat = np.stack([np.stack([cs, sn], 1), np.stack([-sn, cs], 1)], 0)
    inverse_lat = np.stack([np.stack([cs, -sn], 1), np.stack([sn, cs], 1)], 0)
    return forward_lon, inverse_lon, forward_lat, inverse_lat


def slab_rows(modes):
    return -(-2 * modes // 8) * 8


def lon_table(table, shards, modes):
    slab = slab_rows(modes)
    out = np.zeros((COLS, shards, slab), np.float32)
    split = table.reshape(LON, 2, shards, modes).transpose(0, 2, 3, 1)
    out[:LON, :, : 2 * modes] = split.reshape(LON, shards, 2 * modes)
    return out.reshape(COLS, shards * slab)


def make_tables(shards, modes):
    forward_lon, inverse_lon, forward_lat, inverse_lat = base_tables()
    low = lambda t: jnp.asarray(np.ascontiguousarray(t).astype(ml_dtypes.bfloat16))
    n = 2 * LAT_PAD
    fl = lon_table(forward_lon, shards, modes)
    il = lon_table(inverse_lon, shards, modes)
    fa = forward_lat.reshape(n, n)
    ia = inverse_lat.reshape(n, n)
    return dict(
        fl=low(fl), flt=low(fl.T), il=low(il), ilt=low(il.T),
        fa=low(fa), fat=low(fa.T), ia=low(ia), iat=low(ia.T),
    )


def dot(a, b):
    return jnp.dot(a, b, preferred_element_type=F32)


def dot_nt(a, b):
    return lax.dot_general(a, b, (((1,), (1,)), ((), ())), preferred_element_type=F32)


def dot_tn(a, b):
    return lax.dot_general(a, b, (((0,), (0,)), ((), ())), preferred_element_type=F32)


def gelu_both(v):
    cdf = 0.5 * (1.0 + lax.erf(v * SQRT_HALF))
    pdf = jnp.exp(-0.5 * v * v) * PDF_SCALE
    return v * cdf, cdf + v * pdf


def center_scale(v):
    inv = 1.0 / v.shape[-1]
    c = v - jnp.sum(v, -1, keepdims=True) * inv
    return c, lax.rsqrt(jnp.sum(c * c, -1, keepdims=True) * inv + EPS)


def pad_rows(v, n):
    return jnp.concatenate([v, jnp.zeros((n - v.shape[0], v.shape[1]), v.dtype)], 0)


def norm_back(grad, xhat, rs, gain):
    inv = 1.0 / grad.shape[-1]
    dx = grad * gain
    m1 = jnp.sum(dx, -1, keepdims=True) * inv
    m2 = jnp.sum(dx * xhat, -1, keepdims=True) * inv
    return rs * (dx - m1 - xhat * m2)


def full(a):
    return pl.BlockSpec(a.shape, lambda *_: (0,) * a.ndim, pipeline_mode=pl.Buffered(1))


def sds(shape, dtype):
    return jax.ShapeDtypeStruct(shape, dtype)


def params(**kw):
    return pltpu.CompilerParams(vmem_limit_bytes=VMEM_LIMIT, **kw)


def enter_kernel(x_ref, flt_ref, gain_ref, shift_ref, out_ref):
    shards, _, slab, width = out_ref.shape
    x = pad_rows(x_ref[0].astype(F32), COLS)
    c, rs = center_scale(x)
    first = (c * rs * gain_ref[...] + shift_ref[...]).astype(BF16)
    out_ref[:, 0] = dot(flt_ref[...], first).astype(BF16).reshape(shards, slab, width)


def enter(x, flt, gain, shift, shards, slab):
    rows, lon, width = x.shape
    return pl.pallas_call(
        enter_kernel,
        grid=(rows,),
        in_specs=[pl.BlockSpec((1, lon, width), lambda r: (r, 0, 0)), full(flt), full(gain), full(shift)],
        out_specs=pl.BlockSpec((shards, 1, slab, width), lambda r: (0, r, 0, 0)),
        out_shape=sds((shards, rows, slab, width), BF16),
        compiler_params=params(),
        name="enter",
    )(x, flt, gain, shift)


def exchange_kernel(src_ref, out_ref, send_sem, recv_sem, own_sem):
    shards = src_ref.shape[0]
    me = lax.axis_index("lat")
    dp = lax.axis_index("dp")
    barrier = pltpu.get_barrier_semaphore()
    for i in range(1, shards):
        peer = lax.rem(me + i, shards)
        pl.semaphore_signal(barrier, inc=1, device_id=(dp, peer), device_id_type=MESH)
    pl.semaphore_wait(barrier, shards - 1)
    own = pltpu.make_async_copy(src_ref.at[me], out_ref.at[me], own_sem)
    own.start()
    copies = []
    for i in range(1, shards):
        peer = lax.rem(me + i, shards)
        copy = pltpu.make_async_remote_copy(
            src_ref=src_ref.at[peer],
            dst_ref=out_ref.at[me],
            send_sem=send_sem.at[i],
            recv_sem=recv_sem.at[i],
            device_id=(dp, peer),
            device_id_type=MESH,
        )
        copy.start()
        copies.append(copy)
    own.wait()
    for copy in copies:
        copy.wait()


def exchange(x, collective_id):
    shards = x.shape[0]
    return pl.pallas_call(
        exchange_kernel,
        in_specs=[pl.BlockSpec(memory_space=pl.ANY)],
        out_specs=pl.BlockSpec(memory_space=pl.ANY),
        out_shape=sds(x.shape, x.dtype),
        scratch_shapes=[
            pltpu.SemaphoreType.DMA((shards,)),
            pltpu.SemaphoreType.DMA((shards,)),
            pltpu.SemaphoreType.DMA,
        ],
        compiler_params=pltpu.CompilerParams(collective_id=collective_id, has_side_effects=True),
        cost_estimate=pl.CostEstimate(flops=0, bytes_accessed=2 * x.size * 2, transcendentals=0),
        name="exchange",
    )(x)


def strided(ref, start, count, stride):
    return jnp.concatenate([ref[t, pl.ds(start, count, stride=stride), :] for t in range(ref.shape[0])], 1)


def put_rows(ref, start, value):
    n = value.shape[0]
    for t in range(ref.shape[0]):
        ref[t, pl.ds(pl.multiple_of(start, 8), n), :] = value[:, t * LANES : (t + 1) * LANES]


def load_mode(wide_ref, m, slab):
    re = strided(wide_ref, 2 * m, LAT_PAD, slab)
    im = strided(wide_ref, 2 * m + 1, LAT_PAD, slab)
    return jnp.concatenate([re, im], 0).astype(BF16)


def widen(recv_ref, wide_ref):
    shards, rows, slab, width = recv_ref.shape
    n = rows * slab

    def one(s, _):
        put_rows(wide_ref, s * n, recv_ref[s].astype(F32).reshape(n, width))
        return 0

    lax.fori_loop(0, shards, one, 0)


def store_mode(out_s, m, value):
    put_rows(out_s, 2 * m * LAT_PAD, value)


def emit_slabs(out_s, out_ref):
    shards, rows, slab, _ = out_ref.shape

    def one(i, _):
        out_ref[i // rows, lax.rem(i, rows)] = strided(out_s, i, slab, LAT_PAD).astype(BF16)
        return 0

    lax.fori_loop(0, shards * rows, one, 0)


def spectral_forward_kernel(
    recv_ref, fa_ref, ia_ref, wi_ref, bi_ref, wo_ref, bo_ref,
    out_ref, freq_ref, hid_ref, gp_ref, t2_ref, wide_s, out_s,
):
    slab, width = recv_ref.shape[2:]
    modes = freq_ref.shape[0]
    h = LAT_PAD
    widen(recv_ref, wide_s)
    if slab != 2 * modes:
        out_s[...] = jnp.zeros_like(out_s)

    def mix(v, w_ref, b_ref):
        a = dot(v, w_ref[0])
        re = a[:h, :width] - a[h:, width:] + b_ref[0:1]
        im = a[h:, :width] + a[:h, width:] + b_ref[1:2]
        return jnp.concatenate([re, im], 0)

    def one(m, _):
        fq = dot(fa_ref[...], load_mode(wide_s, m, slab)).astype(BF16)
        freq_ref[m] = fq
        hid, gp = gelu_both(mix(fq, wi_ref, bi_ref))
        hid = hid.astype(BF16)
        hid_ref[m] = hid
        gp_ref[m] = gp
        outer = mix(hid, wo_ref, bo_ref)
        t = jnp.tanh(outer * (1.0 / SHRINK))
        t2_ref[m] = t * t
        shrunk = (outer - SHRINK * t).astype(BF16)
        store_mode(out_s, m, dot(ia_ref[...], shrunk))
        return 0

    lax.fori_loop(0, modes, one, 0)
    emit_slabs(out_s, out_ref)


def group_specs(shards, rows, slab, modes, part):
    n = 2 * LAT_PAD
    slabs = pl.BlockSpec((shards, rows, slab, part), lambda g: (0, 0, 0, g))
    spec = pl.BlockSpec((modes, n, part), lambda g: (0, 0, g))
    weight = pl.BlockSpec((1, part, 2 * part), lambda g: (g, 0, 0))
    pair = pl.BlockSpec((2, part), lambda g: (0, g))
    return slabs, spec, weight, pair


def spectral_forward(recv, tb, wi, bi, wo, bo, modes):
    shards, rows, slab, width = recv.shape
    part = width // GROUPS
    n = 2 * LAT_PAD
    slabs, spec, weight, pair = group_specs(shards, rows, slab, modes, part)
    return pl.pallas_call(
        spectral_forward_kernel,
        grid=(GROUPS,),
        in_specs=[slabs, full(tb["fa"]), full(tb["ia"]), weight, pair, weight, pair],
        out_specs=[slabs, spec, spec, spec, spec],
        out_shape=[
            sds(recv.shape, BF16),
            sds((modes, n, width), BF16),
            sds((modes, n, width), BF16),
            sds((modes, n, width), F32),
            sds((modes, n, width), F32),
        ],
        scratch_shapes=[
            pltpu.VMEM((part // LANES, shards * rows * slab, LANES), F32),
            pltpu.VMEM((part // LANES, slab * LAT_PAD, LANES), F32),
        ],
        compiler_params=params(),
        name="spectral_forward",
    )(recv, tb["fa"], tb["ia"], wi, bi, wo, bo)


def spectral_backward_kernel(
    recv_ref, iat_ref, fat_ref, wo_ref, wi_ref, freq_ref, hid_ref, gp_ref, t2_ref,
    out_ref, dwo_ref, dbo_ref, dwi_ref, dbi_ref, wide_s, out_s,
):
    slab, width = recv_ref.shape[2:]
    modes = freq_ref.shape[0]
    h = LAT_PAD
    widen(recv_ref, wide_s)
    if slab != 2 * modes:
        out_s[...] = jnp.zeros_like(out_s)
    for ref in (dwo_ref, dbo_ref, dwi_ref, dbi_ref):
        ref[...] = jnp.zeros_like(ref)

    def grads(value, grad, dw_ref, db_ref):
        re, im = grad[:h], grad[h:]
        low_re, low_im = re.astype(BF16), im.astype(BF16)
        low = jnp.concatenate([low_re, low_im], 0)
        turned = jnp.concatenate([low_im, -low_re], 0)
        dw_ref[0] += dot_tn(value, jnp.concatenate([low, turned], 1))
        db_ref[0:1] += jnp.sum(low_re.astype(F32), 0, keepdims=True)
        db_ref[1:2] += jnp.sum(low_im.astype(F32), 0, keepdims=True)
        return low

    def pull(v, w_ref):
        a = dot(v, w_ref[0])
        re = a[:h, :width] + a[h:, width:]
        im = a[h:, :width] - a[:h, width:]
        return jnp.concatenate([re, im], 0)

    def one(m, _):
        merged = dot(iat_ref[...], load_mode(wide_s, m, slab))
        og = grads(hid_ref[m], merged * t2_ref[m], dwo_ref, dbo_ref)
        ig = grads(freq_ref[m], pull(og, wo_ref) * gp_ref[m], dwi_ref, dbi_ref)
        fg = pull(ig, wi_ref).astype(BF16)
        store_mode(out_s, m, dot(fat_ref[...], fg))
        return 0

    lax.fori_loop(0, modes, one, 0)
    emit_slabs(out_s, out_ref)


def spectral_backward(recv, tb, wo, wi, freq, hid, gp, t2):
    shards, rows, slab, width = recv.shape
    modes = freq.shape[0]
    part = width // GROUPS
    slabs, spec, weight, pair = group_specs(shards, rows, slab, modes, part)
    dw = sds((GROUPS, part, 2 * part), F32)
    db = sds((2, width), F32)
    return pl.pallas_call(
        spectral_backward_kernel,
        grid=(GROUPS,),
        in_specs=[slabs, full(tb["iat"]), full(tb["fat"]), weight, weight, spec, spec, spec, spec],
        out_specs=[slabs, weight, pair, weight, pair],
        out_shape=[sds(recv.shape, BF16), dw, db, dw, db],
        scratch_shapes=[
            pltpu.VMEM((part // LANES, shards * rows * slab, LANES), F32),
            pltpu.VMEM((part // LANES, slab * LAT_PAD, LANES), F32),
        ],
        compiler_params=params(),
        name="spectral_backward",
    )(recv, tb["iat"], tb["fat"], wo, wi, freq, hid, gp, t2)


def gather_row(r_ref, i):
    shards, _, slab, width = r_ref.shape
    return r_ref[:, i].astype(F32).reshape(shards * slab, width).astype(BF16)


def feed_kernel(
    per, chunk, scale_ref, x_ref, c_ref, r_ref, il_ref, ilt_ref, w1_ref, w2_ref, eb_ref, rb_ref,
    ng_ref, ns_ref, pg_ref, ps_ref,
    lo_ref, mg_ref, rg_ref, act_ref, pre_ref, sec_ref, up_ref, deb_ref, drb_ref, dpg_ref, dps_ref,
    mixed_s, xhat_s, rs_s, branch_s, grad_s,
):
    g = pl.program_id(0)
    lon, width = x_ref.shape[1:]
    hidden = w1_ref.shape[1]
    shards, _, slab, _ = r_ref.shape

    @pl.when(g == 0)
    def _():
        for ref in (deb_ref, drb_ref, dpg_ref, dps_ref):
            ref[...] = jnp.zeros_like(ref)

    for i in range(per):
        rows = pl.ds(i * COLS, COLS)
        x = pad_rows(x_ref[i].astype(F32), COLS)
        c, rs = center_scale(x)
        first = c * rs * ng_ref[...] + ns_ref[...]
        mixed = dot(il_ref[...], gather_row(r_ref, i)) + first + x
        c, rs = center_scale(mixed)
        xhat = c * rs
        mixed_s[rows, :] = mixed
        xhat_s[rows, :] = xhat
        rs_s[rows, :] = jnp.broadcast_to(rs, (COLS, 128))
        sec_ref[rows, :] = (xhat * pg_ref[...] + ps_ref[...]).astype(BF16)
        up = (pad_rows(c_ref[i].astype(F32), COLS) * scale_ref[0, g * per + i]).astype(BF16)
        up_ref[rows, :] = up
        drb_ref[...] += jnp.sum(up.astype(F32), 0, keepdims=True)
    branch_s[...] = jnp.broadcast_to(rb_ref[...], branch_s.shape)
    grad_s[...] = jnp.zeros_like(grad_s)

    def hidden_chunk(j, _):
        ds = pl.ds(pl.multiple_of(j * chunk, chunk), chunk)
        act, slope = gelu_both(dot(sec_ref[...], w1_ref[:, ds]) + eb_ref[:, ds])
        act = act.astype(BF16)
        act_ref[:, ds] = act
        pre = (dot_nt(up_ref[...], w2_ref[ds, :]) * slope).astype(BF16)
        pre_ref[:, ds] = pre
        deb_ref[:, ds] += jnp.sum(pre.astype(F32), 0, keepdims=True)
        branch_s[...] += dot(act, w2_ref[ds, :])
        grad_s[...] += dot_nt(pre, w1_ref[:, ds])
        return 0

    lax.fori_loop(0, hidden // chunk, hidden_chunk, 0)
    for i in range(per):
        rows = pl.ds(i * COLS, COLS)
        keep = scale_ref[1, g * per + i]
        lo_ref[i] = ((mixed_s[rows, :] + branch_s[rows, :]) * keep).astype(BF16)[:lon]
        grad = grad_s[rows, :]
        xhat = xhat_s[rows, :]
        dpg_ref[...] += jnp.sum(grad * xhat, 0, keepdims=True)
        dps_ref[...] += jnp.sum(grad, 0, keepdims=True)
        up = pad_rows(c_ref[i].astype(F32), COLS) * scale_ref[0, g * per + i]
        mg = up + norm_back(grad, xhat, rs_s[rows, 0:1], pg_ref[...])
        mg_ref[i] = mg[:lon]
        rg_ref[:, i] = dot(ilt_ref[...], mg.astype(BF16)).astype(BF16).reshape(shards, slab, width)


def feed(scale, x, cot, recv, tb, w1, w2, eb, rb, ng, ns, pg, ps):
    rows, lon, width = x.shape
    hidden = w1.shape[1]
    shards, _, slab, _ = recv.shape
    per = 3 if rows % 3 == 0 else 1
    row = pl.BlockSpec((per, lon, width), lambda g: (g, 0, 0))
    slabs = pl.BlockSpec((shards, per, slab, width), lambda g: (0, g, 0, 0))
    flat = lambda w: pl.BlockSpec((per * COLS, w), lambda g: (g, 0))
    vec = lambda w: pl.BlockSpec((1, w), lambda g: (0, 0))
    tall = per * COLS
    return pl.pallas_call(
        functools.partial(feed_kernel, per, 512),
        grid=(rows // per,),
        in_specs=[pl.BlockSpec(memory_space=pltpu.SMEM), row, row, slabs]
        + [full(a) for a in (tb["il"], tb["ilt"], w1, w2, eb, rb, ng, ns, pg, ps)],
        out_specs=[row, row, slabs, flat(hidden), flat(hidden), flat(width), flat(width)]
        + [vec(hidden), vec(width), vec(width), vec(width)],
        out_shape=[
            sds((rows, lon, width), BF16),
            sds((rows, lon, width), F32),
            sds(recv.shape, BF16),
            sds((rows * COLS, hidden), BF16),
            sds((rows * COLS, hidden), BF16),
            sds((rows * COLS, width), BF16),
            sds((rows * COLS, width), BF16),
            sds((1, hidden), F32),
            sds((1, width), F32),
            sds((1, width), F32),
            sds((1, width), F32),
        ],
        scratch_shapes=[
            pltpu.VMEM((tall, width), F32),
            pltpu.VMEM((tall, width), F32),
            pltpu.VMEM((tall, 128), F32),
            pltpu.VMEM((tall, width), F32),
            pltpu.VMEM((tall, width), F32),
        ],
        compiler_params=params(),
        name="feed",
    )(scale, x, cot, recv, tb["il"], tb["ilt"], w1, w2, eb, rb, ng, ns, pg, ps)


def leave_kernel(x_ref, r_ref, mg_ref, fl_ref, gain_ref, out_ref, dg_ref, db_ref):
    lon = x_ref.shape[1]

    @pl.when(pl.program_id(0) == 0)
    def _():
        dg_ref[...] = jnp.zeros_like(dg_ref)
        db_ref[...] = jnp.zeros_like(db_ref)

    x = pad_rows(x_ref[0].astype(F32), COLS)
    c, rs = center_scale(x)
    xhat = c * rs
    mg = pad_rows(mg_ref[0], COLS)
    grad = dot(fl_ref[...], gather_row(r_ref, 0)) + mg
    dg_ref[...] += jnp.sum(grad * xhat, 0, keepdims=True)
    db_ref[...] += jnp.sum(grad, 0, keepdims=True)
    out_ref[0] = (mg + norm_back(grad, xhat, rs, gain_ref[...]))[:lon]


def leave(x, recv, mg, fl, gain):
    rows, lon, width = x.shape
    shards, _, slab, _ = recv.shape
    row = pl.BlockSpec((1, lon, width), lambda r: (r, 0, 0))
    vec = pl.BlockSpec((1, width), lambda r: (0, 0))
    return pl.pallas_call(
        leave_kernel,
        grid=(rows,),
        in_specs=[row, pl.BlockSpec((shards, 1, slab, width), lambda r: (0, r, 0, 0)), row, full(fl), full(gain)],
        out_specs=[row, vec, vec],
        out_shape=[sds((rows, lon, width), F32), sds((1, width), F32), sds((1, width), F32)],
        compiler_params=params(),
        name="leave",
    )(x, recv, mg, fl, gain)


def dense_weights(weight):
    _, blocks, n, _ = weight.shape
    per = blocks // GROUPS
    w = weight.reshape(2, GROUPS, per, n, n)
    eye = jnp.eye(per, dtype=weight.dtype)
    side = per * n
    forward = jnp.einsum("pgbio,bd->gbipdo", w, eye).reshape(GROUPS, side, 2 * side)
    backward = jnp.einsum("pgbio,bd->gdopbi", w, eye).reshape(GROUPS, side, 2 * side)
    return forward, backward


def block_grads(dense):
    side = dense.shape[1]
    per = BLOCKS // GROUPS
    n = side // per
    d = dense.reshape(GROUPS, per, n, 2, per, n)
    picked = jnp.stack([d[:, b, :, :, b, :] for b in range(per)], 1)
    return picked.transpose(3, 0, 1, 2, 4).reshape(2, BLOCKS, n, n)


def shards_fn(
    shards, inputs, cotangent, storm_weight, norm_gain, norm_shift, inner_weight, inner_bias,
    outer_weight, outer_bias, post_gain, post_shift, expand_weight, expand_bias, reduce_weight, reduce_bias,
):
    _, rows, lon, width = inputs.shape
    modes = LON_PAD // shards
    slab = slab_rows(modes)
    tb = make_tables(shards, modes)
    row_ids = lax.axis_index("lat") * rows + jnp.arange(rows, dtype=jnp.int32)
    keep = (row_ids < LAT).astype(F32)
    scale = jnp.stack([keep * (storm_weight[0].astype(F32) / 64.0), keep])
    x = inputs[0]
    cot = cotangent[0]
    line = lambda v: v.reshape(1, -1)
    ng, ns, pg, ps = line(norm_gain), line(norm_shift), line(post_gain), line(post_shift)
    eb, rb = line(expand_bias), line(reduce_bias)
    bi, bo = inner_bias.reshape(2, width), outer_bias.reshape(2, width)
    wi, wi_back = dense_weights(inner_weight)
    wo, wo_back = dense_weights(outer_weight)

    spec = exchange(enter(x, tb["flt"], ng, ns, shards, slab), 0)
    back, freq, hid, gp, t2 = spectral_forward(spec, tb, wi, bi, wo, bo, modes)
    row_spec = exchange(back, 1)
    (layer_out, mixed_grad, row_grad, act, pre, second, up, deb, drb, dpg, dps) = feed(
        scale, x, cot, row_spec, tb, expand_weight, reduce_weight, eb, rb, ng, ns, pg, ps
    )
    dw2 = dot_tn(act, up)
    dw1 = dot_tn(second, pre)
    dw1, dw2 = lax.psum((dw1, dw2), ("dp", "lat"))
    mode_grad = exchange(row_grad, 2)
    slab_grad, dwo, dbo, dwi, dbi = spectral_backward(mode_grad, tb, wo_back, wi_back, freq, hid, gp, t2)
    lon_grad = exchange(slab_grad, 3)
    input_grad, dng, dns = leave(x, lon_grad, mixed_grad, tb["fl"], ng)
    small = lax.psum(
        (dng, dns, block_grads(dwi), dbi, block_grads(dwo), dbo, dpg, dps, deb, drb), ("dp", "lat")
    )
    dng, dns, dwi, dbi, dwo, dbo, dpg, dps, deb, drb = small
    flat = lambda v: v.reshape(-1)
    return (
        layer_out[None], input_grad[None], flat(dng), flat(dns),
        dwi, dbi.reshape(inner_bias.shape), dwo, dbo.reshape(outer_bias.shape),
        flat(dpg), flat(dps), dw1, flat(deb), dw2, flat(drb),
    )


def solution(mesh):
    split = P("dp", "lat", None, None)
    return jax.shard_map(
        functools.partial(shards_fn, mesh.shape["lat"]),
        mesh=mesh,
        in_specs=(split, split, P("dp")) + (P(),) * 12,
        out_specs=(split, split) + (P(),) * 12,
        check_vma=False,
    )
```

```python
import functools
import math

import jax
import jax.numpy as jnp
import ml_dtypes
import numpy as np
from jax import lax
from jax.experimental import pallas as pl
from jax.experimental.pallas import tpu as pltpu
from jax.sharding import PartitionSpec as P

BLOCKS = 8
LAT = 90
LON = 180
LAT_PAD = 96
LON_PAD = 96
KEPT = LON // 2 + 1
COLS = 192
GROUPS = 2
LANES = 128

SHRINK = 0.01
EPS = 1e-6
SQRT_HALF = 0.7071067811865476
PDF_SCALE = 0.3989422804014327

F32 = jnp.float32
BF16 = jnp.bfloat16
MESH = pl.DeviceIdType.MESH
VMEM_LIMIT = 62 * 2**20


def base_tables():
    f = np.float32
    modes = np.arange(LON_PAD)
    columns = np.arange(LON)
    phases = (columns[:, None] * modes[None, :] % LON).astype(f) * f(2.0 * math.pi / LON)
    kept = (modes < LON // 2 + 1).astype(f)
    factor = np.where((modes == 0) | (modes == LON // 2), f(1), f(2)) * kept
    scale = f(1.0 / math.sqrt(LON))
    forward_lon = np.stack([np.cos(phases) * kept, -np.sin(phases) * kept], axis=1) * scale
    inverse_lon = np.stack([np.cos(phases) * factor, -np.sin(phases) * factor], axis=1) * scale
    rows = np.arange(LAT_PAD)
    angles = (rows[:, None] * rows[None, :] % LAT).astype(f) * f(2.0 * math.pi / LAT)
    inside = ((rows[:, None] < LAT) & (rows[None, :] < LAT)).astype(f) / f(math.sqrt(LAT))
    cs = np.cos(angles) * inside
    sn = np.sin(angles) * inside
    forward_lat = np.stack([np.stack([cs, sn], 1), np.stack([-sn, cs], 1)], 0)
    inverse_lat = np.stack([np.stack([cs, -sn], 1), np.stack([sn, cs], 1)], 0)
    return forward_lon, inverse_lon, forward_lat, inverse_lat


def slab_rows(modes):
    return -(-2 * modes // 8) * 8


def lon_table(table, shards, modes):
    slab = slab_rows(modes)
    out = np.zeros((COLS, shards, slab), np.float32)
    split = table.reshape(LON, 2, shards, modes).transpose(0, 2, 3, 1)
    out[:LON, :, : 2 * modes] = split.reshape(LON, shards, 2 * modes)
    return out.reshape(COLS, shards * slab)


def make_tables(shards, modes):
    forward_lon, inverse_lon, forward_lat, inverse_lat = base_tables()
    low = lambda t: jnp.asarray(np.ascontiguousarray(t).astype(ml_dtypes.bfloat16))
    n = 2 * LAT_PAD
    fl = lon_table(forward_lon, shards, modes)
    il = lon_table(inverse_lon, shards, modes)
    fa = forward_lat.reshape(n, n)
    ia = inverse_lat.reshape(n, n)
    return dict(
        fl=low(fl), flt=low(fl.T), il=low(il), ilt=low(il.T),
        fa=low(fa), fat=low(fa.T), ia=low(ia), iat=low(ia.T),
    )


def dot(a, b):
    return jnp.dot(a, b, preferred_element_type=F32)


def dot_nt(a, b):
    return lax.dot_general(a, b, (((1,), (1,)), ((), ())), preferred_element_type=F32)


def dot_tn(a, b):
    return lax.dot_general(a, b, (((0,), (0,)), ((), ())), preferred_element_type=F32)


def gelu_both(v):
    cdf = 0.5 * (1.0 + lax.erf(v * SQRT_HALF))
    pdf = jnp.exp(-0.5 * v * v) * PDF_SCALE
    return v * cdf, cdf + v * pdf


def center_scale(v):
    inv = 1.0 / v.shape[-1]
    c = v - jnp.sum(v, -1, keepdims=True) * inv
    return c, lax.rsqrt(jnp.sum(c * c, -1, keepdims=True) * inv + EPS)


def pad_rows(v, n):
    return jnp.concatenate([v, jnp.zeros((n - v.shape[0], v.shape[1]), v.dtype)], 0)


def norm_back(grad, xhat, rs, gain):
    inv = 1.0 / grad.shape[-1]
    dx = grad * gain
    m1 = jnp.sum(dx, -1, keepdims=True) * inv
    m2 = jnp.sum(dx * xhat, -1, keepdims=True) * inv
    return rs * (dx - m1 - xhat * m2)


def full(a):
    return pl.BlockSpec(a.shape, lambda *_: (0,) * a.ndim, pipeline_mode=pl.Buffered(1))


def sds(shape, dtype):
    return jax.ShapeDtypeStruct(shape, dtype)


def params(**kw):
    return pltpu.CompilerParams(vmem_limit_bytes=VMEM_LIMIT, **kw)


def enter_kernel(x_ref, flt_ref, gain_ref, shift_ref, out_ref):
    shards, _, slab, width = out_ref.shape
    x = pad_rows(x_ref[0].astype(F32), COLS)
    c, rs = center_scale(x)
    first = (c * rs * gain_ref[...] + shift_ref[...]).astype(BF16)
    out_ref[:, 0] = dot(flt_ref[...], first).astype(BF16).reshape(shards, slab, width)


def enter(x, flt, gain, shift, shards, slab):
    rows, lon, width = x.shape
    return pl.pallas_call(
        enter_kernel,
        grid=(rows,),
        in_specs=[pl.BlockSpec((1, lon, width), lambda r: (r, 0, 0)), full(flt), full(gain), full(shift)],
        out_specs=pl.BlockSpec((shards, 1, slab, width), lambda r: (0, r, 0, 0)),
        out_shape=sds((shards, rows, slab, width), BF16),
        compiler_params=params(),
        name="enter",
    )(x, flt, gain, shift)


def up8(n):
    return -(-n // 8) * 8


def slab_sizes(index, modes, slab):
    sizes = [(index < KEPT // modes, slab)]
    if KEPT % modes:
        sizes.append((index == KEPT // modes, up8(2 * (KEPT % modes))))
    return sizes


def row_sizes(index, rows):
    sizes = [(index < LAT // rows, rows)]
    if LAT % rows:
        sizes.append((index == LAT // rows, LAT % rows))
    return sizes


def each_size(row_options, slab_options, fn):
    for row_ok, nr in row_options:
        for slab_ok, ns in slab_options:
            pl.when(row_ok & slab_ok)(functools.partial(fn, nr, ns))


def greet(shards, me, dp):
    barrier = pltpu.get_barrier_semaphore()

    def one(i, _):
        peer = lax.rem(me + i, shards)
        pl.semaphore_signal(barrier, inc=1, device_id=(dp, peer), device_id_type=MESH)
        return 0

    lax.fori_loop(1, shards, one, 0)
    pl.semaphore_wait(barrier, shards - 1)


def send(src, dst, send_sem, recv_sem, dp, peer):
    return pltpu.make_async_remote_copy(
        src_ref=src, dst_ref=dst, send_sem=send_sem, recv_sem=recv_sem,
        device_id=(dp, peer), device_id_type=MESH,
    )


def exchange_kernel(from_rows, modes, src_ref, out_ref, send_sem, recv_sem, own_sem):
    shards, rows, slab, _ = src_ref.shape
    me = lax.axis_index("lat")
    dp = lax.axis_index("dp")
    greet(shards, me, dp)
    own = pltpu.make_async_copy(src_ref.at[me], out_ref.at[me], own_sem)
    own.start()

    def go(i, sender, receiver, act):
        row_owner, mode_owner = (sender, receiver) if from_rows else (receiver, sender)

        def piece(nr, ns):
            part = (pl.ds(0, nr), pl.ds(0, ns))
            copy = send(
                src_ref.at[(receiver,) + part], out_ref.at[(sender,) + part],
                send_sem.at[i], recv_sem.at[i], dp, receiver,
            )
            act(copy)

        each_size(row_sizes(row_owner, rows), slab_sizes(mode_owner, modes, slab), piece)

    def start(i, _):
        go(i, me, lax.rem(me + i, shards), lambda copy: copy.start())
        return 0

    def finish(i, _):
        go(i, me, lax.rem(me + i, shards), lambda copy: copy.wait_send())
        go(i, lax.rem(me + shards - i, shards), me, lambda copy: copy.wait_recv())
        return 0

    lax.fori_loop(1, shards, start, 0)
    own.wait()
    lax.fori_loop(1, shards, finish, 0)


def exchange(x, from_rows, modes, collective_id):
    shards = x.shape[0]
    return pl.pallas_call(
        functools.partial(exchange_kernel, from_rows, modes),
        in_specs=[pl.BlockSpec(memory_space=pl.ANY)],
        out_specs=pl.BlockSpec(memory_space=pl.ANY),
        out_shape=sds(x.shape, x.dtype),
        scratch_shapes=[
            pltpu.SemaphoreType.DMA((shards,)),
            pltpu.SemaphoreType.DMA((shards,)),
            pltpu.SemaphoreType.DMA,
        ],
        compiler_params=pltpu.CompilerParams(collective_id=collective_id, has_side_effects=True),
        cost_estimate=pl.CostEstimate(flops=0, bytes_accessed=2 * x.size * 2, transcendentals=0),
        name="exchange",
    )(x)


def strided(ref, start, count, stride):
    return jnp.concatenate([ref[t, pl.ds(start, count, stride=stride), :] for t in range(ref.shape[0])], 1)


def put_rows(ref, start, value):
    n = value.shape[0]
    for t in range(ref.shape[0]):
        ref[t, pl.ds(pl.multiple_of(start, 8), n), :] = value[:, t * LANES : (t + 1) * LANES]


def load_mode(wide_ref, m, slab, modes):
    re = strided(wide_ref, 2 * m, LAT_PAD, slab)
    im = strided(wide_ref, 2 * m + 1, LAT_PAD, slab)
    live = lax.axis_index("lat") * modes + m < KEPT
    value = jnp.concatenate([re, im], 0)
    return jnp.where(live, value, jnp.zeros_like(value)).astype(BF16)


def widen(recv_ref, wide_ref):
    shards, rows, slab, width = recv_ref.shape
    n = rows * slab

    def one(s, _):
        put_rows(wide_ref, s * n, recv_ref[s].astype(F32).reshape(n, width))
        return 0

    lax.fori_loop(0, shards, one, 0)
    if LAT % rows:
        first = LAT * slab
        last = (LAT // rows + 1) * n
        put_rows(wide_ref, first, jnp.zeros((last - first, width), F32))
    for s in range(-(-LAT // rows), shards):
        put_rows(wide_ref, s * n, jnp.zeros((n, width), F32))


def store_mode(out_s, m, value):
    put_rows(out_s, 2 * m * LAT_PAD, value)


def emit_slabs(out_s, out_ref):
    shards, rows, slab, _ = out_ref.shape

    def one(i, _):
        out_ref[i // rows, lax.rem(i, rows)] = strided(out_s, i, slab, LAT_PAD).astype(BF16)
        return 0

    lax.fori_loop(0, shards * rows, one, 0)


def spectral_forward_kernel(
    recv_ref, fa_ref, ia_ref, wi_ref, bi_ref, wo_ref, bo_ref,
    out_ref, freq_ref, hid_ref, gp_ref, t2_ref, wide_s, out_s,
):
    slab, width = recv_ref.shape[2:]
    modes = freq_ref.shape[0]
    h = LAT_PAD
    widen(recv_ref, wide_s)
    if slab != 2 * modes:
        out_s[...] = jnp.zeros_like(out_s)

    def mix(v, w_ref, b_ref):
        a = dot(v, w_ref[0])
        re = a[:h, :width] - a[h:, width:] + b_ref[0:1]
        im = a[h:, :width] + a[:h, width:] + b_ref[1:2]
        return jnp.concatenate([re, im], 0)

    def one(m, _):
        fq = dot(fa_ref[...], load_mode(wide_s, m, slab, modes)).astype(BF16)
        freq_ref[m] = fq
        hid, gp = gelu_both(mix(fq, wi_ref, bi_ref))
        hid = hid.astype(BF16)
        hid_ref[m] = hid
        gp_ref[m] = gp
        outer = mix(hid, wo_ref, bo_ref)
        t = jnp.tanh(outer * (1.0 / SHRINK))
        t2_ref[m] = t * t
        shrunk = (outer - SHRINK * t).astype(BF16)
        store_mode(out_s, m, dot(ia_ref[...], shrunk))
        return 0

    lax.fori_loop(0, modes, one, 0)
    emit_slabs(out_s, out_ref)


def group_specs(shards, rows, slab, modes, part):
    n = 2 * LAT_PAD
    slabs = pl.BlockSpec((shards, rows, slab, part), lambda g: (0, 0, 0, g))
    spec = pl.BlockSpec((modes, n, part), lambda g: (0, 0, g))
    weight = pl.BlockSpec((1, part, 2 * part), lambda g: (g, 0, 0))
    pair = pl.BlockSpec((2, part), lambda g: (0, g))
    return slabs, spec, weight, pair


def spectral_forward(recv, tb, wi, bi, wo, bo, modes):
    shards, rows, slab, width = recv.shape
    part = width // GROUPS
    n = 2 * LAT_PAD
    slabs, spec, weight, pair = group_specs(shards, rows, slab, modes, part)
    return pl.pallas_call(
        spectral_forward_kernel,
        grid=(GROUPS,),
        in_specs=[slabs, full(tb["fa"]), full(tb["ia"]), weight, pair, weight, pair],
        out_specs=[slabs, spec, spec, spec, spec],
        out_shape=[
            sds(recv.shape, BF16),
            sds((modes, n, width), BF16),
            sds((modes, n, width), BF16),
            sds((modes, n, width), F32),
            sds((modes, n, width), F32),
        ],
        scratch_shapes=[
            pltpu.VMEM((part // LANES, shards * rows * slab, LANES), F32),
            pltpu.VMEM((part // LANES, slab * LAT_PAD, LANES), F32),
        ],
        compiler_params=params(),
        name="spectral_forward",
    )(recv, tb["fa"], tb["ia"], wi, bi, wo, bo)


def spectral_backward_kernel(
    recv_ref, iat_ref, fat_ref, wo_ref, wi_ref, freq_ref, hid_ref, gp_ref, t2_ref,
    out_ref, dwo_ref, dbo_ref, dwi_ref, dbi_ref, wide_s, out_s,
):
    slab, width = recv_ref.shape[2:]
    modes = freq_ref.shape[0]
    h = LAT_PAD
    widen(recv_ref, wide_s)
    if slab != 2 * modes:
        out_s[...] = jnp.zeros_like(out_s)
    for ref in (dwo_ref, dbo_ref, dwi_ref, dbi_ref):
        ref[...] = jnp.zeros_like(ref)

    def grads(value, grad, dw_ref, db_ref):
        re, im = grad[:h], grad[h:]
        low_re, low_im = re.astype(BF16), im.astype(BF16)
        low = jnp.concatenate([low_re, low_im], 0)
        turned = jnp.concatenate([low_im, -low_re], 0)
        dw_ref[0] += dot_tn(value, jnp.concatenate([low, turned], 1))
        db_ref[0:1] += jnp.sum(low_re.astype(F32), 0, keepdims=True)
        db_ref[1:2] += jnp.sum(low_im.astype(F32), 0, keepdims=True)
        return low

    def pull(v, w_ref):
        a = dot(v, w_ref[0])
        re = a[:h, :width] + a[h:, width:]
        im = a[h:, :width] - a[:h, width:]
        return jnp.concatenate([re, im], 0)

    def one(m, _):
        merged = dot(iat_ref[...], load_mode(wide_s, m, slab, modes))
        og = grads(hid_ref[m], merged * t2_ref[m], dwo_ref, dbo_ref)
        ig = grads(freq_ref[m], pull(og, wo_ref) * gp_ref[m], dwi_ref, dbi_ref)
        fg = pull(ig, wi_ref).astype(BF16)
        store_mode(out_s, m, dot(fat_ref[...], fg))
        return 0

    lax.fori_loop(0, modes, one, 0)
    emit_slabs(out_s, out_ref)


def spectral_backward(recv, tb, wo, wi, freq, hid, gp, t2):
    shards, rows, slab, width = recv.shape
    modes = freq.shape[0]
    part = width // GROUPS
    slabs, spec, weight, pair = group_specs(shards, rows, slab, modes, part)
    dw = sds((GROUPS, part, 2 * part), F32)
    db = sds((2, width), F32)
    return pl.pallas_call(
        spectral_backward_kernel,
        grid=(GROUPS,),
        in_specs=[slabs, full(tb["iat"]), full(tb["fat"]), weight, weight, spec, spec, spec, spec],
        out_specs=[slabs, weight, pair, weight, pair],
        out_shape=[sds(recv.shape, BF16), dw, db, dw, db],
        scratch_shapes=[
            pltpu.VMEM((part // LANES, shards * rows * slab, LANES), F32),
            pltpu.VMEM((part // LANES, slab * LAT_PAD, LANES), F32),
        ],
        compiler_params=params(),
        name="spectral_backward",
    )(recv, tb["iat"], tb["fat"], wo, wi, freq, hid, gp, t2)


def gather_row(r_ref, row, modes):
    shards, _, slab, width = r_ref.shape
    whole = KEPT // modes
    parts = [r_ref[:whole, row].astype(F32).reshape(whole * slab, width)]
    rest = (shards - whole) * slab
    if KEPT % modes:
        n = up8(2 * (KEPT % modes))
        parts.append(r_ref[whole, row].astype(F32)[:n])
        rest -= n
    if rest:
        parts.append(jnp.zeros((rest, width), F32))
    return jnp.concatenate(parts, 0).astype(BF16)


def feed_kernel(
    per, chunk, modes, scale_ref, x_ref, c_ref, back_ref, il_ref, ilt_ref, w1_ref, w2_ref, eb_ref, rb_ref,
    ng_ref, ns_ref, pg_ref, ps_ref,
    lo_ref, mg_ref, out_ref, act_ref, pre_ref, sec_ref, up_ref, deb_ref, drb_ref, dpg_ref, dps_ref,
    recv_s, stage_s, mixed_s, xhat_s, rs_s, branch_s, grad_s,
    in_send, in_recv, in_own, out_send, out_recv, out_own,
):
    g = pl.program_id(0)
    steps = pl.num_programs(0)
    lon, width = x_ref.shape[1:]
    hidden = w1_ref.shape[1]
    shards, rows, slab, _ = recv_s.shape
    me = lax.axis_index("lat")
    dp = lax.axis_index("dp")

    def incoming(step, i, sender, receiver, act):
        part = pl.ds(step * per, per)

        def piece(nr, ns):
            act(send(
                back_ref.at[receiver, part, pl.ds(0, ns)], recv_s.at[sender, part, pl.ds(0, ns)],
                in_send.at[step, i], in_recv.at[step, i], dp, receiver,
            ))

        live = receiver * rows + step * per < LAT
        each_size([(live, per)], slab_sizes(sender, modes, slab), piece)

    def outgoing(step, i, sender, receiver, act):
        part = pl.ds(step * per, per)

        def piece(nr, ns):
            act(send(
                stage_s.at[receiver, part, pl.ds(0, ns)], out_ref.at[sender, part, pl.ds(0, ns)],
                out_send.at[step, i], out_recv.at[step, i], dp, receiver,
            ))

        live = sender * rows + step * per < LAT
        each_size([(live, per)], slab_sizes(receiver, modes, slab), piece)

    def own_in(step):
        part = pl.ds(step * per, per)
        return pltpu.make_async_copy(back_ref.at[me, part], recv_s.at[me, part], in_own.at[step])

    def own_out(step):
        part = pl.ds(step * per, per)
        return pltpu.make_async_copy(stage_s.at[me, part], out_ref.at[me, part], out_own.at[step])

    def to(i):
        return lax.rem(me + i, shards)

    def source(i):
        return lax.rem(me + shards - i, shards)

    def peers(fn):
        def one(i, _):
            fn(i)
            return 0

        lax.fori_loop(1, shards, one, 0)

    @pl.when(g == 0)
    def _():
        greet(shards, me, dp)

        def one(step, _):
            own_in(step).start()
            peers(lambda i: incoming(step, i, me, to(i), lambda c: c.start()))
            return 0

        lax.fori_loop(0, steps, one, 0)
        for ref in (deb_ref, drb_ref, dpg_ref, dps_ref):
            ref[...] = jnp.zeros_like(ref)

    own_in(g).wait()
    peers(lambda i: incoming(g, i, source(i), me, lambda c: c.wait_recv()))
    for i in range(per):
        rows_i = pl.ds(i * COLS, COLS)
        x = pad_rows(x_ref[i].astype(F32), COLS)
        c, rs = center_scale(x)
        first = c * rs * ng_ref[...] + ns_ref[...]
        filtered = dot(il_ref[...], gather_row(recv_s, g * per + i, modes))
        live = me * rows + g * per + i < LAT
        mixed = jnp.where(live, filtered, jnp.zeros_like(filtered)) + first + x
        c, rs = center_scale(mixed)
        xhat = c * rs
        mixed_s[rows_i, :] = mixed
        xhat_s[rows_i, :] = xhat
        rs_s[rows_i, :] = jnp.broadcast_to(rs, (COLS, LANES))
        sec_ref[rows_i, :] = (xhat * pg_ref[...] + ps_ref[...]).astype(BF16)
        up = (pad_rows(c_ref[i].astype(F32), COLS) * scale_ref[0, g * per + i]).astype(BF16)
        up_ref[rows_i, :] = up
        drb_ref[...] += jnp.sum(up.astype(F32), 0, keepdims=True)
    branch_s[...] = jnp.broadcast_to(rb_ref[...], branch_s.shape)
    grad_s[...] = jnp.zeros_like(grad_s)

    def hidden_chunk(j, _):
        ds = pl.ds(pl.multiple_of(j * chunk, chunk), chunk)
        act, slope = gelu_both(dot(sec_ref[...], w1_ref[:, ds]) + eb_ref[:, ds])
        act = act.astype(BF16)
        act_ref[:, ds] = act
        pre = (dot_nt(up_ref[...], w2_ref[ds, :]) * slope).astype(BF16)
        pre_ref[:, ds] = pre
        deb_ref[:, ds] += jnp.sum(pre.astype(F32), 0, keepdims=True)
        branch_s[...] += dot(act, w2_ref[ds, :])
        grad_s[...] += dot_nt(pre, w1_ref[:, ds])
        return 0

    lax.fori_loop(0, hidden // chunk, hidden_chunk, 0)
    for i in range(per):
        rows_i = pl.ds(i * COLS, COLS)
        grad = grad_s[rows_i, :]
        xhat = xhat_s[rows_i, :]
        up = pad_rows(c_ref[i].astype(F32), COLS) * scale_ref[0, g * per + i]
        mg = up + norm_back(grad, xhat, rs_s[rows_i, 0:1], pg_ref[...])
        mg_ref[i] = mg[:lon]
        rg = dot(ilt_ref[...], mg.astype(BF16)).astype(BF16)
        stage_s[:, g * per + i] = rg.reshape(shards, slab, width)
    own_out(g).start()
    peers(lambda i: outgoing(g, i, me, to(i), lambda c: c.start()))
    for i in range(per):
        rows_i = pl.ds(i * COLS, COLS)
        keep = scale_ref[1, g * per + i]
        lo_ref[i] = ((mixed_s[rows_i, :] + branch_s[rows_i, :]) * keep).astype(BF16)[:lon]
        grad = grad_s[rows_i, :]
        dpg_ref[...] += jnp.sum(grad * xhat_s[rows_i, :], 0, keepdims=True)
        dps_ref[...] += jnp.sum(grad, 0, keepdims=True)

    @pl.when(g == steps - 1)
    def _():
        def one(step, _):
            own_out(step).wait()

            def wait_all(i):
                incoming(step, i, me, to(i), lambda c: c.wait_send())
                outgoing(step, i, me, to(i), lambda c: c.wait_send())
                outgoing(step, i, source(i), me, lambda c: c.wait_recv())

            peers(wait_all)
            return 0

        lax.fori_loop(0, steps, one, 0)


def feed(scale, x, cot, back, tb, w1, w2, eb, rb, ng, ns, pg, ps, modes, collective_id):
    rows, lon, width = x.shape
    hidden = w1.shape[1]
    shards, _, slab, _ = back.shape
    per = 3 if rows % 3 == 0 else 1
    steps = rows // per
    row = pl.BlockSpec((per, lon, width), lambda g: (g, 0, 0))
    any_ = pl.BlockSpec(memory_space=pl.ANY)
    flat = lambda w: pl.BlockSpec((per * COLS, w), lambda g: (g, 0))
    vec = lambda w: pl.BlockSpec((1, w), lambda g: (0, 0))
    tall = per * COLS
    dma = pltpu.SemaphoreType.DMA
    return pl.pallas_call(
        functools.partial(feed_kernel, per, 512, modes),
        grid=(steps,),
        in_specs=[pl.BlockSpec(memory_space=pltpu.SMEM), row, row, any_]
        + [full(a) for a in (tb["il"], tb["ilt"], w1, w2, eb, rb, ng, ns, pg, ps)],
        out_specs=[row, row, any_, flat(hidden), flat(hidden), flat(width), flat(width)]
        + [vec(hidden), vec(width), vec(width), vec(width)],
        out_shape=[
            sds((rows, lon, width), BF16),
            sds((rows, lon, width), F32),
            sds(back.shape, BF16),
            sds((rows * COLS, hidden), BF16),
            sds((rows * COLS, hidden), BF16),
            sds((rows * COLS, width), BF16),
            sds((rows * COLS, width), BF16),
            sds((1, hidden), F32),
            sds((1, width), F32),
            sds((1, width), F32),
            sds((1, width), F32),
        ],
        scratch_shapes=[
            pltpu.VMEM(back.shape, BF16),
            pltpu.VMEM(back.shape, BF16),
            pltpu.VMEM((tall, width), F32),
            pltpu.VMEM((tall, width), F32),
            pltpu.VMEM((tall, LANES), F32),
            pltpu.VMEM((tall, width), F32),
            pltpu.VMEM((tall, width), F32),
            dma((steps, shards)), dma((steps, shards)), dma((steps,)),
            dma((steps, shards)), dma((steps, shards)), dma((steps,)),
        ],
        compiler_params=params(collective_id=collective_id, has_side_effects=True),
        name="feed",
    )(scale, x, cot, back, tb["il"], tb["ilt"], w1, w2, eb, rb, ng, ns, pg, ps)


def leave_kernel(modes, x_ref, r_ref, mg_ref, fl_ref, gain_ref, out_ref, dg_ref, db_ref):
    lon = x_ref.shape[1]

    @pl.when(pl.program_id(0) == 0)
    def _():
        dg_ref[...] = jnp.zeros_like(dg_ref)
        db_ref[...] = jnp.zeros_like(db_ref)

    x = pad_rows(x_ref[0].astype(F32), COLS)
    c, rs = center_scale(x)
    xhat = c * rs
    mg = pad_rows(mg_ref[0], COLS)
    live = lax.axis_index("lat") * pl.num_programs(0) + pl.program_id(0) < LAT
    spread = dot(fl_ref[...], gather_row(r_ref, 0, modes))
    grad = jnp.where(live, spread, jnp.zeros_like(spread)) + mg
    dg_ref[...] += jnp.sum(grad * xhat, 0, keepdims=True)
    db_ref[...] += jnp.sum(grad, 0, keepdims=True)
    out_ref[0] = (mg + norm_back(grad, xhat, rs, gain_ref[...]))[:lon]


def leave(x, recv, mg, fl, gain, modes):
    rows, lon, width = x.shape
    shards, _, slab, _ = recv.shape
    row = pl.BlockSpec((1, lon, width), lambda r: (r, 0, 0))
    vec = pl.BlockSpec((1, width), lambda r: (0, 0))
    return pl.pallas_call(
        functools.partial(leave_kernel, modes),
        grid=(rows,),
        in_specs=[row, pl.BlockSpec((shards, 1, slab, width), lambda r: (0, r, 0, 0)), row, full(fl), full(gain)],
        out_specs=[row, vec, vec],
        out_shape=[sds((rows, lon, width), F32), sds((1, width), F32), sds((1, width), F32)],
        compiler_params=params(),
        name="leave",
    )(x, recv, mg, fl, gain)


def dense_weights(weight):
    _, blocks, n, _ = weight.shape
    per = blocks // GROUPS
    w = weight.reshape(2, GROUPS, per, n, n)
    eye = jnp.eye(per, dtype=weight.dtype)
    side = per * n
    forward = jnp.einsum("pgbio,bd->gbipdo", w, eye).reshape(GROUPS, side, 2 * side)
    backward = jnp.einsum("pgbio,bd->gdopbi", w, eye).reshape(GROUPS, side, 2 * side)
    return forward, backward


def block_grads(dense):
    side = dense.shape[1]
    per = BLOCKS // GROUPS
    n = side // per
    d = dense.reshape(GROUPS, per, n, 2, per, n)
    picked = jnp.stack([d[:, b, :, :, b, :] for b in range(per)], 1)
    return picked.transpose(3, 0, 1, 2, 4).reshape(2, BLOCKS, n, n)


def shards_fn(
    shards, inputs, cotangent, storm_weight, norm_gain, norm_shift, inner_weight, inner_bias,
    outer_weight, outer_bias, post_gain, post_shift, expand_weight, expand_bias, reduce_weight, reduce_bias,
):
    _, rows, lon, width = inputs.shape
    modes = LON_PAD // shards
    slab = slab_rows(modes)
    tb = make_tables(shards, modes)
    row_ids = lax.axis_index("lat") * rows + jnp.arange(rows, dtype=jnp.int32)
    keep = (row_ids < LAT).astype(F32)
    scale = jnp.stack([keep * (storm_weight[0].astype(F32) / 64.0), keep])
    x = inputs[0]
    cot = cotangent[0]
    line = lambda v: v.reshape(1, -1)
    ng, ns, pg, ps = line(norm_gain), line(norm_shift), line(post_gain), line(post_shift)
    eb, rb = line(expand_bias), line(reduce_bias)
    bi, bo = inner_bias.reshape(2, width), outer_bias.reshape(2, width)
    wi, wi_back = dense_weights(inner_weight)
    wo, wo_back = dense_weights(outer_weight)

    spec = exchange(enter(x, tb["flt"], ng, ns, shards, slab), True, modes, 0)
    back, freq, hid, gp, t2 = spectral_forward(spec, tb, wi, bi, wo, bo, modes)
    (layer_out, mixed_grad, mode_grad, act, pre, second, up, deb, drb, dpg, dps) = feed(
        scale, x, cot, back, tb, expand_weight, reduce_weight, eb, rb, ng, ns, pg, ps, modes, 1
    )
    dw2 = dot_tn(act, up).astype(BF16)
    dw1 = dot_tn(second, pre).astype(BF16)
    dw1, dw2 = lax.psum((dw1, dw2), ("dp", "lat"))
    dw1, dw2 = dw1.astype(F32), dw2.astype(F32)
    slab_grad, dwo, dbo, dwi, dbi = spectral_backward(mode_grad, tb, wo_back, wi_back, freq, hid, gp, t2)
    lon_grad = exchange(slab_grad, False, modes, 2)
    input_grad, dng, dns = leave(x, lon_grad, mixed_grad, tb["fl"], ng, modes)
    small = lax.psum(
        (dng, dns, block_grads(dwi), dbi, block_grads(dwo), dbo, dpg, dps, deb, drb), ("dp", "lat")
    )
    dng, dns, dwi, dbi, dwo, dbo, dpg, dps, deb, drb = small
    flat = lambda v: v.reshape(-1)
    return (
        layer_out[None], input_grad[None], flat(dng), flat(dns),
        dwi, dbi.reshape(inner_bias.shape), dwo, dbo.reshape(outer_bias.shape),
        flat(dpg), flat(dps), dw1, flat(deb), dw2, flat(drb),
    )


def solution(mesh):
    split = P("dp", "lat", None, None)
    return jax.shard_map(
        functools.partial(shards_fn, mesh.shape["lat"]),
        mesh=mesh,
        in_specs=(split, split, P("dp")) + (P(),) * 12,
        out_specs=(split, split) + (P(),) * 12,
        check_vma=False,
    )
```

```python
import functools
import math

import jax
import jax.numpy as jnp
import ml_dtypes
import numpy as np
from jax import lax
from jax.experimental import pallas as pl
from jax.experimental.pallas import tpu as pltpu
from jax.sharding import PartitionSpec as P

BLOCKS = 8
LAT = 90
LON = 180
LAT_PAD = 96
LON_PAD = 96
KEPT = LON // 2 + 1
COLS = 192
GROUPS = 2
LANES = 128
LOW_ROWS = 16
NORM_G, NORM_S, POST_G, POST_S, REDUCE_B, INNER_B, OUTER_B, EXPAND_B = 0, 1, 2, 3, 4, 5, 7, 9

SHRINK = 0.01
EPS = 1e-6
SQRT_HALF = 0.7071067811865476
PDF_SCALE = 0.3989422804014327

F32 = jnp.float32
BF16 = jnp.bfloat16
MESH = pl.DeviceIdType.MESH
VMEM_LIMIT = 62 * 2**20


def base_tables():
    f = np.float32
    modes = np.arange(LON_PAD)
    columns = np.arange(LON)
    phases = (columns[:, None] * modes[None, :] % LON).astype(f) * f(2.0 * math.pi / LON)
    kept = (modes < LON // 2 + 1).astype(f)
    factor = np.where((modes == 0) | (modes == LON // 2), f(1), f(2)) * kept
    scale = f(1.0 / math.sqrt(LON))
    forward_lon = np.stack([np.cos(phases) * kept, -np.sin(phases) * kept], axis=1) * scale
    inverse_lon = np.stack([np.cos(phases) * factor, -np.sin(phases) * factor], axis=1) * scale
    rows = np.arange(LAT_PAD)
    angles = (rows[:, None] * rows[None, :] % LAT).astype(f) * f(2.0 * math.pi / LAT)
    inside = ((rows[:, None] < LAT) & (rows[None, :] < LAT)).astype(f) / f(math.sqrt(LAT))
    cs = np.cos(angles) * inside
    sn = np.sin(angles) * inside
    forward_lat = np.stack([np.stack([cs, sn], 1), np.stack([-sn, cs], 1)], 0)
    inverse_lat = np.stack([np.stack([cs, -sn], 1), np.stack([sn, cs], 1)], 0)
    return forward_lon, inverse_lon, forward_lat, inverse_lat


def slab_rows(modes):
    return -(-2 * modes // 8) * 8


def lon_table(table, shards, modes):
    slab = slab_rows(modes)
    out = np.zeros((COLS, shards, slab), np.float32)
    split = table.reshape(LON, 2, shards, modes).transpose(0, 2, 3, 1)
    out[:LON, :, : 2 * modes] = split.reshape(LON, shards, 2 * modes)
    return out.reshape(COLS, shards * slab)


def make_tables(shards, modes):
    forward_lon, inverse_lon, forward_lat, inverse_lat = base_tables()
    low = lambda t: jnp.asarray(np.ascontiguousarray(t).astype(ml_dtypes.bfloat16))
    n = 2 * LAT_PAD
    fl = lon_table(forward_lon, shards, modes)
    il = lon_table(inverse_lon, shards, modes)
    fa = forward_lat.reshape(n, n)
    ia = inverse_lat.reshape(n, n)
    return dict(
        fl=low(fl), flt=low(fl.T), il=low(il), ilt=low(il.T),
        fa=low(fa), fat=low(fa.T), ia=low(ia), iat=low(ia.T),
    )


def dot(a, b):
    return jnp.dot(a, b, preferred_element_type=F32)


def dot_nt(a, b):
    return lax.dot_general(a, b, (((1,), (1,)), ((), ())), preferred_element_type=F32)


def dot_tn(a, b):
    return lax.dot_general(a, b, (((0,), (0,)), ((), ())), preferred_element_type=F32)


def gelu_both(v):
    cdf = 0.5 * (1.0 + lax.erf(v * SQRT_HALF))
    pdf = jnp.exp(-0.5 * v * v) * PDF_SCALE
    return v * cdf, cdf + v * pdf


def center_scale(v):
    inv = 1.0 / v.shape[-1]
    c = v - jnp.sum(v, -1, keepdims=True) * inv
    return c, lax.rsqrt(jnp.sum(c * c, -1, keepdims=True) * inv + EPS)


def pad_rows(v, n):
    return jnp.concatenate([v, jnp.zeros((n - v.shape[0], v.shape[1]), v.dtype)], 0)


def norm_back(grad, xhat, rs, gain):
    inv = 1.0 / grad.shape[-1]
    dx = grad * gain
    m1 = jnp.sum(dx, -1, keepdims=True) * inv
    m2 = jnp.sum(dx * xhat, -1, keepdims=True) * inv
    return rs * (dx - m1 - xhat * m2)


def full(a):
    return pl.BlockSpec(a.shape, lambda *_: (0,) * a.ndim, pipeline_mode=pl.Buffered(1))


def sds(shape, dtype):
    return jax.ShapeDtypeStruct(shape, dtype)


def params(**kw):
    return pltpu.CompilerParams(vmem_limit_bytes=VMEM_LIMIT, **kw)


def vector(v_ref, row):
    return v_ref[row : row + 1, :]


def enter_kernel(x_ref, flt_ref, v_ref, out_ref):
    shards, _, slab, width = out_ref.shape
    x = pad_rows(x_ref[0].astype(F32), COLS)
    c, rs = center_scale(x)
    first = (c * rs * vector(v_ref, NORM_G) + vector(v_ref, NORM_S)).astype(BF16)
    out_ref[:, 0] = dot(flt_ref[...], first).astype(BF16).reshape(shards, slab, width)


def enter(x, flt, vectors, shards, slab):
    rows, lon, width = x.shape
    return pl.pallas_call(
        enter_kernel,
        grid=(rows,),
        in_specs=[pl.BlockSpec((1, lon, width), lambda r: (r, 0, 0)), full(flt), full(vectors)],
        out_specs=pl.BlockSpec((shards, 1, slab, width), lambda r: (0, r, 0, 0)),
        out_shape=sds((shards, rows, slab, width), BF16),
        compiler_params=params(),
        name="enter",
    )(x, flt, vectors)


def up8(n):
    return -(-n // 8) * 8


def slab_sizes(index, modes, slab):
    sizes = [(index < KEPT // modes, slab)]
    if KEPT % modes:
        sizes.append((index == KEPT // modes, up8(2 * (KEPT % modes))))
    return sizes


def row_sizes(index, rows):
    sizes = [(index < LAT // rows, rows)]
    if LAT % rows:
        sizes.append((index == LAT // rows, LAT % rows))
    return sizes


def each_size(row_options, slab_options, fn):
    for row_ok, nr in row_options:
        for slab_ok, ns in slab_options:
            pl.when(row_ok & slab_ok)(functools.partial(fn, nr, ns))


def greet(shards, me, dp):
    barrier = pltpu.get_barrier_semaphore()

    def one(i, _):
        peer = lax.rem(me + i, shards)
        pl.semaphore_signal(barrier, inc=1, device_id=(dp, peer), device_id_type=MESH)
        return 0

    lax.fori_loop(1, shards, one, 0)
    pl.semaphore_wait(barrier, shards - 1)


def send(src, dst, send_sem, recv_sem, dp, peer):
    return pltpu.make_async_remote_copy(
        src_ref=src, dst_ref=dst, send_sem=send_sem, recv_sem=recv_sem,
        device_id=(dp, peer), device_id_type=MESH,
    )


def exchange_kernel(from_rows, modes, src_ref, out_ref, send_sem, recv_sem, own_sem):
    shards, rows, slab, _ = src_ref.shape
    me = lax.axis_index("lat")
    dp = lax.axis_index("dp")
    greet(shards, me, dp)
    own = pltpu.make_async_copy(src_ref.at[me], out_ref.at[me], own_sem)
    own.start()

    def go(i, sender, receiver, act):
        row_owner, mode_owner = (sender, receiver) if from_rows else (receiver, sender)

        def piece(nr, ns):
            part = (pl.ds(0, nr), pl.ds(0, ns))
            copy = send(
                src_ref.at[(receiver,) + part], out_ref.at[(sender,) + part],
                send_sem.at[i], recv_sem.at[i], dp, receiver,
            )
            act(copy)

        each_size(row_sizes(row_owner, rows), slab_sizes(mode_owner, modes, slab), piece)

    def start(i, _):
        go(i, me, lax.rem(me + i, shards), lambda copy: copy.start())
        return 0

    def finish(i, _):
        go(i, me, lax.rem(me + i, shards), lambda copy: copy.wait_send())
        go(i, lax.rem(me + shards - i, shards), me, lambda copy: copy.wait_recv())
        return 0

    lax.fori_loop(1, shards, start, 0)
    own.wait()
    lax.fori_loop(1, shards, finish, 0)


def exchange(x, from_rows, modes, collective_id):
    shards = x.shape[0]
    return pl.pallas_call(
        functools.partial(exchange_kernel, from_rows, modes),
        in_specs=[pl.BlockSpec(memory_space=pl.ANY)],
        out_specs=pl.BlockSpec(memory_space=pl.ANY),
        out_shape=sds(x.shape, x.dtype),
        scratch_shapes=[
            pltpu.SemaphoreType.DMA((shards,)),
            pltpu.SemaphoreType.DMA((shards,)),
            pltpu.SemaphoreType.DMA,
        ],
        compiler_params=pltpu.CompilerParams(collective_id=collective_id, has_side_effects=True),
        cost_estimate=pl.CostEstimate(flops=0, bytes_accessed=2 * x.size * 2, transcendentals=0),
        name="exchange",
    )(x)


def halving_plan(groups, shards, n, turn):
    dp_bits = [("dp", b) for b in range(groups.bit_length() - 1)]
    lat_bits = [("lat", b) for b in range(shards.bit_length() - 1)]
    middle = dp_bits[1:2] + lat_bits[:2]
    turn = turn % len(middle)
    order = dp_bits[:1] + middle[turn:] + middle[:turn] + dp_bits[2:] + lat_bits[2:]
    plan = []
    for axis, bit in order:
        halved = n % (2 * LOW_ROWS) == 0
        plan.append((axis, bit, n, halved))
        n = n // 2 if halved else n
    return plan, n


def halving_plans(groups, shards, sizes):
    return [
        (k, t * size // 3) + halving_plan(groups, shards, size // 3, t)
        for k, size in enumerate(sizes)
        for t in range(3)
    ]


def halving_walk(first, plan, dp, me):
    offsets, bits, peers = [first], [], []
    for axis, bit, n, halved in plan:
        index = dp if axis == "dp" else me
        b = lax.rem(index // 2**bit, 2)
        other = index + 2**bit * (1 - 2 * b)
        peers.append((other, me) if axis == "dp" else (dp, other))
        bits.append(b)
        offsets.append(offsets[-1] + b * (n // 2) if halved else offsets[-1])
    return offsets, bits, peers


def sorted_peers(groups, shards, dp, me):
    out = []
    for axis, count in (("dp", groups), ("lat", shards)):
        index = dp if axis == "dp" else me
        for bit in range(count.bit_length() - 1):
            other = index + 2**bit * (1 - 2 * lax.rem(index // 2**bit, 2))
            out.append((other, me) if axis == "dp" else (dp, other))
    return out


def rows_at(start, n, unit=8):
    return pl.ds(pl.multiple_of(start, unit), n)


def low_rows_at(start, n):
    return rows_at(start, n, LOW_ROWS)


def signal_all(devices):
    barrier = pltpu.get_barrier_semaphore()
    for device in devices:
        pl.semaphore_signal(barrier, inc=1, device_id=device, device_id_type=MESH)
    pl.semaphore_wait(barrier, len(devices))


def received(plan):
    return sum(n // 2 if halved else n for _, _, n, halved in plan)


class Halving:
    def __init__(self, plans, accs, recvs, send_sems, recv_sems, dp, me):
        self.plans, self.accs, self.recvs = plans, accs, recvs
        self.send_sems, self.recv_sems = send_sems, recv_sems
        self.walks = [halving_walk(first, plan, dp, me) for _, first, plan, _ in plans]
        self.stages = len(plans[0][2])

    def base(self, j, stage):
        k, _, plan, _ = self.plans[j]
        before = sum(received(p) for which, _, p, _ in self.plans[:j] if which == k)
        return before + received(plan[:stage])

    def copy(self, j, stage):
        k = self.plans[j][0]
        _, _, n, halved = self.plans[j][2][stage]
        offsets, bits, peers = self.walks[j]
        count = n // 2 if halved else n
        start = offsets[stage] + (1 - bits[stage]) * count if halved else offsets[stage]
        return pltpu.make_async_remote_copy(
            src_ref=self.accs[k].at[low_rows_at(start, count)],
            dst_ref=self.recvs[k].at[pl.ds(self.base(j, stage), count)],
            send_sem=self.send_sems.at[j, stage], recv_sem=self.recv_sems.at[j, stage],
            device_id=peers[stage], device_id_type=MESH,
        )

    def start(self, stage):
        for j in range(len(self.plans)):
            self.copy(j, stage).start()

    def finish(self, stage):
        for j in range(len(self.plans)):
            self.copy(j, stage).wait()
            k = self.plans[j][0]
            _, _, n, halved = self.plans[j][2][stage]
            count = n // 2 if halved else n
            first = self.walks[j][0][stage + 1]
            base = self.base(j, stage)
            acc, recv = self.accs[k], self.recvs[k]
            most = 98304 // acc.shape[1]
            step = max(c for c in range(LOW_ROWS, most + 1, LOW_ROWS) if count % c == 0)

            def add(i, _):
                mine = low_rows_at(first + i * step, step)
                other = low_rows_at(base + i * step, step)
                acc[mine, :] = (acc[mine, :].astype(F32) + recv[other, :].astype(F32)).astype(BF16)
                return 0

            lax.fori_loop(0, count // step, add, 0)

    def tick(self, stage):
        self.finish(stage)
        if stage + 1 < self.stages:
            self.start(stage + 1)

    def keep(self, refs):
        at = [0] * len(refs)
        for j, (k, _, _, n) in enumerate(self.plans):
            refs[k][at[k] : at[k] + n, :] = self.accs[k][low_rows_at(self.walks[j][0][-1], n), :]
            at[k] += n


def strided(ref, start, count, stride):
    return jnp.concatenate([ref[t, pl.ds(start, count, stride=stride), :] for t in range(ref.shape[0])], 1)


def put_rows(ref, start, value):
    n = value.shape[0]
    for t in range(ref.shape[0]):
        ref[t, pl.ds(pl.multiple_of(start, 8), n), :] = value[:, t * LANES : (t + 1) * LANES]


def load_mode(wide_ref, m, slab, modes):
    re = strided(wide_ref, 2 * m, LAT_PAD, slab)
    im = strided(wide_ref, 2 * m + 1, LAT_PAD, slab)
    live = lax.axis_index("lat") * modes + m < KEPT
    value = jnp.concatenate([re, im], 0)
    return jnp.where(live, value, jnp.zeros_like(value)).astype(BF16)


def widen(recv_ref, wide_ref):
    shards, rows, slab, width = recv_ref.shape
    n = rows * slab

    def one(s, _):
        put_rows(wide_ref, s * n, recv_ref[s].astype(F32).reshape(n, width))
        return 0

    lax.fori_loop(0, shards, one, 0)
    if LAT % rows:
        first = LAT * slab
        last = (LAT // rows + 1) * n
        put_rows(wide_ref, first, jnp.zeros((last - first, width), F32))
    for s in range(-(-LAT // rows), shards):
        put_rows(wide_ref, s * n, jnp.zeros((n, width), F32))


def store_mode(out_s, m, value):
    put_rows(out_s, 2 * m * LAT_PAD, value)


def emit_slabs(out_s, out_ref):
    shards, rows, slab, _ = out_ref.shape

    def one(s, _):
        for r in range(rows):
            out_ref[s, r] = strided(out_s, s * rows + r, slab, LAT_PAD).astype(BF16)
        return 0

    lax.fori_loop(0, shards, one, 0)


def each_mode(modes, fn, between=None):
    few = next(n for n in (3, 2, 1) if modes % n == 0)

    def some(j, _):
        if between is not None:
            between(j * few)
        for u in range(few):
            fn(j * few + u)
        return 0

    lax.fori_loop(0, modes // few, some, 0)


def spread_blocks(w_ref, dense_s):
    _, blocks, n, _ = w_ref.shape
    dense_s[...] = jnp.zeros_like(dense_s)
    for p in range(2):
        for b in range(blocks):
            at = (p * blocks + b) * n
            dense_s[b * n : (b + 1) * n, at : at + n] = w_ref[p, b]


def pick_blocks(dense_ref, out_ref):
    _, blocks, n, lanes = out_ref.shape
    for p in range(2):
        for b in range(blocks):
            at = (p * blocks + b) * n
            block = dense_ref[b * n : (b + 1) * n, at : at + n]
            out_ref[p, b] = jnp.concatenate([block, jnp.zeros((n, lanes - n), F32)], 1)


def spectral_forward_kernel(
    recv_ref, fa_ref, ia_ref, wi_ref, wo_ref, v_ref,
    out_ref, freq_ref, hid_ref, gp_ref, t2_ref, wide_s, out_s, wi_s, wo_s,
):
    slab, width = recv_ref.shape[2:]
    modes = freq_ref.shape[0]
    h = LAT_PAD
    widen(recv_ref, wide_s)
    spread_blocks(wi_ref, wi_s)
    spread_blocks(wo_ref, wo_s)
    if slab != 2 * modes:
        out_s[...] = jnp.zeros_like(out_s)

    def mix(v, w_ref, bias):
        a = dot(v, w_ref[...])
        re = a[:h, :width] - a[h:, width:] + vector(v_ref, bias)
        im = a[h:, :width] + a[:h, width:] + vector(v_ref, bias + 1)
        return jnp.concatenate([re, im], 0)

    def one(m):
        fq = dot(fa_ref[...], load_mode(wide_s, m, slab, modes)).astype(BF16)
        freq_ref[m] = fq
        hid, gp = gelu_both(mix(fq, wi_s, INNER_B))
        hid = hid.astype(BF16)
        hid_ref[m] = hid
        gp_ref[m] = gp
        outer = mix(hid, wo_s, OUTER_B)
        t = jnp.tanh(outer * (1.0 / SHRINK))
        t2_ref[m] = t * t
        shrunk = (outer - SHRINK * t).astype(BF16)
        store_mode(out_s, m, dot(ia_ref[...], shrunk))

    each_mode(modes, one)
    emit_slabs(out_s, out_ref)


def group_specs(shards, rows, slab, modes, part):
    n = 2 * LAT_PAD
    slabs = pl.BlockSpec((shards, rows, slab, part), lambda g: (0, 0, 0, g))
    spec = pl.BlockSpec((modes, n, part), lambda g: (0, 0, g))
    pair = pl.BlockSpec((2, part), lambda g: (0, g))
    return slabs, spec, pair


def weight_spec(weight, lanes=None):
    _, blocks, n, _ = weight.shape
    return pl.BlockSpec((2, blocks // GROUPS, n, lanes or n), lambda g: (0, g, 0, 0))


def spectral_forward(recv, tb, wi, wo, vectors, modes):
    shards, rows, slab, width = recv.shape
    part = width // GROUPS
    n = 2 * LAT_PAD
    slabs, spec, _ = group_specs(shards, rows, slab, modes, part)
    lines = pl.BlockSpec((vectors.shape[0], part), lambda g: (0, g))
    return pl.pallas_call(
        spectral_forward_kernel,
        grid=(GROUPS,),
        in_specs=[slabs, full(tb["fa"]), full(tb["ia"]), weight_spec(wi), weight_spec(wo), lines],
        out_specs=[slabs, spec, spec, spec, spec],
        out_shape=[
            sds(recv.shape, BF16),
            sds((modes, n, width), BF16),
            sds((modes, n, width), BF16),
            sds((modes, n, width), F32),
            sds((modes, n, width), F32),
        ],
        scratch_shapes=[
            pltpu.VMEM((part // LANES, shards * rows * slab, LANES), F32),
            pltpu.VMEM((part // LANES, slab * LAT_PAD, LANES), F32),
            pltpu.VMEM((part, 2 * part), BF16),
            pltpu.VMEM((part, 2 * part), BF16),
        ],
        compiler_params=params(),
        name="spectral_forward",
    )(recv, tb["fa"], tb["ia"], wi, wo, vectors)


def spectral_backward_kernel(
    groups, plans, recv_ref, iat_ref, fat_ref, wo_ref, wi_ref, freq_ref, hid_ref, gp_ref, t2_ref, dw1_ref, dw2_ref,
    out_ref, dwo_ref, dbo_ref, dwi_ref, dbi_ref, part1_ref, part2_ref,
    wide_s, out_s, wo_s, wi_s, dwo_s, dwi_s, acc1_s, acc2_s, recv1_s, recv2_s, load_sem, send_sems, recv_sems,
):
    shards = recv_ref.shape[0]
    slab, width = recv_ref.shape[2:]
    modes = freq_ref.shape[0]
    h = LAT_PAD
    g = pl.program_id(0)
    me = lax.axis_index("lat")
    dp = lax.axis_index("dp")
    halving = Halving(plans, (acc1_s, acc2_s), (recv1_s, recv2_s), send_sems, recv_sems, dp, me)
    loads = [
        pltpu.make_async_copy(dw1_ref, acc1_s, load_sem.at[0]),
        pltpu.make_async_copy(dw2_ref, acc2_s, load_sem.at[1]),
    ]

    @pl.when(g == 0)
    def _():
        for copy in loads:
            copy.start()
        signal_all(sorted_peers(groups, shards, dp, me))
        for copy in loads:
            copy.wait()
        halving.start(0)

    whole = GROUPS * modes
    early = [whole * n // 8 // 3 * 3 for n in (1, 4, 6, 7)]

    widen(recv_ref, wide_s)
    spread_blocks(wo_ref, wo_s)
    spread_blocks(wi_ref, wi_s)
    if slab != 2 * modes:
        out_s[...] = jnp.zeros_like(out_s)
    for ref in (dwo_s, dbo_ref, dwi_s, dbi_ref):
        ref[...] = jnp.zeros_like(ref)

    def grads(value, grad, dw_ref, db_ref):
        re, im = grad[:h], grad[h:]
        low_re, low_im = re.astype(BF16), im.astype(BF16)
        low = jnp.concatenate([low_re, low_im], 0)
        turned = jnp.concatenate([low_im, -low_re], 0)
        dw_ref[...] += dot_tn(value, jnp.concatenate([low, turned], 1))
        db_ref[0:1] += jnp.sum(low_re.astype(F32), 0, keepdims=True)
        db_ref[1:2] += jnp.sum(low_im.astype(F32), 0, keepdims=True)
        return low

    def pull(v, w_ref):
        a = dot_nt(v, w_ref[:, :width])
        b = dot_nt(v, w_ref[:, width:])
        return jnp.concatenate([a[:h] + b[h:], a[h:] - b[:h]], 0)

    def between(m):
        for stage, when in enumerate(early):
            pl.when(g * modes + m == when)(functools.partial(halving.tick, stage))

    def one(m):
        merged = dot(iat_ref[...], load_mode(wide_s, m, slab, modes))
        og = grads(hid_ref[m], merged * t2_ref[m], dwo_s, dbo_ref)
        ig = grads(freq_ref[m], pull(og, wo_s) * gp_ref[m], dwi_s, dbi_ref)
        fg = pull(ig, wi_s).astype(BF16)
        store_mode(out_s, m, dot(fat_ref[...], fg))

    each_mode(modes, one, between)
    pick_blocks(dwo_s, dwo_ref)
    pick_blocks(dwi_s, dwi_ref)
    emit_slabs(out_s, out_ref)

    @pl.when(g == GROUPS - 1)
    def _():
        for stage in range(len(early), halving.stages):
            halving.tick(stage)
        halving.keep((part1_ref, part2_ref))


def spectral_backward(recv, tb, wo, wi, freq, hid, gp, t2, dw1, dw2, groups, plans, collective_id):
    shards, rows, slab, width = recv.shape
    modes = freq.shape[0]
    part = width // GROUPS
    slabs, spec, pair = group_specs(shards, rows, slab, modes, part)
    dw = sds(wo.shape[:3] + (LANES,), F32)
    grad = weight_spec(wo, LANES)
    db = sds((2, width), F32)
    any_ = pl.BlockSpec(memory_space=pl.ANY)
    whole = lambda n, w: pl.BlockSpec((n, w), lambda g: (0, 0))
    n1, n2 = (sum(n for k, _, _, n in plans if k == which) for which in range(2))
    stages = len(plans[0][2])
    dma = pltpu.SemaphoreType.DMA
    return pl.pallas_call(
        functools.partial(spectral_backward_kernel, groups, plans),
        grid=(GROUPS,),
        in_specs=[slabs, full(tb["iat"]), full(tb["fat"]), weight_spec(wo), weight_spec(wi), spec, spec, spec, spec]
        + [any_, any_],
        out_specs=[slabs, grad, pair, grad, pair, whole(n1, dw1.shape[1]), whole(n2, dw2.shape[1])],
        out_shape=[
            sds(recv.shape, BF16), dw, db, dw, db,
            sds((n1, dw1.shape[1]), BF16), sds((n2, dw2.shape[1]), BF16),
        ],
        scratch_shapes=[
            pltpu.VMEM((part // LANES, shards * rows * slab, LANES), F32),
            pltpu.VMEM((part // LANES, slab * LAT_PAD, LANES), F32),
            pltpu.VMEM((part, 2 * part), BF16),
            pltpu.VMEM((part, 2 * part), BF16),
            pltpu.VMEM((part, 2 * part), F32),
            pltpu.VMEM((part, 2 * part), F32),
            pltpu.VMEM(dw1.shape, BF16),
            pltpu.VMEM(dw2.shape, BF16),
            pltpu.VMEM((sum(received(p) for k, _, p, _ in plans if k == 0), dw1.shape[1]), BF16),
            pltpu.VMEM((sum(received(p) for k, _, p, _ in plans if k == 1), dw2.shape[1]), BF16),
            dma((2,)), dma((len(plans), stages)), dma((len(plans), stages)),
        ],
        compiler_params=params(collective_id=collective_id, has_side_effects=True),
        name="spectral_backward",
    )(recv, tb["iat"], tb["fat"], wo, wi, freq, hid, gp, t2, dw1, dw2)


def gather_row(r_ref, row, modes):
    shards, _, slab, width = r_ref.shape
    whole = KEPT // modes
    parts = [r_ref[:whole, row].astype(F32).reshape(whole * slab, width)]
    rest = (shards - whole) * slab
    if KEPT % modes:
        n = up8(2 * (KEPT % modes))
        parts.append(r_ref[whole, row].astype(F32)[:n])
        rest -= n
    if rest:
        parts.append(jnp.zeros((rest, width), F32))
    return jnp.concatenate(parts, 0).astype(BF16)


def feed_kernel(
    per, chunk, hops, modes, scale_ref, x_ref, c_ref, back_ref, il_ref, ilt_ref, w1_ref, w2_ref, v_ref,
    lo_ref, mg_ref, out_ref, dw1_ref, dw2_ref, deb_ref, drb_ref, dpg_ref, dps_ref,
    slab_s, w1_s, w2_s, act_s, pre_s, sec_s, sect_s, up_s, mixed_s, xhat_s, rs_s, branch_s, grad_s,
    w_sem, dw_sem, in_send, in_recv, in_own, out_send, out_recv, out_own,
):
    g = pl.program_id(0)
    steps = pl.num_programs(0)
    lon, width = x_ref.shape[1:]
    hidden = w1_s.shape[1]
    shards, rows, slab, _ = slab_s.shape
    hop = rows // hops
    every = steps // hops
    tall = per * COLS
    me = lax.axis_index("lat")
    dp = lax.axis_index("dp")

    def transfer(src, dst, sems, h, i, sender, receiver, row_owner, mode_owner, act):
        part = pl.ds(h * hop, hop)

        def piece(nr, ns):
            act(send(
                src.at[receiver, part, pl.ds(0, ns)], dst.at[sender, part, pl.ds(0, ns)],
                sems[0].at[h, i], sems[1].at[h, i], dp, receiver,
            ))

        live = row_owner * rows + h * hop < LAT
        each_size([(live, hop)], slab_sizes(mode_owner, modes, slab), piece)

    def incoming(h, i, sender, receiver, act):
        transfer(back_ref, slab_s, (in_send, in_recv), h, i, sender, receiver, receiver, sender, act)

    def outgoing(h, i, sender, receiver, act):
        transfer(slab_s, out_ref, (out_send, out_recv), h, i, sender, receiver, sender, receiver, act)

    def own_in(h):
        part = pl.ds(h * hop, hop)
        return pltpu.make_async_copy(back_ref.at[me, part], slab_s.at[me, part], in_own.at[h])

    def own_out(h):
        part = pl.ds(h * hop, hop)
        return pltpu.make_async_copy(slab_s.at[me, part], out_ref.at[me, part], out_own.at[h])

    def to(i):
        return lax.rem(me + i, shards)

    def source(i):
        return lax.rem(me + shards - i, shards)

    def peers(fn):
        def one(i, _):
            fn(i)
            return 0

        lax.fori_loop(1, shards, one, 0)

    def fetch(h):
        own_in(h).start()
        peers(lambda i: incoming(h, i, me, to(i), lambda c: c.start()))

    weights = [
        pltpu.make_async_copy(w1_ref, w1_s, w_sem.at[0]),
        pltpu.make_async_copy(w2_ref, w2_s, w_sem.at[1]),
    ]

    @pl.when(g == 0)
    def _():
        for copy in weights:
            copy.start()
        greet(shards, me, dp)
        fetch(0)
        for ref in (deb_ref, drb_ref, dpg_ref, dps_ref):
            ref[...] = jnp.zeros_like(ref)

    @pl.when(lax.rem(g, every) == 0)
    def _():
        h = g // every
        own_in(h).wait()
        peers(lambda i: incoming(h, i, source(i), me, lambda c: c.wait_recv()))

        @pl.when(h + 1 < hops)
        def _():
            fetch(h + 1)

    at = pl.ds(0 if rows == per else pl.multiple_of(g * tall, tall), tall)
    for i in range(per):
        rows_i = pl.ds(i * COLS, COLS)
        x = pad_rows(x_ref[i].astype(F32), COLS)
        c, rs = center_scale(x)
        first = c * rs * vector(v_ref, NORM_G) + vector(v_ref, NORM_S)
        filtered = dot(il_ref[...], gather_row(slab_s, g * per + i, modes))
        live = me * rows + g * per + i < LAT
        mixed = jnp.where(live, filtered, jnp.zeros_like(filtered)) + first + x
        c, rs = center_scale(mixed)
        xhat = c * rs
        mixed_s[rows_i, :] = mixed
        xhat_s[rows_i, :] = xhat
        rs_s[rows_i, :] = jnp.broadcast_to(rs, (COLS, LANES))
        sec_s[rows_i, :] = (xhat * vector(v_ref, POST_G) + vector(v_ref, POST_S)).astype(BF16)
        up = (pad_rows(c_ref[i].astype(F32), COLS) * scale_ref[0, g * per + i]).astype(BF16)
        up_s[pl.ds(pl.multiple_of(g * tall + i * COLS, COLS), COLS), :] = up
        drb_ref[...] += jnp.sum(up.astype(F32), 0, keepdims=True)
    sect_s[:, at] = sec_s[...].T
    branch_s[...] = jnp.broadcast_to(vector(v_ref, REDUCE_B), branch_s.shape)
    grad_s[...] = jnp.zeros_like(grad_s)

    @pl.when(g == 0)
    def _():
        for copy in weights:
            copy.wait()

    def hidden_chunk(j, _):
        ds = pl.ds(pl.multiple_of(j * chunk, chunk), chunk)
        act, slope = gelu_both(dot(sec_s[...], w1_s[:, ds]) + v_ref[pl.ds(EXPAND_B + j, 1), :])
        act = act.astype(BF16)
        act_s[at, ds] = act
        pre = (dot_nt(up_s[at, :], w2_s[ds, :]) * slope).astype(BF16)
        pre_s[at, ds] = pre
        deb_ref[pl.ds(j, 1), :] += jnp.sum(pre.astype(F32), 0, keepdims=True)
        branch_s[...] += dot(act, w2_s[ds, :])
        grad_s[...] += dot_nt(pre, w1_s[:, ds])
        return 0

    lax.fori_loop(0, hidden // chunk, hidden_chunk, 0)
    for i in range(per):
        rows_i = pl.ds(i * COLS, COLS)
        grad = grad_s[rows_i, :]
        xhat = xhat_s[rows_i, :]
        up = pad_rows(c_ref[i].astype(F32), COLS) * scale_ref[0, g * per + i]
        mg = up + norm_back(grad, xhat, rs_s[rows_i, 0:1], vector(v_ref, POST_G))
        mg_ref[i] = mg[:lon]
        rg = dot(ilt_ref[...], mg.astype(BF16)).astype(BF16)
        slab_s[:, g * per + i] = rg.reshape(shards, slab, width)

    @pl.when(lax.rem(g, every) == every - 1)
    def _():
        h = g // every
        own_out(h).start()
        peers(lambda i: outgoing(h, i, me, to(i), lambda c: c.start()))

    for i in range(per):
        rows_i = pl.ds(i * COLS, COLS)
        keep = scale_ref[1, g * per + i]
        lo_ref[i] = ((mixed_s[rows_i, :] + branch_s[rows_i, :]) * keep).astype(BF16)[:lon]
        grad = grad_s[rows_i, :]
        dpg_ref[...] += jnp.sum(grad * xhat_s[rows_i, :], 0, keepdims=True)
        dps_ref[...] += jnp.sum(grad, 0, keepdims=True)

    def gradients(j):
        ds = pl.ds(pl.multiple_of(j * chunk, chunk), chunk)
        side = dw1_ref.shape[1] // chunk
        place = (
            pl.ds(pl.multiple_of(j // side * width, width), width),
            pl.ds(pl.multiple_of(lax.rem(j, side) * chunk, chunk), chunk),
        )
        return (
            pltpu.make_async_copy(w1_s.at[:, ds], dw1_ref.at[place], dw_sem.at[0, j]),
            pltpu.make_async_copy(w2_s.at[ds, :], dw2_ref.at[ds, :], dw_sem.at[1, j]),
        )

    @pl.when(g == steps - 1)
    def _():
        def weight_chunk(j, _):
            ds = pl.ds(pl.multiple_of(j * chunk, chunk), chunk)
            w1_s[:, ds] = dot(sect_s[...], pre_s[:, ds]).astype(BF16)
            w2_s[ds, :] = dot_tn(act_s[:, ds], up_s[...]).astype(BF16)
            for copy in gradients(j):
                copy.start()
            return 0

        lax.fori_loop(0, hidden // chunk, weight_chunk, 0)

        def one(h, _):
            own_out(h).wait()

            def wait_all(i):
                incoming(h, i, me, to(i), lambda c: c.wait_send())
                outgoing(h, i, me, to(i), lambda c: c.wait_send())
                outgoing(h, i, source(i), me, lambda c: c.wait_recv())

            peers(wait_all)
            return 0

        lax.fori_loop(0, hops, one, 0)

        def finish(j, _):
            for copy in gradients(j):
                copy.wait()
            return 0

        lax.fori_loop(0, hidden // chunk, finish, 0)


def feed(scale, x, cot, back, tb, w1, w2, vectors, modes, collective_id):
    rows, lon, width = x.shape
    hidden = w1.shape[1]
    shards, _, slab, _ = back.shape
    per = next(n for n in (2, 3, 1) if rows % n == 0)
    steps = rows // per
    hops = 2 if steps % 2 == 0 else 1
    chunk = width
    row = pl.BlockSpec((per, lon, width), lambda g: (g, 0, 0))
    any_ = pl.BlockSpec(memory_space=pl.ANY)
    vec = lambda n: pl.BlockSpec((n, width), lambda g: (0, 0))
    tall = per * COLS
    total = rows * COLS
    dma = pltpu.SemaphoreType.DMA
    return pl.pallas_call(
        functools.partial(feed_kernel, per, chunk, hops, modes),
        grid=(steps,),
        in_specs=[
            pl.BlockSpec(memory_space=pltpu.SMEM), row, row, any_, full(tb["il"]), full(tb["ilt"]), any_, any_,
            full(vectors),
        ],
        out_specs=[row, row, any_, any_, any_, vec(hidden // width), vec(1), vec(1), vec(1)],
        out_shape=[
            sds((rows, lon, width), BF16),
            sds((rows, lon, width), F32),
            sds(back.shape, BF16),
            sds((2 * width, hidden // 2), BF16),
            sds(w2.shape, BF16),
            sds((hidden // width, width), F32),
            sds((1, width), F32),
            sds((1, width), F32),
            sds((1, width), F32),
        ],
        scratch_shapes=[
            pltpu.VMEM(back.shape, BF16),
            pltpu.VMEM(w1.shape, BF16),
            pltpu.VMEM(w2.shape, BF16),
            pltpu.VMEM((total, hidden), BF16),
            pltpu.VMEM((total, hidden), BF16),
            pltpu.VMEM((tall, width), BF16),
            pltpu.VMEM((width, total), BF16),
            pltpu.VMEM((total, width), BF16),
            pltpu.VMEM((tall, width), F32),
            pltpu.VMEM((tall, width), F32),
            pltpu.VMEM((tall, LANES), F32),
            pltpu.VMEM((tall, width), F32),
            pltpu.VMEM((tall, width), F32),
            dma((2,)), dma((2, hidden // chunk)),
            dma((hops, shards)), dma((hops, shards)), dma((hops,)),
            dma((hops, shards)), dma((hops, shards)), dma((hops,)),
        ],
        compiler_params=pltpu.CompilerParams(
            vmem_limit_bytes=63 * 2**20, collective_id=collective_id, has_side_effects=True
        ),
        name="feed",
    )(scale, x, cot, back, tb["il"], tb["ilt"], w1, w2, vectors)


def leave_kernel(
    groups, hops, modes, plans, x_ref, back_ref, mg_ref, fl_ref, v_ref, *refs,
):
    weight_refs, line_refs, refs = refs[:2], refs[2:8], refs[8:]
    (
        part1_ref, part2_ref, out_ref, sums_ref, norm_ref, dw1_ref, dw2_ref,
        slab_s, line_s, mine_s, from_dp, part_s, from_lat, all_s, norm_lat, norm_dp,
        in_send, in_recv, in_own, wide_send, wide_recv, own_sem, small_sems,
    ) = refs
    g = pl.program_id(0)
    steps = pl.num_programs(0)
    lon = x_ref.shape[1]
    shards, rows, slab, _ = slab_s.shape
    n = from_lat.shape[1]
    hop = rows // hops
    me = lax.axis_index("lat")
    dp = lax.axis_index("dp")
    lat_peers = [lax.rem(me + i, shards) for i in range(1, shards)]
    dp_peers = [lax.rem(dp + i, groups) for i in range(1, groups)]

    def incoming(h, i, sender, receiver, act):
        part = pl.ds(h * hop, hop)

        def piece(nr, ns):
            act(send(
                back_ref.at[receiver, part, pl.ds(0, ns)], slab_s.at[sender, part, pl.ds(0, ns)],
                in_send.at[h, i], in_recv.at[h, i], dp, receiver,
            ))

        live = receiver * rows + h * hop < LAT
        each_size([(live, hop)], slab_sizes(sender, modes, slab), piece)

    def own_in(h):
        part = pl.ds(h * hop, hop)
        return pltpu.make_async_copy(back_ref.at[me, part], slab_s.at[me, part], in_own.at[h])

    def peers(fn):
        def one(i, _):
            fn(i)
            return 0

        lax.fori_loop(1, shards, one, 0)

    def fetch(h):
        own_in(h).start()
        peers(lambda i: incoming(h, i, me, lax.rem(me + i, shards), lambda c: c.start()))

    def arrived(h):
        own_in(h).wait()
        peers(lambda i: incoming(h, i, lax.rem(me + shards - i, shards), me, lambda c: c.wait_recv()))

    walks = [halving_walk(first, plan, dp, me) for _, first, plan, _ in plans]
    outs = (dw1_ref, dw2_ref)
    parts = (part1_ref, part2_ref)
    stages = len(plans[0][2])
    count = len(plans)

    def part(j):
        k, _, _, n = plans[j]
        at = sum(rest for which, _, _, rest in plans[:j] if which == k)
        return parts[k].at[pl.ds(at, n)]

    def own_part(j):
        k, _, _, n = plans[j]
        return pltpu.make_async_copy(part(j), outs[k].at[low_rows_at(walks[j][0][-1], n)], own_sem.at[j])

    def spread(j, stage):
        k, _, plan, _ = plans[j]
        _, _, n, halved = plan[stage]
        if not halved:
            return None
        where = low_rows_at(walks[j][0][stage + 1], n // 2)
        first = not any(later[3] for later in plan[stage + 1 :])
        return pltpu.make_async_remote_copy(
            src_ref=part(j) if first else outs[k].at[where], dst_ref=outs[k].at[where],
            send_sem=wide_send.at[j, stage], recv_sem=wide_recv.at[j, stage],
            device_id=walks[j][2][stage], device_id_type=MESH,
        )

    def spread_all(stage, act):
        for j in range(count):
            copy = spread(j, stage)
            if copy is not None:
                act(copy)

    def tick(i):
        stage = stages - 1 - i
        spread_all(stage, lambda c: c.wait())
        if i == 0:
            for j in range(count):
                own_part(j).wait()
        if stage:
            spread_all(stage - 1, lambda c: c.start())


    def remote(src, dst, stage, i, to):
        return pltpu.make_async_remote_copy(
            src_ref=src, dst_ref=dst, send_sem=small_sems.at[stage, 0, i], recv_sem=small_sems.at[stage, 1, i],
            device_id=to, device_id_type=MESH,
        )

    def over(peers_, axis):
        return [(i, p, (p, me) if axis == "dp" else (dp, p)) for i, p in enumerate(peers_)]

    block = shards * n
    mine = rows_at((dp * shards + me) * n, n)
    mine_dp = rows_at(dp * block, block)
    tiles = line_s.shape[1] // LANES

    def small(stage):
        if stage == 0:
            return [
                remote(mine_s.at[rows_at(p * block, block)], from_dp.at[i], 0, i, to)
                for i, p, to in over(dp_peers, "dp")
            ]
        if stage == 1:
            return [
                remote(part_s.at[rows_at(p * n, n)], from_lat.at[i], 1, i, to)
                for i, p, to in over(lat_peers, "lat")
            ]
        if stage == 2:
            return [remote(all_s.at[mine], all_s.at[mine], 2, i, to) for i, p, to in over(lat_peers, "lat")]
        if stage == 3:
            return [remote(all_s.at[mine_dp], all_s.at[mine_dp], 3, i, to) for i, p, to in over(dp_peers, "dp")]
        if stage == 4:
            return [remote(norm_lat.at[me], norm_lat.at[me], 4, i, to) for i, p, to in over(lat_peers, "lat")]
        return [remote(norm_dp.at[dp], norm_dp.at[dp], 5, i, to) for i, p, to in over(dp_peers, "dp")]

    def begin(stage):
        for copy in small(stage):
            copy.start()

    def end(stage):
        for copy in small(stage):
            copy.wait()
        if stage == 0:
            part_s[...] = mine_s[mine_dp, :] + jnp.sum(from_dp[...], 0)
        if stage == 1:
            all_s[mine, :] = part_s[rows_at(me * n, n), :] + jnp.sum(from_lat[...], 0)

    def small_tick(stage):
        end(stage)
        begin(stage + 1)

    @pl.when(g == 0)
    def _():
        at = 0
        for ref in weight_refs:
            value = ref[...].reshape(-1, LANES)
            mine_s[at : at + value.shape[0], :] = value
            at += value.shape[0]
        mine_s[at:, :] = jnp.zeros((mine_s.shape[0] - at, LANES), F32)
        for ref in line_refs:
            for row in range(ref.shape[0]):
                for t in range(tiles):
                    mine_s[at : at + 1, :] = ref[row : row + 1, t * LANES : (t + 1) * LANES]
                    at += 1
        signal_all([(dp, p) for p in lat_peers] + [(p, me) for p in dp_peers])
        for j in range(count):
            own_part(j).start()
        spread_all(stages - 1, lambda c: c.start())
        begin(0)
        fetch(0)
        line_s[...] = jnp.zeros_like(line_s)
        tick(0)
        small_tick(0)
        arrived(0)
        tick(1)
        small_tick(1)
        if hops > 1:
            fetch(1)

    for h in range(1, hops):
        pl.when(g == h * hop)(functools.partial(arrived, h))

    x = pad_rows(x_ref[0].astype(F32), COLS)
    c, rs = center_scale(x)
    xhat = c * rs
    mg = pad_rows(mg_ref[0], COLS)
    live = me * rows + g < LAT
    spectrum = dot(fl_ref[...], gather_row(slab_s, g, modes))
    grad = jnp.where(live, spectrum, jnp.zeros_like(spectrum)) + mg
    line_s[0:1] += jnp.sum(grad * xhat, 0, keepdims=True)
    line_s[1:2] += jnp.sum(grad, 0, keepdims=True)
    out_ref[0] = (mg + norm_back(grad, xhat, rs, vector(v_ref, NORM_G)))[:lon]

    @pl.when(g == hop - 1)
    def _():
        tick(2)
        small_tick(2)

    @pl.when(g == steps - 1)
    def _():
        norm_lat[me] = line_s[...]
        begin(4)
        for i in range(3, stages):
            tick(i)
        end(4)
        norm_dp[dp] = jnp.sum(norm_lat[...], 0)
        begin(5)
        end(3)
        sums_ref[...] = all_s[...]
        for h in range(hops):
            peers(lambda i: incoming(h, i, me, lax.rem(me + i, shards), lambda c: c.wait_send()))
        end(5)
        norm_ref[...] = jnp.sum(norm_dp[...], 0)


def leave(x, back, mg, fl, vectors, small, part1, part2, shapes, groups, plans, modes, collective_id):
    rows, lon, width = x.shape
    shards, _, slab, _ = back.shape
    hops = 2 if rows % 2 == 0 else 1
    stages = len(plans[0][2])
    unit = 8 * groups * shards
    total = -(-sum(v.size // LANES for v in small) // unit) * unit
    n = total // (groups * shards)
    row = pl.BlockSpec((1, lon, width), lambda r: (r, 0, 0))
    any_ = pl.BlockSpec(memory_space=pl.ANY)
    whole = lambda *shape: pl.BlockSpec(shape, lambda r: (0,) * len(shape))
    dma = pltpu.SemaphoreType.DMA
    return pl.pallas_call(
        functools.partial(leave_kernel, groups, hops, modes, plans),
        grid=(rows,),
        in_specs=[row, any_, row, full(fl), full(vectors)] + [full(v) for v in small] + [any_, any_],
        out_specs=[row, whole(total, LANES), whole(2, width), any_, any_],
        out_shape=[sds((rows, lon, width), F32), sds((total, LANES), F32), sds((2, width), F32)]
        + [sds(shape, BF16) for shape in shapes],
        scratch_shapes=[
            pltpu.VMEM(back.shape, BF16),
            pltpu.VMEM((2, width), F32),
            pltpu.VMEM((total, LANES), F32),
            pltpu.VMEM((groups - 1, shards * n, LANES), F32),
            pltpu.VMEM((shards * n, LANES), F32),
            pltpu.VMEM((shards - 1, n, LANES), F32),
            pltpu.VMEM((total, LANES), F32),
            pltpu.VMEM((shards, 2, width), F32),
            pltpu.VMEM((groups, 2, width), F32),
            dma((hops, shards)), dma((hops, shards)), dma((hops,)),
            dma((len(plans), stages)), dma((len(plans), stages)), dma((len(plans),)),
            dma((6, 2, max(groups, shards) - 1)),
        ],
        compiler_params=params(collective_id=collective_id, has_side_effects=True),
        name="leave",
    )(x, back, mg, fl, vectors, *small, part1, part2)


def shards_fn(
    groups, shards, inputs, cotangent, storm_weight, norm_gain, norm_shift, inner_weight, inner_bias,
    outer_weight, outer_bias, post_gain, post_shift, expand_weight, expand_bias, reduce_weight, reduce_bias,
):
    _, rows, lon, width = inputs.shape
    modes = LON_PAD // shards
    slab = slab_rows(modes)
    tb = make_tables(shards, modes)
    row_ids = lax.axis_index("lat") * rows + jnp.arange(rows, dtype=jnp.int32)
    keep = (row_ids < LAT).astype(F32)
    scale = jnp.stack([keep * (storm_weight[0].astype(F32) / 64.0), keep])
    x = inputs[0]
    cot = cotangent[0]
    vectors = jnp.concatenate([
        norm_gain, norm_shift, post_gain, post_shift, reduce_bias,
        inner_bias.reshape(-1), outer_bias.reshape(-1), expand_bias,
    ]).reshape(-1, width)

    spec = exchange(enter(x, tb["flt"], vectors, shards, slab), True, modes, 0)
    back, freq, hid, gp, t2 = spectral_forward(spec, tb, inner_weight, outer_weight, vectors, modes)
    (layer_out, mixed_grad, mode_grad, dw1, dw2, deb, drb, dpg, dps) = feed(
        scale, x, cot, back, tb, expand_weight, reduce_weight, vectors, modes, 1
    )
    plans = halving_plans(groups, shards, (dw1.shape[0], dw2.shape[0]))
    slab_grad, dwo, dbo, dwi, dbi, part1, part2 = spectral_backward(
        mode_grad, tb, outer_weight, inner_weight, freq, hid, gp, t2, dw1, dw2, groups, plans, 2
    )
    small = (dwi, dwo, dbi, dbo, dpg, dps, deb, drb)
    input_grad, sums, norm, dw1, dw2 = leave(
        x, slab_grad, mixed_grad, tb["fl"], vectors, small, part1, part2,
        (dw1.shape, dw2.shape), groups, plans, modes, 3
    )
    dw1 = jnp.concatenate([dw1[:width], dw1[width:]], 1).astype(F32)
    dw2 = dw2.astype(F32)
    ends = np.cumsum([v.size // LANES for v in small])
    dwi, dwo, dbi, dbo, dpg, dps, deb, drb = [
        sums[e - v.size // LANES : e] for v, e in zip(small, ends)
    ]
    block = inner_weight.shape[-1]
    weight = lambda v: v.reshape(inner_weight.shape[:3] + (LANES,))[..., :block]
    line = lambda v: v.reshape(-1)
    return (
        layer_out[None], input_grad[None], norm[0], norm[1],
        weight(dwi), dbi.reshape(inner_bias.shape), weight(dwo), dbo.reshape(outer_bias.shape),
        line(dpg), line(dps), dw1, line(deb), dw2, line(drb),
    )


def solution(mesh):
    split = P("dp", "lat", None, None)
    return jax.shard_map(
        functools.partial(shards_fn, mesh.shape["dp"], mesh.shape["lat"]),
        mesh=mesh,
        in_specs=(split, split, P("dp")) + (P(),) * 12,
        out_specs=(split, split) + (P(),) * 12,
        check_vma=False,
    )
```

```python
import functools
import math

import jax
import jax.numpy as jnp
import ml_dtypes
import numpy as np
from jax import lax
from jax.experimental import pallas as pl
from jax.experimental.pallas import tpu as pltpu
from jax.sharding import PartitionSpec as P

BLOCKS = 8
LAT = 90
LON = 180
LAT_PAD = 96
LON_PAD = 96
KEPT = LON // 2 + 1
COLS = 192
GROUPS = 2
LANES = 128
LOW_ROWS = 16
NORM_G, NORM_S, POST_G, POST_S, REDUCE_B, INNER_B, OUTER_B, EXPAND_B = 0, 1, 2, 3, 4, 5, 7, 9

SHRINK = 0.01
EPS = 1e-6
SQRT_HALF = 0.7071067811865476
PDF_SCALE = 0.3989422804014327

F32 = jnp.float32
BF16 = jnp.bfloat16
MESH = pl.DeviceIdType.MESH
VMEM_LIMIT = 62 * 2**20


def base_tables():
    f = np.float32
    modes = np.arange(LON_PAD)
    columns = np.arange(LON)
    phases = (columns[:, None] * modes[None, :] % LON).astype(f) * f(2.0 * math.pi / LON)
    kept = (modes < LON // 2 + 1).astype(f)
    factor = np.where((modes == 0) | (modes == LON // 2), f(1), f(2)) * kept
    scale = f(1.0 / math.sqrt(LON))
    forward_lon = np.stack([np.cos(phases) * kept, -np.sin(phases) * kept], axis=1) * scale
    inverse_lon = np.stack([np.cos(phases) * factor, -np.sin(phases) * factor], axis=1) * scale
    rows = np.arange(LAT_PAD)
    angles = (rows[:, None] * rows[None, :] % LAT).astype(f) * f(2.0 * math.pi / LAT)
    inside = ((rows[:, None] < LAT) & (rows[None, :] < LAT)).astype(f) / f(math.sqrt(LAT))
    cs = np.cos(angles) * inside
    sn = np.sin(angles) * inside
    forward_lat = np.stack([np.stack([cs, sn], 1), np.stack([-sn, cs], 1)], 0)
    inverse_lat = np.stack([np.stack([cs, -sn], 1), np.stack([sn, cs], 1)], 0)
    return forward_lon, inverse_lon, forward_lat, inverse_lat


def slab_rows(modes):
    return -(-2 * modes // 8) * 8


def lon_table(table, shards, modes):
    slab = slab_rows(modes)
    out = np.zeros((COLS, shards, slab), np.float32)
    split = table.reshape(LON, 2, shards, modes).transpose(0, 2, 3, 1)
    out[:LON, :, : 2 * modes] = split.reshape(LON, shards, 2 * modes)
    return out.reshape(COLS, shards * slab)


def make_tables(shards, modes):
    forward_lon, inverse_lon, forward_lat, inverse_lat = base_tables()
    low = lambda t: jnp.asarray(np.ascontiguousarray(t).astype(ml_dtypes.bfloat16))
    n = 2 * LAT_PAD
    fl = lon_table(forward_lon, shards, modes)
    il = lon_table(inverse_lon, shards, modes)
    fa = forward_lat.reshape(n, n)
    ia = inverse_lat.reshape(n, n)
    return dict(
        fl=low(fl), flt=low(fl.T), il=low(il), ilt=low(il.T),
        fa=low(fa), fat=low(fa.T), ia=low(ia), iat=low(ia.T),
    )


def dot(a, b):
    return jnp.dot(a, b, preferred_element_type=F32)


def dot_nt(a, b):
    return lax.dot_general(a, b, (((1,), (1,)), ((), ())), preferred_element_type=F32)


def dot_tn(a, b):
    return lax.dot_general(a, b, (((0,), (0,)), ((), ())), preferred_element_type=F32)


def gelu_both(v):
    cdf = 0.5 * (1.0 + lax.erf(v * SQRT_HALF))
    pdf = jnp.exp(-0.5 * v * v) * PDF_SCALE
    return v * cdf, cdf + v * pdf


def center_scale(v):
    inv = 1.0 / v.shape[-1]
    c = v - jnp.sum(v, -1, keepdims=True) * inv
    return c, lax.rsqrt(jnp.sum(c * c, -1, keepdims=True) * inv + EPS)


def pad_rows(v, n):
    return jnp.concatenate([v, jnp.zeros((n - v.shape[0], v.shape[1]), v.dtype)], 0)


def norm_back(grad, xhat, rs, gain):
    inv = 1.0 / grad.shape[-1]
    dx = grad * gain
    m1 = jnp.sum(dx, -1, keepdims=True) * inv
    m2 = jnp.sum(dx * xhat, -1, keepdims=True) * inv
    return rs * (dx - m1 - xhat * m2)


def full(a):
    return pl.BlockSpec(a.shape, lambda *_: (0,) * a.ndim, pipeline_mode=pl.Buffered(1))


def sds(shape, dtype):
    return jax.ShapeDtypeStruct(shape, dtype)


def params(**kw):
    return pltpu.CompilerParams(vmem_limit_bytes=VMEM_LIMIT, **kw)


def vector(v_ref, row):
    return v_ref[row : row + 1, :]


def up8(n):
    return -(-n // 8) * 8


def slab_sizes(index, modes, slab):
    sizes = [(index < KEPT // modes, slab)]
    if KEPT % modes:
        sizes.append((index == KEPT // modes, up8(2 * (KEPT % modes))))
    return sizes


def row_sizes(index, rows):
    sizes = [(index < LAT // rows, rows)]
    if LAT % rows:
        sizes.append((index == LAT // rows, LAT % rows))
    return sizes


def each_size(row_options, slab_options, fn):
    for row_ok, nr in row_options:
        for slab_ok, ns in slab_options:
            pl.when(row_ok & slab_ok)(functools.partial(fn, nr, ns))


def greet(shards, me, dp):
    barrier = pltpu.get_barrier_semaphore()

    def one(i, _):
        peer = lax.rem(me + i, shards)
        pl.semaphore_signal(barrier, inc=1, device_id=(dp, peer), device_id_type=MESH)
        return 0

    lax.fori_loop(1, shards, one, 0)
    pl.semaphore_wait(barrier, shards - 1)


def send(src, dst, send_sem, recv_sem, dp, peer):
    return pltpu.make_async_remote_copy(
        src_ref=src, dst_ref=dst, send_sem=send_sem, recv_sem=recv_sem,
        device_id=(dp, peer), device_id_type=MESH,
    )


def halving_plan(groups, shards, n, turn):
    dp_bits = [("dp", b) for b in range(groups.bit_length() - 1)]
    lat_bits = [("lat", b) for b in range(shards.bit_length() - 1)]
    middle = dp_bits[1:2] + lat_bits[:2]
    turn = turn % len(middle)
    order = dp_bits[:1] + middle[turn:] + middle[:turn] + dp_bits[2:] + lat_bits[2:]
    plan = []
    for axis, bit in order:
        halved = n % (2 * LOW_ROWS) == 0
        plan.append((axis, bit, n, halved))
        n = n // 2 if halved else n
    return plan, n


def halving_plans(groups, shards, sizes):
    return [
        (k, t * size // 3) + halving_plan(groups, shards, size // 3, t)
        for k, size in enumerate(sizes)
        for t in range(3)
    ]


def halving_walk(first, plan, dp, me):
    offsets, bits, peers = [first], [], []
    for axis, bit, n, halved in plan:
        index = dp if axis == "dp" else me
        b = lax.rem(index // 2**bit, 2)
        other = index + 2**bit * (1 - 2 * b)
        peers.append((other, me) if axis == "dp" else (dp, other))
        bits.append(b)
        offsets.append(offsets[-1] + b * (n // 2) if halved else offsets[-1])
    return offsets, bits, peers


def dp_halving_peers(groups, dp, me):
    bits = range(groups.bit_length() - 1)
    return [(dp + 2**bit * (1 - 2 * lax.rem(dp // 2**bit, 2)), me) for bit in bits]


def rows_at(start, n, unit=8):
    return pl.ds(pl.multiple_of(start, unit), n)


def low_rows_at(start, n):
    return rows_at(start, n, LOW_ROWS)


def signal_all(devices):
    barrier = pltpu.get_barrier_semaphore()
    for device in devices:
        pl.semaphore_signal(barrier, inc=1, device_id=device, device_id_type=MESH)
    pl.semaphore_wait(barrier, len(devices))


def received(plan):
    return sum(n // 2 if halved else n for _, _, n, halved in plan)


class Halving:
    def __init__(self, plans, accs, recvs, send_sems, recv_sems, dp, me):
        self.plans, self.accs, self.recvs = plans, accs, recvs
        self.send_sems, self.recv_sems = send_sems, recv_sems
        self.walks = [halving_walk(first, plan, dp, me) for _, first, plan, _ in plans]
        self.stages = len(plans[0][2])

    def base(self, j, stage):
        k, _, plan, _ = self.plans[j]
        before = sum(received(p) for which, _, p, _ in self.plans[:j] if which == k)
        return before + received(plan[:stage])

    def copy(self, j, stage):
        k = self.plans[j][0]
        _, _, n, halved = self.plans[j][2][stage]
        offsets, bits, peers = self.walks[j]
        count = n // 2 if halved else n
        start = offsets[stage] + (1 - bits[stage]) * count if halved else offsets[stage]
        return pltpu.make_async_remote_copy(
            src_ref=self.accs[k].at[low_rows_at(start, count)],
            dst_ref=self.recvs[k].at[pl.ds(self.base(j, stage), count)],
            send_sem=self.send_sems.at[j, stage], recv_sem=self.recv_sems.at[j, stage],
            device_id=peers[stage], device_id_type=MESH,
        )

    def start(self, stage):
        for j in range(len(self.plans)):
            self.copy(j, stage).start()

    def finish(self, stage):
        for j in range(len(self.plans)):
            self.copy(j, stage).wait()
            k = self.plans[j][0]
            _, _, n, halved = self.plans[j][2][stage]
            count = n // 2 if halved else n
            first = self.walks[j][0][stage + 1]
            base = self.base(j, stage)
            acc, recv = self.accs[k], self.recvs[k]
            most = 98304 // acc.shape[1]
            step = max(c for c in range(LOW_ROWS, most + 1, LOW_ROWS) if count % c == 0)

            def add(i, _):
                mine = low_rows_at(first + i * step, step)
                other = low_rows_at(base + i * step, step)
                acc[mine, :] = (acc[mine, :].astype(F32) + recv[other, :].astype(F32)).astype(BF16)
                return 0

            lax.fori_loop(0, count // step, add, 0)

    def tick(self, stage):
        self.finish(stage)
        if stage + 1 < self.stages:
            self.start(stage + 1)

    def keep(self, refs):
        at = [0] * len(refs)
        for j, (k, _, _, n) in enumerate(self.plans):
            refs[k][at[k] : at[k] + n, :] = self.accs[k][low_rows_at(self.walks[j][0][-1], n), :]
            at[k] += n


def strided(ref, start, count, stride):
    return jnp.concatenate([ref[t, pl.ds(start, count, stride=stride), :] for t in range(ref.shape[0])], 1)


def put_rows(ref, start, value):
    n = value.shape[0]
    for t in range(ref.shape[0]):
        ref[t, pl.ds(pl.multiple_of(start, 8), n), :] = value[:, t * LANES : (t + 1) * LANES]


def load_mode(wide_ref, m, slab, modes):
    re = strided(wide_ref, 2 * m, LAT_PAD, slab)
    im = strided(wide_ref, 2 * m + 1, LAT_PAD, slab)
    live = lax.axis_index("lat") * modes + m < KEPT
    value = jnp.concatenate([re, im], 0)
    return jnp.where(live, value, jnp.zeros_like(value)).astype(BF16)


def widen(recv_ref, wide_ref):
    shards, rows, slab, width = recv_ref.shape
    n = rows * slab

    def one(s, _):
        put_rows(wide_ref, s * n, recv_ref[s].astype(F32).reshape(n, width))
        return 0

    lax.fori_loop(0, shards, one, 0)
    if LAT % rows:
        first = LAT * slab
        last = (LAT // rows + 1) * n
        put_rows(wide_ref, first, jnp.zeros((last - first, width), F32))
    for s in range(-(-LAT // rows), shards):
        put_rows(wide_ref, s * n, jnp.zeros((n, width), F32))


def store_mode(out_s, m, value):
    put_rows(out_s, 2 * m * LAT_PAD, value)


def emit_slabs(out_s, out_ref):
    shards, rows, slab, _ = out_ref.shape

    def one(s, _):
        for r in range(rows):
            out_ref[s, r] = strided(out_s, s * rows + r, slab, LAT_PAD).astype(BF16)
        return 0

    lax.fori_loop(0, shards, one, 0)


def each_mode(modes, fn):
    few = next(n for n in (3, 2, 1) if modes % n == 0)

    def some(j, _):
        for u in range(few):
            fn(j * few + u)
        return 0

    lax.fori_loop(0, modes // few, some, 0)


def spread_blocks(w_ref, dense_s):
    _, blocks, n, _ = w_ref.shape
    dense_s[...] = jnp.zeros_like(dense_s)
    for p in range(2):
        for b in range(blocks):
            at = (p * blocks + b) * n
            dense_s[b * n : (b + 1) * n, at : at + n] = w_ref[p, b]


def pick_blocks(dense_ref, out_ref):
    _, blocks, n, lanes = out_ref.shape
    for p in range(2):
        for b in range(blocks):
            at = (p * blocks + b) * n
            block = dense_ref[b * n : (b + 1) * n, at : at + n]
            out_ref[p, b] = jnp.concatenate([block, jnp.zeros((n, lanes - n), F32)], 1)


def peers(shards, fn):
    def one(i, _):
        fn(i)
        return 0

    lax.fori_loop(1, shards, one, 0)


def emit_early(out_ref, early_s):
    rows = early_s.shape[1]
    for s in range(out_ref.shape[0]):
        early_s[s] = out_ref[s, :rows]


class Early:
    def __init__(self, src, dst, sems, rows, modes, slab, dp, me):
        self.src, self.dst, self.sems = src, dst, sems
        self.rows, self.modes, self.slab = rows, modes, slab
        self.dp, self.me, self.shards = dp, me, src.shape[0]

    def move(self, i, sender, receiver, act):
        count = self.src.shape[1]

        def piece(nr, ns):
            act(send(
                self.src.at[receiver, pl.ds(0, nr), pl.ds(0, ns)], self.dst.at[sender, pl.ds(0, nr), pl.ds(0, ns)],
                self.sems[0].at[i], self.sems[1].at[i], self.dp, receiver,
            ))

        live = row_sizes(receiver, count) if count == self.rows else [(receiver * self.rows < LAT, count)]
        each_size(live, slab_sizes(sender, self.modes, self.slab), piece)

    def own(self):
        return pltpu.make_async_copy(self.src.at[self.me], self.dst.at[self.me], self.sems[0].at[0])

    def start(self):
        self.own().start()
        peers(self.shards, lambda i: self.move(i, self.me, lax.rem(self.me + i, self.shards), lambda c: c.start()))

    def finish(self):
        self.own().wait()

        def one(i):
            self.move(i, self.me, lax.rem(self.me + i, self.shards), lambda c: c.wait_send())
            self.move(i, lax.rem(self.me + self.shards - i, self.shards), self.me, lambda c: c.wait_recv())

        peers(self.shards, one)


def spectral_forward_kernel(
    hops, x_ref, flt_ref, fa_ref, ia_ref, wi_ref, wo_ref, all_ref, v_ref,
    out_ref, freq_ref, hid_ref, gp_ref, t2_ref, early_ref,
    stage_s, recv_s, early_s, wide_s, out_s, wi_s, wo_s, go_send, go_recv, go_own, early_send, early_recv,
):
    g = pl.program_id(0)
    rows, lon, _ = x_ref.shape
    shards, _, slab, width = out_ref.shape
    modes = freq_ref.shape[0]
    h = LAT_PAD
    me = lax.axis_index("lat")
    dp = lax.axis_index("dp")
    early = Early(early_s, early_ref, (early_send, early_recv), rows, modes, slab, dp, me)

    hop = rows // hops

    def go(group, h, i, sender, receiver, act):
        def piece(nr, ns):
            part = (pl.ds(h * hop, nr), pl.ds(0, ns))
            act(send(
                stage_s.at[(group, receiver) + part], recv_s.at[(group, sender) + part],
                go_send.at[group, h, i], go_recv.at[group, h, i], dp, receiver,
            ))

        each_size([(sender * rows + h * hop < LAT, hop)], slab_sizes(receiver, modes, slab), piece)

    def own(group):
        return pltpu.make_async_copy(stage_s.at[group, me], recv_s.at[group, me], go_own.at[group])

    def to(i):
        return lax.rem(me + i, shards)

    def send_group(group, h):
        peers(shards, lambda i: go(group, h, i, me, to(i), lambda c: c.start()))

    @pl.when(g == 0)
    def _():
        def row(r, _):
            c, rs = center_scale(pad_rows(x_ref[r].astype(F32), COLS))
            first = (c * rs * vector(all_ref, NORM_G) + vector(all_ref, NORM_S)).astype(BF16)
            spec = dot(flt_ref[...], first).astype(BF16)
            for group in range(GROUPS):
                part = spec[:, group * width : (group + 1) * width]
                stage_s[group, :, r] = part.reshape(shards, slab, width)
            return 0

        for h in range(hops):
            lax.fori_loop(h * hop, (h + 1) * hop, row, 0)
            if h == 0:
                greet(shards, me, dp)
            send_group(0, h)
        for group in range(GROUPS):
            own(group).start()
            if group:
                for h in range(hops):
                    send_group(group, h)

    spread_blocks(wi_ref, wi_s)
    spread_blocks(wo_ref, wo_s)
    if slab != 2 * modes:
        out_s[...] = jnp.zeros_like(out_s)
    for group in range(GROUPS):

        @pl.when(g == group)
        def _():
            own(group).wait()
            for h in range(hops):
                peers(shards, lambda i: go(group, h, i, lax.rem(me + shards - i, shards), me, lambda c: c.wait_recv()))
            widen(recv_s.at[group], wide_s)

    def mix(v, w_ref, bias):
        a = dot(v, w_ref[...])
        re = a[:h, :width] - a[h:, width:] + vector(v_ref, bias)
        im = a[h:, :width] + a[:h, width:] + vector(v_ref, bias + 1)
        return jnp.concatenate([re, im], 0)

    def one(m):
        fq = dot(fa_ref[...], load_mode(wide_s, m, slab, modes)).astype(BF16)
        freq_ref[m] = fq
        hid, gp = gelu_both(mix(fq, wi_s, INNER_B))
        hid = hid.astype(BF16)
        hid_ref[m] = hid
        gp_ref[m] = gp
        outer = mix(hid, wo_s, OUTER_B)
        t = jnp.tanh(outer * (1.0 / SHRINK))
        t2_ref[m] = t * t
        shrunk = (outer - SHRINK * t).astype(BF16)
        store_mode(out_s, m, dot(ia_ref[...], shrunk))

    each_mode(modes, one)
    emit_slabs(out_s, out_ref)

    @pl.when(g == 0)
    def _():
        emit_early(out_ref, early_s)
        early.start()

    @pl.when(g == GROUPS - 1)
    def _():
        early.finish()
        for group in range(GROUPS):
            for h in range(hops):
                peers(shards, lambda i: go(group, h, i, me, to(i), lambda c: c.wait_send()))


def group_specs(shards, rows, slab, modes, part):
    n = 2 * LAT_PAD
    slabs = pl.BlockSpec((shards, rows, slab, part), lambda g: (0, 0, 0, g))
    spec = pl.BlockSpec((modes, n, part), lambda g: (0, 0, g))
    pair = pl.BlockSpec((2, part), lambda g: (0, g))
    return slabs, spec, pair


def weight_spec(weight, lanes=None):
    _, blocks, n, _ = weight.shape
    return pl.BlockSpec((2, blocks // GROUPS, n, lanes or n), lambda g: (0, g, 0, 0))


def hops_of(rows):
    return 2 if rows % 4 == 0 else 1


def spectral_forward(x, tb, wi, wo, vectors, shards, slab, modes, collective_id):
    rows, lon, width = x.shape
    part = width // GROUPS
    n = 2 * LAT_PAD
    slabs, spec, _ = group_specs(shards, rows, slab, modes, part)
    lines = pl.BlockSpec((vectors.shape[0], part), lambda g: (0, g))
    hops = hops_of(rows)
    dma = pltpu.SemaphoreType.DMA
    early = (shards, rows // hops, slab, part)
    return pl.pallas_call(
        functools.partial(spectral_forward_kernel, hops),
        grid=(GROUPS,),
        in_specs=[full(x), full(tb["flt"]), full(tb["fa"]), full(tb["ia"]), weight_spec(wi), weight_spec(wo)]
        + [full(vectors), lines],
        out_specs=[slabs, spec, spec, spec, spec, pl.BlockSpec(memory_space=pl.ANY)],
        out_shape=[
            sds((shards, rows, slab, width), BF16),
            sds((modes, n, width), BF16),
            sds((modes, n, width), BF16),
            sds((modes, n, width), F32),
            sds((modes, n, width), F32),
            sds(early, BF16),
        ],
        scratch_shapes=[
            pltpu.VMEM((GROUPS, shards, rows, slab, part), BF16),
            pltpu.VMEM((GROUPS, shards, rows, slab, part), BF16),
            pltpu.VMEM(early, BF16),
            pltpu.VMEM((part // LANES, shards * rows * slab, LANES), F32),
            pltpu.VMEM((part // LANES, slab * LAT_PAD, LANES), F32),
            pltpu.VMEM((part, 2 * part), BF16),
            pltpu.VMEM((part, 2 * part), BF16),
            dma((GROUPS, hops, shards)), dma((GROUPS, hops, shards)), dma((GROUPS,)), dma((shards,)), dma((shards,)),
        ],
        compiler_params=params(collective_id=collective_id, has_side_effects=True),
        name="spectral_forward",
    )(x, tb["flt"], tb["fa"], tb["ia"], wi, wo, vectors, vectors)


def spectral_backward_kernel(
    groups, plans, recv_ref, iat_ref, fat_ref, wo_ref, wi_ref, freq_ref, hid_ref, gp_ref, t2_ref, dw1_ref, dw2_ref,
    out_ref, dwo_ref, dbo_ref, dwi_ref, dbi_ref, part1_ref, part2_ref, early_ref,
    wide_s, out_s, wo_s, wi_s, dwo_s, dwi_s, acc1_s, acc2_s, recv1_s, recv2_s, early_s,
    load_sem, send_sems, recv_sems, early_send, early_recv,
):
    shards = recv_ref.shape[0]
    slab, width = recv_ref.shape[2:]
    modes = freq_ref.shape[0]
    h = LAT_PAD
    g = pl.program_id(0)
    me = lax.axis_index("lat")
    dp = lax.axis_index("dp")
    early = Early(early_s, early_ref, (early_send, early_recv), early_s.shape[1], modes, slab, dp, me)
    halving = Halving(plans, (acc1_s, acc2_s), (recv1_s, recv2_s), send_sems, recv_sems, dp, me)
    loads = [
        pltpu.make_async_copy(dw1_ref, acc1_s, load_sem.at[0]),
        pltpu.make_async_copy(dw2_ref, acc2_s, load_sem.at[1]),
    ]

    @pl.when(g == 0)
    def _():
        for copy in loads:
            copy.start()
        lat_peers = [(dp, lax.rem(me + i, shards)) for i in range(1, shards)]
        signal_all(lat_peers + [peer for peer in dp_halving_peers(groups, dp, me)])
        for copy in loads:
            copy.wait()
        halving.start(0)

    whole = GROUPS * modes
    when_due = [whole * n // 8 // 3 * 3 for n in (1, 4, 6, 7)]

    widen(recv_ref, wide_s)
    spread_blocks(wo_ref, wo_s)
    spread_blocks(wi_ref, wi_s)
    if slab != 2 * modes:
        out_s[...] = jnp.zeros_like(out_s)
    for ref in (dwo_s, dbo_ref, dwi_s, dbi_ref):
        ref[...] = jnp.zeros_like(ref)

    def lowered(grad):
        return grad[:h].astype(BF16), grad[h:].astype(BF16)

    def grads(ref, first, lows, dw_ref, db_ref):
        value = ref[pl.ds(first, len(lows))].reshape(len(lows) * 2 * h, width)
        both = [jnp.concatenate(low, 0) for low in lows]
        turned = [jnp.concatenate([im, -re], 0) for re, im in lows]
        grad = jnp.concatenate([jnp.concatenate(both, 0), jnp.concatenate(turned, 0)], 1)
        dw_ref[...] += dot_tn(value, grad)
        for part in range(2):
            total = sum(jnp.sum(low[part].astype(F32), 0, keepdims=True) for low in lows)
            db_ref[part : part + 1] += total
        return both

    def pull(v, w_ref):
        a = dot_nt(v, w_ref[:, :width])
        b = dot_nt(v, w_ref[:, width:])
        return jnp.concatenate([a[:h] + b[h:], a[h:] - b[:h]], 0)

    few = next(n for n in (3, 2, 1) if modes % n == 0)

    def some(j, _):
        first = j * few
        for stage, when in enumerate(when_due):
            pl.when(g * modes + first == when)(functools.partial(halving.tick, stage))
        lows = []
        for u in range(few):
            m = first + u
            merged = dot(iat_ref[...], load_mode(wide_s, m, slab, modes))
            lows.append(lowered(merged * t2_ref[m]))
        outer_grads = grads(hid_ref, first, lows, dwo_s, dbo_ref)
        lows = [lowered(pull(og, wo_s) * gp_ref[first + u]) for u, og in enumerate(outer_grads)]
        inner_grads = grads(freq_ref, first, lows, dwi_s, dbi_ref)
        for u, ig in enumerate(inner_grads):
            store_mode(out_s, first + u, dot(fat_ref[...], pull(ig, wi_s).astype(BF16)))
        return 0

    lax.fori_loop(0, modes // few, some, 0)
    pick_blocks(dwo_s, dwo_ref)
    pick_blocks(dwi_s, dwi_ref)
    emit_slabs(out_s, out_ref)

    @pl.when(g == 0)
    def _():
        emit_early(out_ref, early_s)
        early.start()

    @pl.when(g == GROUPS - 1)
    def _():
        for stage in range(len(when_due), halving.stages):
            halving.tick(stage)
        halving.keep((part1_ref, part2_ref))
        early.finish()


def spectral_backward(recv, tb, wo, wi, freq, hid, gp, t2, dw1, dw2, groups, plans, collective_id):
    shards, rows, slab, width = recv.shape
    modes = freq.shape[0]
    part = width // GROUPS
    slabs, spec, pair = group_specs(shards, rows, slab, modes, part)
    dw = sds(wo.shape[:3] + (LANES,), F32)
    grad = weight_spec(wo, LANES)
    db = sds((2, width), F32)
    any_ = pl.BlockSpec(memory_space=pl.ANY)
    whole = lambda n, w: pl.BlockSpec((n, w), lambda g: (0, 0))
    n1, n2 = (sum(n for k, _, _, n in plans if k == which) for which in range(2))
    stages = len(plans[0][2])
    dma = pltpu.SemaphoreType.DMA
    return pl.pallas_call(
        functools.partial(spectral_backward_kernel, groups, plans),
        grid=(GROUPS,),
        in_specs=[slabs, full(tb["iat"]), full(tb["fat"]), weight_spec(wo), weight_spec(wi), spec, spec, spec, spec]
        + [any_, any_],
        out_specs=[slabs, grad, pair, grad, pair, whole(n1, dw1.shape[1]), whole(n2, dw2.shape[1]), any_],
        out_shape=[
            sds(recv.shape, BF16), dw, db, dw, db,
            sds((n1, dw1.shape[1]), BF16), sds((n2, dw2.shape[1]), BF16),
            sds((shards, rows, slab, part), BF16),
        ],
        scratch_shapes=[
            pltpu.VMEM((part // LANES, shards * rows * slab, LANES), F32),
            pltpu.VMEM((part // LANES, slab * LAT_PAD, LANES), F32),
            pltpu.VMEM((part, 2 * part), BF16),
            pltpu.VMEM((part, 2 * part), BF16),
            pltpu.VMEM((part, 2 * part), F32),
            pltpu.VMEM((part, 2 * part), F32),
            pltpu.VMEM(dw1.shape, BF16),
            pltpu.VMEM(dw2.shape, BF16),
            pltpu.VMEM((sum(received(p) for k, _, p, _ in plans if k == 0), dw1.shape[1]), BF16),
            pltpu.VMEM((sum(received(p) for k, _, p, _ in plans if k == 1), dw2.shape[1]), BF16),
            pltpu.VMEM((shards, rows, slab, part), BF16),
            dma((2,)), dma((len(plans), stages)), dma((len(plans), stages)), dma((shards,)), dma((shards,)),
        ],
        compiler_params=params(collective_id=collective_id, has_side_effects=True),
        name="spectral_backward",
    )(recv, tb["iat"], tb["fat"], wo, wi, freq, hid, gp, t2, dw1, dw2)


def gather_row(r_ref, row, modes):
    shards, _, slab, width = r_ref.shape
    whole = KEPT // modes
    parts = [r_ref[:whole, row].astype(F32).reshape(whole * slab, width)]
    rest = (shards - whole) * slab
    if KEPT % modes:
        n = up8(2 * (KEPT % modes))
        parts.append(r_ref[whole, row].astype(F32)[:n])
        rest -= n
    if rest:
        parts.append(jnp.zeros((rest, width), F32))
    return jnp.concatenate(parts, 0).astype(BF16)


def feed_kernel(
    per, chunk, hops, modes, scale_ref, x_ref, c_ref, back_ref, early_ref, il_ref, ilt_ref, w1_ref, w2_ref, v_ref,
    lo_ref, mg_ref, out_ref, dw1_ref, dw2_ref, deb_ref, drb_ref, dpg_ref, dps_ref,
    slab_s, w1_s, w2_s, act_s, pre_s, sec_s, sect_s, up_s, mixed_s, xhat_s, rs_s, branch_s, grad_s,
    w_sem, dw_sem, early_sem, in_send, in_recv, in_own, out_send, out_recv, out_own,
):
    g = pl.program_id(0)
    steps = pl.num_programs(0)
    lon, width = x_ref.shape[1:]
    hidden = w1_s.shape[1]
    shards, rows, slab, _ = slab_s.shape
    hop = rows // hops
    every = steps // hops
    tall = per * COLS
    me = lax.axis_index("lat")
    dp = lax.axis_index("dp")

    def transfer(src, dst, sems, h, lanes, i, sender, receiver, row_owner, mode_owner, act):
        part = pl.ds(h * hop, hop)

        def piece(nr, ns):
            act(send(
                src.at[receiver, part, pl.ds(0, ns), lanes], dst.at[sender, part, pl.ds(0, ns), lanes],
                sems[0].at[h, i], sems[1].at[h, i], dp, receiver,
            ))

        live = row_owner * rows + h * hop < LAT
        each_size([(live, hop)], slab_sizes(mode_owner, modes, slab), piece)

    known = early_ref.shape[3]

    def fresh(h):
        return pl.ds(known, width - known) if h == 0 else pl.ds(0, width)

    def incoming(h, i, sender, receiver, act):
        transfer(
            back_ref, slab_s, (in_send, in_recv), h, fresh(h), i, sender, receiver, receiver, sender, act
        )

    def outgoing(h, i, sender, receiver, act):
        transfer(
            slab_s, out_ref, (out_send, out_recv), h, pl.ds(0, width), i, sender, receiver, sender, receiver, act
        )

    def own_in(h):
        part = pl.ds(h * hop, hop)
        return pltpu.make_async_copy(
            back_ref.at[me, part, :, fresh(h)], slab_s.at[me, part, :, fresh(h)], in_own.at[h]
        )

    early = pltpu.make_async_copy(early_ref, slab_s.at[:, pl.ds(0, hop), :, pl.ds(0, known)], early_sem)

    def own_out(h):
        part = pl.ds(h * hop, hop)
        return pltpu.make_async_copy(slab_s.at[me, part], out_ref.at[me, part], out_own.at[h])

    def to(i):
        return lax.rem(me + i, shards)

    def source(i):
        return lax.rem(me + shards - i, shards)

    def fetch(h):
        own_in(h).start()
        peers(shards, lambda i: incoming(h, i, me, to(i), lambda c: c.start()))

    weights = [
        pltpu.make_async_copy(w1_ref, w1_s, w_sem.at[0]),
        pltpu.make_async_copy(w2_ref, w2_s, w_sem.at[1]),
    ]

    @pl.when(g == 0)
    def _():
        for copy in weights:
            copy.start()
        early.start()
        greet(shards, me, dp)
        fetch(0)
        for ref in (deb_ref, drb_ref, dpg_ref, dps_ref):
            ref[...] = jnp.zeros_like(ref)

    for h in range(hops):

        @pl.when(g == h * every)
        def _():
            if h == 0:
                early.wait()
            own_in(h).wait()
            peers(shards, lambda i: incoming(h, i, source(i), me, lambda c: c.wait_recv()))
            if h + 1 < hops:
                fetch(h + 1)

    at = pl.ds(0 if rows == per else pl.multiple_of(g * tall, tall), tall)
    for i in range(per):
        rows_i = pl.ds(i * COLS, COLS)
        x = pad_rows(x_ref[i].astype(F32), COLS)
        c, rs = center_scale(x)
        first = c * rs * vector(v_ref, NORM_G) + vector(v_ref, NORM_S)
        filtered = dot(il_ref[...], gather_row(slab_s, g * per + i, modes))
        live = me * rows + g * per + i < LAT
        mixed = jnp.where(live, filtered, jnp.zeros_like(filtered)) + first + x
        c, rs = center_scale(mixed)
        xhat = c * rs
        mixed_s[rows_i, :] = mixed
        xhat_s[rows_i, :] = xhat
        rs_s[rows_i, :] = jnp.broadcast_to(rs, (COLS, LANES))
        sec_s[rows_i, :] = (xhat * vector(v_ref, POST_G) + vector(v_ref, POST_S)).astype(BF16)
        up = (pad_rows(c_ref[i].astype(F32), COLS) * scale_ref[0, g * per + i]).astype(BF16)
        up_s[pl.ds(pl.multiple_of(g * tall + i * COLS, COLS), COLS), :] = up
        drb_ref[...] += jnp.sum(up.astype(F32), 0, keepdims=True)
    sect_s[:, at] = sec_s[...].T
    branch_s[...] = jnp.broadcast_to(vector(v_ref, REDUCE_B), branch_s.shape)
    grad_s[...] = jnp.zeros_like(grad_s)

    @pl.when(g == 0)
    def _():
        for copy in weights:
            copy.wait()

    def hidden_chunk(j, _):
        ds = pl.ds(pl.multiple_of(j * chunk, chunk), chunk)
        act, slope = gelu_both(dot(sec_s[...], w1_s[:, ds]) + v_ref[pl.ds(EXPAND_B + j, 1), :])
        act = act.astype(BF16)
        act_s[at, ds] = act
        pre = (dot_nt(up_s[at, :], w2_s[ds, :]) * slope).astype(BF16)
        pre_s[at, ds] = pre
        deb_ref[pl.ds(j, 1), :] += jnp.sum(pre.astype(F32), 0, keepdims=True)
        branch_s[...] += dot(act, w2_s[ds, :])
        grad_s[...] += dot_nt(pre, w1_s[:, ds])
        return 0

    lax.fori_loop(0, hidden // chunk, hidden_chunk, 0)
    for i in range(per):
        rows_i = pl.ds(i * COLS, COLS)
        grad = grad_s[rows_i, :]
        xhat = xhat_s[rows_i, :]
        up = pad_rows(c_ref[i].astype(F32), COLS) * scale_ref[0, g * per + i]
        mg = up + norm_back(grad, xhat, rs_s[rows_i, 0:1], vector(v_ref, POST_G))
        mg_ref[i] = mg[:lon]
        rg = dot(ilt_ref[...], mg.astype(BF16)).astype(BF16)
        slab_s[:, g * per + i] = rg.reshape(shards, slab, width)

    @pl.when(lax.rem(g, every) == every - 1)
    def _():
        h = g // every
        own_out(h).start()
        peers(shards, lambda i: outgoing(h, i, me, to(i), lambda c: c.start()))

    for i in range(per):
        rows_i = pl.ds(i * COLS, COLS)
        keep = scale_ref[1, g * per + i]
        lo_ref[i] = ((mixed_s[rows_i, :] + branch_s[rows_i, :]) * keep).astype(BF16)[:lon]
        grad = grad_s[rows_i, :]
        dpg_ref[...] += jnp.sum(grad * xhat_s[rows_i, :], 0, keepdims=True)
        dps_ref[...] += jnp.sum(grad, 0, keepdims=True)

    def gradients(j):
        ds = pl.ds(pl.multiple_of(j * chunk, chunk), chunk)
        side = dw1_ref.shape[1] // chunk
        place = (
            pl.ds(pl.multiple_of(j // side * width, width), width),
            pl.ds(pl.multiple_of(lax.rem(j, side) * chunk, chunk), chunk),
        )
        return (
            pltpu.make_async_copy(w1_s.at[:, ds], dw1_ref.at[place], dw_sem.at[0, j]),
            pltpu.make_async_copy(w2_s.at[ds, :], dw2_ref.at[ds, :], dw_sem.at[1, j]),
        )

    @pl.when(g == steps - 1)
    def _():
        def weight_chunk(j, _):
            ds = pl.ds(pl.multiple_of(j * chunk, chunk), chunk)
            w1_s[:, ds] = dot(sect_s[...], pre_s[:, ds]).astype(BF16)
            w2_s[ds, :] = dot_tn(act_s[:, ds], up_s[...]).astype(BF16)
            for copy in gradients(j):
                copy.start()
            return 0

        lax.fori_loop(0, hidden // chunk, weight_chunk, 0)

        for h in range(hops):
            own_out(h).wait()

            def wait_all(i):
                incoming(h, i, me, to(i), lambda c: c.wait_send())
                outgoing(h, i, me, to(i), lambda c: c.wait_send())
                outgoing(h, i, source(i), me, lambda c: c.wait_recv())

            peers(shards, wait_all)

        def finish(j, _):
            for copy in gradients(j):
                copy.wait()
            return 0

        lax.fori_loop(0, hidden // chunk, finish, 0)


def feed(scale, x, cot, back, early, tb, w1, w2, vectors, modes, collective_id):
    rows, lon, width = x.shape
    hidden = w1.shape[1]
    shards, _, slab, _ = back.shape
    per = next(n for n in (2, 3, 1) if rows % n == 0)
    steps = rows // per
    hops = hops_of(rows)
    chunk = width
    row = pl.BlockSpec((per, lon, width), lambda g: (g, 0, 0))
    any_ = pl.BlockSpec(memory_space=pl.ANY)
    vec = lambda n: pl.BlockSpec((n, width), lambda g: (0, 0))
    tall = per * COLS
    total = rows * COLS
    dma = pltpu.SemaphoreType.DMA
    return pl.pallas_call(
        functools.partial(feed_kernel, per, chunk, hops, modes),
        grid=(steps,),
        in_specs=[
            pl.BlockSpec(memory_space=pltpu.SMEM), row, row, any_, any_, full(tb["il"]), full(tb["ilt"]), any_, any_,
            full(vectors),
        ],
        out_specs=[row, row, any_, any_, any_, vec(hidden // width), vec(1), vec(1), vec(1)],
        out_shape=[
            sds((rows, lon, width), BF16),
            sds((rows, lon, width), F32),
            sds(back.shape, BF16),
            sds((2 * width, hidden // 2), BF16),
            sds(w2.shape, BF16),
            sds((hidden // width, width), F32),
            sds((1, width), F32),
            sds((1, width), F32),
            sds((1, width), F32),
        ],
        scratch_shapes=[
            pltpu.VMEM(back.shape, BF16),
            pltpu.VMEM(w1.shape, BF16),
            pltpu.VMEM(w2.shape, BF16),
            pltpu.VMEM((total, hidden), BF16),
            pltpu.VMEM((total, hidden), BF16),
            pltpu.VMEM((tall, width), BF16),
            pltpu.VMEM((width, total), BF16),
            pltpu.VMEM((total, width), BF16),
            pltpu.VMEM((tall, width), F32),
            pltpu.VMEM((tall, width), F32),
            pltpu.VMEM((tall, LANES), F32),
            pltpu.VMEM((tall, width), F32),
            pltpu.VMEM((tall, width), F32),
            dma((2,)), dma((2, hidden // chunk)), dma,
            dma((hops, shards)), dma((hops, shards)), dma((hops,)),
            dma((hops, shards)), dma((hops, shards)), dma((hops,)),
        ],
        compiler_params=pltpu.CompilerParams(
            vmem_limit_bytes=63 * 2**20, collective_id=collective_id, has_side_effects=True
        ),
        name="feed",
    )(scale, x, cot, back, early, tb["il"], tb["ilt"], w1, w2, vectors)


def leave_kernel(
    groups, hops, modes, plans, x_ref, back_ref, early_ref, mg_ref, fl_ref, v_ref, *refs,
):
    weight_refs, line_refs, refs = refs[:2], refs[2:8], refs[8:]
    (
        part1_ref, part2_ref, out_ref, sums_ref, norm_ref, dw1_ref, dw2_ref,
        slab_s, line_s, mine_s, from_dp, part_s, from_lat, all_s, norm_lat, norm_dp,
        in_send, in_recv, in_own, early_sem, wide_send, wide_recv, own_sem, small_sems,
    ) = refs
    g = pl.program_id(0)
    steps = pl.num_programs(0)
    lon = x_ref.shape[1]
    shards, rows, slab, _ = slab_s.shape
    n = from_lat.shape[1]
    hop = rows // hops
    me = lax.axis_index("lat")
    dp = lax.axis_index("dp")
    lat_peers = [lax.rem(me + i, shards) for i in range(1, shards)]
    dp_peers = [lax.rem(dp + i, groups) for i in range(1, groups)]

    known = early_ref.shape[3]
    fresh = pl.ds(known, slab_s.shape[3] - known)
    early = pltpu.make_async_copy(early_ref, slab_s.at[:, :, :, pl.ds(0, known)], early_sem)

    def incoming(h, i, sender, receiver, act):
        part = pl.ds(h * hop, hop)

        def piece(nr, ns):
            act(send(
                back_ref.at[receiver, part, pl.ds(0, ns), fresh], slab_s.at[sender, part, pl.ds(0, ns), fresh],
                in_send.at[h, i], in_recv.at[h, i], dp, receiver,
            ))

        live = receiver * rows + h * hop < LAT
        each_size([(live, hop)], slab_sizes(sender, modes, slab), piece)

    def own_in(h):
        part = pl.ds(h * hop, hop)
        return pltpu.make_async_copy(back_ref.at[me, part, :, fresh], slab_s.at[me, part, :, fresh], in_own.at[h])

    def fetch(h):
        own_in(h).start()
        peers(shards, lambda i: incoming(h, i, me, lax.rem(me + i, shards), lambda c: c.start()))

    def arrived(h):
        own_in(h).wait()
        peers(shards, lambda i: incoming(h, i, lax.rem(me + shards - i, shards), me, lambda c: c.wait_recv()))

    walks = [halving_walk(first, plan, dp, me) for _, first, plan, _ in plans]
    outs = (dw1_ref, dw2_ref)
    parts = (part1_ref, part2_ref)
    stages = len(plans[0][2])
    count = len(plans)

    def part(j):
        k, _, _, n = plans[j]
        at = sum(rest for which, _, _, rest in plans[:j] if which == k)
        return parts[k].at[pl.ds(at, n)]

    def own_part(j):
        k, _, _, n = plans[j]
        return pltpu.make_async_copy(part(j), outs[k].at[low_rows_at(walks[j][0][-1], n)], own_sem.at[j])

    def spread(j, stage):
        k, _, plan, _ = plans[j]
        _, _, n, halved = plan[stage]
        if not halved:
            return None
        where = low_rows_at(walks[j][0][stage + 1], n // 2)
        first = not any(later[3] for later in plan[stage + 1 :])
        return pltpu.make_async_remote_copy(
            src_ref=part(j) if first else outs[k].at[where], dst_ref=outs[k].at[where],
            send_sem=wide_send.at[j, stage], recv_sem=wide_recv.at[j, stage],
            device_id=walks[j][2][stage], device_id_type=MESH,
        )

    def spread_all(stage, act):
        for j in range(count):
            copy = spread(j, stage)
            if copy is not None:
                act(copy)

    def tick(i):
        stage = stages - 1 - i
        spread_all(stage, lambda c: c.wait())
        if i == 0:
            for j in range(count):
                own_part(j).wait()
        if stage:
            spread_all(stage - 1, lambda c: c.start())


    def remote(src, dst, stage, i, to):
        return pltpu.make_async_remote_copy(
            src_ref=src, dst_ref=dst, send_sem=small_sems.at[stage, 0, i], recv_sem=small_sems.at[stage, 1, i],
            device_id=to, device_id_type=MESH,
        )

    def over(peers_, axis):
        return [(i, p, (p, me) if axis == "dp" else (dp, p)) for i, p in enumerate(peers_)]

    block = shards * n
    mine = low_rows_at((dp * shards + me) * n, n)
    mine_dp = low_rows_at(dp * block, block)
    tiles = line_s.shape[1] // LANES

    def small(stage):
        if stage == 0:
            return [
                remote(mine_s.at[low_rows_at(p * block, block)], from_dp.at[i], 0, i, to)
                for i, p, to in over(dp_peers, "dp")
            ]
        if stage == 1:
            return [
                remote(part_s.at[low_rows_at(p * n, n)], from_lat.at[i], 1, i, to)
                for i, p, to in over(lat_peers, "lat")
            ]
        if stage == 2:
            return [remote(all_s.at[mine], all_s.at[mine], 2, i, to) for i, p, to in over(lat_peers, "lat")]
        if stage == 3:
            return [remote(all_s.at[mine_dp], all_s.at[mine_dp], 3, i, to) for i, p, to in over(dp_peers, "dp")]
        if stage == 4:
            return [remote(norm_lat.at[me], norm_lat.at[me], 4, i, to) for i, p, to in over(lat_peers, "lat")]
        return [remote(norm_dp.at[dp], norm_dp.at[dp], 5, i, to) for i, p, to in over(dp_peers, "dp")]

    def begin(stage):
        for copy in small(stage):
            copy.start()

    def end(stage):
        for copy in small(stage):
            copy.wait()
        if stage == 0:
            whole = mine_s[mine_dp, :].astype(F32) + jnp.sum(from_dp[...].astype(F32), 0)
            part_s[...] = whole.astype(BF16)
        if stage == 1:
            whole = part_s[low_rows_at(me * n, n), :].astype(F32) + jnp.sum(from_lat[...].astype(F32), 0)
            all_s[mine, :] = whole.astype(BF16)

    def small_tick(stage):
        end(stage)
        begin(stage + 1)

    @pl.when(g == 0)
    def _():
        at = 0
        for ref in weight_refs:
            value = ref[...].reshape(-1, LANES)
            mine_s[at : at + value.shape[0], :] = value.astype(BF16)
            at += value.shape[0]
        lines = [
            ref[row : row + 1, t * LANES : (t + 1) * LANES]
            for ref in line_refs
            for row in range(ref.shape[0])
            for t in range(tiles)
        ]
        lines.append(jnp.zeros((mine_s.shape[0] - at - len(lines), LANES), F32))
        mine_s[at:, :] = jnp.concatenate(lines, 0).astype(BF16)
        signal_all([(dp, p) for p in lat_peers] + [(p, me) for p in dp_peers])
        early.start()
        for j in range(count):
            own_part(j).start()
        spread_all(stages - 1, lambda c: c.start())
        begin(0)
        fetch(0)
        line_s[...] = jnp.zeros_like(line_s)
        tick(0)
        small_tick(0)
        early.wait()
        arrived(0)
        tick(1)
        small_tick(1)
        if hops > 1:
            fetch(1)

    for h in range(1, hops):
        pl.when(g == h * hop)(functools.partial(arrived, h))

    x = pad_rows(x_ref[0].astype(F32), COLS)
    c, rs = center_scale(x)
    xhat = c * rs
    mg = pad_rows(mg_ref[0], COLS)
    live = me * rows + g < LAT
    spectrum = dot(fl_ref[...], gather_row(slab_s, g, modes))
    grad = jnp.where(live, spectrum, jnp.zeros_like(spectrum)) + mg
    line_s[0:1] += jnp.sum(grad * xhat, 0, keepdims=True)
    line_s[1:2] += jnp.sum(grad, 0, keepdims=True)
    out_ref[0] = (mg + norm_back(grad, xhat, rs, vector(v_ref, NORM_G)))[:lon]

    @pl.when(g == hop - 1)
    def _():
        tick(2)
        small_tick(2)

    @pl.when(g == steps - 1)
    def _():
        norm_lat[me] = line_s[...]
        begin(4)
        for i in range(3, stages):
            tick(i)
        end(4)
        norm_dp[dp] = jnp.sum(norm_lat[...], 0)
        begin(5)
        end(3)
        sums_ref[...] = all_s[...].astype(F32)
        for h in range(hops):
            peers(shards, lambda i: incoming(h, i, me, lax.rem(me + i, shards), lambda c: c.wait_send()))
        end(5)
        norm_ref[...] = jnp.sum(norm_dp[...], 0)


def leave(x, back, early, mg, fl, vectors, small, part1, part2, shapes, groups, plans, modes, collective_id):
    rows, lon, width = x.shape
    shards, _, slab, _ = back.shape
    hops = hops_of(rows)
    stages = len(plans[0][2])
    unit = LOW_ROWS * groups * shards
    total = -(-sum(v.size // LANES for v in small) // unit) * unit
    n = total // (groups * shards)
    row = pl.BlockSpec((1, lon, width), lambda r: (r, 0, 0))
    any_ = pl.BlockSpec(memory_space=pl.ANY)
    whole = lambda *shape: pl.BlockSpec(shape, lambda r: (0,) * len(shape))
    dma = pltpu.SemaphoreType.DMA
    return pl.pallas_call(
        functools.partial(leave_kernel, groups, hops, modes, plans),
        grid=(rows,),
        in_specs=[row, any_, any_, row, full(fl), full(vectors)] + [full(v) for v in small] + [any_, any_],
        out_specs=[row, whole(total, LANES), whole(2, width), any_, any_],
        out_shape=[sds((rows, lon, width), F32), sds((total, LANES), F32), sds((2, width), F32)]
        + [sds(shape, BF16) for shape in shapes],
        scratch_shapes=[
            pltpu.VMEM(back.shape, BF16),
            pltpu.VMEM((2, width), F32),
            pltpu.VMEM((total, LANES), BF16),
            pltpu.VMEM((groups - 1, shards * n, LANES), BF16),
            pltpu.VMEM((shards * n, LANES), BF16),
            pltpu.VMEM((shards - 1, n, LANES), BF16),
            pltpu.VMEM((total, LANES), BF16),
            pltpu.VMEM((shards, 2, width), F32),
            pltpu.VMEM((groups, 2, width), F32),
            dma((hops, shards)), dma((hops, shards)), dma((hops,)), dma,
            dma((len(plans), stages)), dma((len(plans), stages)), dma((len(plans),)),
            dma((6, 2, max(groups, shards) - 1)),
        ],
        compiler_params=params(collective_id=collective_id, has_side_effects=True),
        name="leave",
    )(x, back, early, mg, fl, vectors, *small, part1, part2)


def shards_fn(
    groups, shards, inputs, cotangent, storm_weight, norm_gain, norm_shift, inner_weight, inner_bias,
    outer_weight, outer_bias, post_gain, post_shift, expand_weight, expand_bias, reduce_weight, reduce_bias,
):
    _, rows, lon, width = inputs.shape
    modes = LON_PAD // shards
    slab = slab_rows(modes)
    tb = make_tables(shards, modes)
    row_ids = lax.axis_index("lat") * rows + jnp.arange(rows, dtype=jnp.int32)
    keep = (row_ids < LAT).astype(F32)
    scale = jnp.stack([keep * (storm_weight[0].astype(F32) / 64.0), keep])
    x = inputs[0]
    cot = cotangent[0]
    vectors = jnp.concatenate([
        norm_gain, norm_shift, post_gain, post_shift, reduce_bias,
        inner_bias.reshape(-1), outer_bias.reshape(-1), expand_bias,
    ]).reshape(-1, width)

    back, freq, hid, gp, t2, early = spectral_forward(
        x, tb, inner_weight, outer_weight, vectors, shards, slab, modes, 0
    )
    (layer_out, mixed_grad, mode_grad, dw1, dw2, deb, drb, dpg, dps) = feed(
        scale, x, cot, back, early, tb, expand_weight, reduce_weight, vectors, modes, 1
    )
    plans = halving_plans(groups, shards, (dw1.shape[0], dw2.shape[0]))
    slab_grad, dwo, dbo, dwi, dbi, part1, part2, early = spectral_backward(
        mode_grad, tb, outer_weight, inner_weight, freq, hid, gp, t2, dw1, dw2, groups, plans, 2
    )
    small = (dwi, dwo, dbi, dbo, dpg, dps, deb, drb)
    input_grad, sums, norm, dw1, dw2 = leave(
        x, slab_grad, early, mixed_grad, tb["fl"], vectors, small, part1, part2,
        (dw1.shape, dw2.shape), groups, plans, modes, 3
    )
    dw1 = jnp.concatenate([dw1[:width], dw1[width:]], 1).astype(F32)
    dw2 = dw2.astype(F32)
    ends = np.cumsum([v.size // LANES for v in small])
    dwi, dwo, dbi, dbo, dpg, dps, deb, drb = [
        sums[e - v.size // LANES : e] for v, e in zip(small, ends)
    ]
    block = inner_weight.shape[-1]
    weight = lambda v: v.reshape(inner_weight.shape[:3] + (LANES,))[..., :block]
    line = lambda v: v.reshape(-1)
    return (
        layer_out[None], input_grad[None], norm[0], norm[1],
        weight(dwi), dbi.reshape(inner_bias.shape), weight(dwo), dbo.reshape(outer_bias.shape),
        line(dpg), line(dps), dw1, line(deb), dw2, line(drb),
    )


def solution(mesh):
    split = P("dp", "lat", None, None)
    return jax.shard_map(
        functools.partial(shards_fn, mesh.shape["dp"], mesh.shape["lat"]),
        mesh=mesh,
        in_specs=(split, split, P("dp")) + (P(),) * 12,
        out_specs=(split, split) + (P(),) * 12,
        check_vma=False,
    )
```

```python
import functools
import math

import jax
import jax.numpy as jnp
import ml_dtypes
import numpy as np
from jax import lax
from jax.experimental import pallas as pl
from jax.experimental.pallas import tpu as pltpu
from jax.sharding import PartitionSpec as P

BLOCKS = 8
LAT = 90
LON = 180
LAT_PAD = 96
LON_PAD = 96
KEPT = LON // 2 + 1
COLS = 192
GROUPS = 2
LANES = 128
LOW_ROWS = 16
NORM_G, NORM_S, POST_G, POST_S, REDUCE_B, INNER_B, OUTER_B, EXPAND_B = 0, 1, 2, 3, 4, 5, 7, 9

SHRINK = 0.01
EPS = 1e-6
SQRT_HALF = 0.7071067811865476
PDF_SCALE = 0.3989422804014327

F32 = jnp.float32
BF16 = jnp.bfloat16
MESH = pl.DeviceIdType.MESH
VMEM_LIMIT = 62 * 2**20


def base_tables():
    f = np.float32
    modes = np.arange(LON_PAD)
    columns = np.arange(LON)
    phases = (columns[:, None] * modes[None, :] % LON).astype(f) * f(2.0 * math.pi / LON)
    kept = (modes < LON // 2 + 1).astype(f)
    factor = np.where((modes == 0) | (modes == LON // 2), f(1), f(2)) * kept
    scale = f(1.0 / math.sqrt(LON))
    forward_lon = np.stack([np.cos(phases) * kept, -np.sin(phases) * kept], axis=1) * scale
    inverse_lon = np.stack([np.cos(phases) * factor, -np.sin(phases) * factor], axis=1) * scale
    rows = np.arange(LAT_PAD)
    angles = (rows[:, None] * rows[None, :] % LAT).astype(f) * f(2.0 * math.pi / LAT)
    inside = ((rows[:, None] < LAT) & (rows[None, :] < LAT)).astype(f) / f(math.sqrt(LAT))
    cs = np.cos(angles) * inside
    sn = np.sin(angles) * inside
    forward_lat = np.stack([np.stack([cs, sn], 1), np.stack([-sn, cs], 1)], 0)
    inverse_lat = np.stack([np.stack([cs, -sn], 1), np.stack([sn, cs], 1)], 0)
    return forward_lon, inverse_lon, forward_lat, inverse_lat


def slab_rows(modes):
    return -(-2 * modes // 8) * 8


def lon_table(table, shards, modes):
    slab = slab_rows(modes)
    out = np.zeros((COLS, shards, slab), np.float32)
    split = table.reshape(LON, 2, shards, modes).transpose(0, 2, 3, 1)
    out[:LON, :, : 2 * modes] = split.reshape(LON, shards, 2 * modes)
    return out.reshape(COLS, shards * slab)


def make_tables(shards, modes):
    forward_lon, inverse_lon, forward_lat, inverse_lat = base_tables()
    low = lambda t: jnp.asarray(np.ascontiguousarray(t).astype(ml_dtypes.bfloat16))
    n = 2 * LAT_PAD
    fl = lon_table(forward_lon, shards, modes)
    il = lon_table(inverse_lon, shards, modes)
    fa = forward_lat.reshape(n, n)
    ia = inverse_lat.reshape(n, n)
    return dict(
        fl=low(fl), flt=low(fl.T), il=low(il), ilt=low(il.T),
        fa=low(fa), fat=low(fa.T), ia=low(ia), iat=low(ia.T),
    )


def dot(a, b):
    return jnp.dot(a, b, preferred_element_type=F32)


def dot_nt(a, b):
    return lax.dot_general(a, b, (((1,), (1,)), ((), ())), preferred_element_type=F32)


def dot_tn(a, b):
    return lax.dot_general(a, b, (((0,), (0,)), ((), ())), preferred_element_type=F32)


def gelu_both(v):
    cdf = 0.5 * (1.0 + lax.erf(v * SQRT_HALF))
    pdf = jnp.exp(-0.5 * v * v) * PDF_SCALE
    return v * cdf, cdf + v * pdf


def center_scale(v):
    inv = 1.0 / v.shape[-1]
    c = v - jnp.sum(v, -1, keepdims=True) * inv
    return c, lax.rsqrt(jnp.sum(c * c, -1, keepdims=True) * inv + EPS)


def pad_rows(v, n):
    return jnp.concatenate([v, jnp.zeros((n - v.shape[0], v.shape[1]), v.dtype)], 0)


def norm_back(grad, xhat, rs, gain):
    inv = 1.0 / grad.shape[-1]
    dx = grad * gain
    m1 = jnp.sum(dx, -1, keepdims=True) * inv
    m2 = jnp.sum(dx * xhat, -1, keepdims=True) * inv
    return rs * (dx - m1 - xhat * m2)


def full(a):
    return pl.BlockSpec(a.shape, lambda *_: (0,) * a.ndim, pipeline_mode=pl.Buffered(1))


def sds(shape, dtype):
    return jax.ShapeDtypeStruct(shape, dtype)


def params(**kw):
    return pltpu.CompilerParams(vmem_limit_bytes=VMEM_LIMIT, **kw)


def vector(v_ref, row):
    return v_ref[row : row + 1, :]


VECTOR_ROWS = 16


def put_vectors(v_s, flat, blocked):
    width = v_s.shape[1]
    for row, ref in flat:
        for i in range(ref.shape[0] // width):
            v_s[row + i : row + i + 1, :] = ref[i * width : (i + 1) * width].reshape(1, width)
    for row, ref in blocked:
        _, blocks, n = ref.shape
        for p in range(2):
            for b in range(blocks):
                v_s[row + p : row + p + 1, b * n : (b + 1) * n] = ref[p, b : b + 1, :]


def up8(n):
    return -(-n // 8) * 8


def slab_sizes(index, modes, slab):
    sizes = [(index < KEPT // modes, slab)]
    if KEPT % modes:
        sizes.append((index == KEPT // modes, up8(2 * (KEPT % modes))))
    return sizes


def row_sizes(index, rows):
    sizes = [(index < LAT // rows, rows)]
    if LAT % rows:
        sizes.append((index == LAT // rows, LAT % rows))
    return sizes


def each_size(row_options, slab_options, fn):
    for row_ok, nr in row_options:
        for slab_ok, ns in slab_options:
            pl.when(row_ok & slab_ok)(functools.partial(fn, nr, ns))


def greet(shards, me, dp):
    barrier = pltpu.get_barrier_semaphore()

    def one(i, _):
        peer = lax.rem(me + i, shards)
        pl.semaphore_signal(barrier, inc=1, device_id=(dp, peer), device_id_type=MESH)
        return 0

    lax.fori_loop(1, shards, one, 0)
    pl.semaphore_wait(barrier, shards - 1)


def send(src, dst, send_sem, recv_sem, dp, peer):
    return pltpu.make_async_remote_copy(
        src_ref=src, dst_ref=dst, send_sem=send_sem, recv_sem=recv_sem,
        device_id=(dp, peer), device_id_type=MESH,
    )


def halving_plan(groups, shards, n, turn):
    dp_bits = [("dp", b) for b in range(groups.bit_length() - 1)]
    lat_bits = [("lat", b) for b in range(shards.bit_length() - 1)]
    middle = dp_bits[1:2] + lat_bits[:2]
    turn = turn % len(middle)
    order = dp_bits[:1] + middle[turn:] + middle[:turn] + dp_bits[2:] + lat_bits[2:]
    plan = []
    for axis, bit in order:
        halved = n % (2 * LOW_ROWS) == 0
        plan.append((axis, bit, n, halved))
        n = n // 2 if halved else n
    return plan, n


def halving_plans(groups, shards, sizes):
    return [
        (k, t * size // 3) + halving_plan(groups, shards, size // 3, t)
        for k, size in enumerate(sizes)
        for t in range(3)
    ]


def halving_walk(first, plan, dp, me):
    offsets, bits, peers = [first], [], []
    for axis, bit, n, halved in plan:
        index = dp if axis == "dp" else me
        b = lax.rem(index // 2**bit, 2)
        other = index + 2**bit * (1 - 2 * b)
        peers.append((other, me) if axis == "dp" else (dp, other))
        bits.append(b)
        offsets.append(offsets[-1] + b * (n // 2) if halved else offsets[-1])
    return offsets, bits, peers


def dp_halving_peers(groups, dp, me):
    bits = range(groups.bit_length() - 1)
    return [(dp + 2**bit * (1 - 2 * lax.rem(dp // 2**bit, 2)), me) for bit in bits]


def rows_at(start, n, unit=8):
    return pl.ds(pl.multiple_of(start, unit), n)


def low_rows_at(start, n):
    return rows_at(start, n, LOW_ROWS)


def signal_all(devices):
    barrier = pltpu.get_barrier_semaphore()
    for device in devices:
        pl.semaphore_signal(barrier, inc=1, device_id=device, device_id_type=MESH)
    pl.semaphore_wait(barrier, len(devices))


def received(plan):
    return sum(n // 2 if halved else n for _, _, n, halved in plan)


class Halving:
    def __init__(self, plans, accs, recvs, send_sems, recv_sems, dp, me):
        self.plans, self.accs, self.recvs = plans, accs, recvs
        self.send_sems, self.recv_sems = send_sems, recv_sems
        self.walks = [halving_walk(first, plan, dp, me) for _, first, plan, _ in plans]
        self.stages = len(plans[0][2])

    def base(self, j, stage):
        k, _, plan, _ = self.plans[j]
        before = sum(received(p) for which, _, p, _ in self.plans[:j] if which == k)
        return before + received(plan[:stage])

    def copy(self, j, stage):
        k = self.plans[j][0]
        _, _, n, halved = self.plans[j][2][stage]
        offsets, bits, peers = self.walks[j]
        count = n // 2 if halved else n
        start = offsets[stage] + (1 - bits[stage]) * count if halved else offsets[stage]
        return pltpu.make_async_remote_copy(
            src_ref=self.accs[k].at[low_rows_at(start, count)],
            dst_ref=self.recvs[k].at[pl.ds(self.base(j, stage), count)],
            send_sem=self.send_sems.at[j, stage], recv_sem=self.recv_sems.at[j, stage],
            device_id=peers[stage], device_id_type=MESH,
        )

    def start(self, stage):
        for j in range(len(self.plans)):
            self.copy(j, stage).start()

    def finish(self, stage):
        for j in range(len(self.plans)):
            self.copy(j, stage).wait()
            k = self.plans[j][0]
            _, _, n, halved = self.plans[j][2][stage]
            count = n // 2 if halved else n
            first = self.walks[j][0][stage + 1]
            base = self.base(j, stage)
            acc, recv = self.accs[k], self.recvs[k]
            most = 98304 // acc.shape[1]
            step = max(c for c in range(LOW_ROWS, most + 1, LOW_ROWS) if count % c == 0)

            def add(i, _):
                mine = low_rows_at(first + i * step, step)
                other = low_rows_at(base + i * step, step)
                acc[mine, :] = (acc[mine, :].astype(F32) + recv[other, :].astype(F32)).astype(BF16)
                return 0

            lax.fori_loop(0, count // step, add, 0)

    def tick(self, stage):
        self.finish(stage)
        if stage + 1 < self.stages:
            self.start(stage + 1)

    def keep(self, refs):
        at = [0] * len(refs)
        for j, (k, _, _, n) in enumerate(self.plans):
            refs[k][at[k] : at[k] + n, :] = self.accs[k][low_rows_at(self.walks[j][0][-1], n), :]
            at[k] += n


def strided(ref, start, count, stride):
    return jnp.concatenate([ref[t, pl.ds(start, count, stride=stride), :] for t in range(ref.shape[0])], 1)


def put_rows(ref, start, value):
    n = value.shape[0]
    for t in range(ref.shape[0]):
        ref[t, pl.ds(pl.multiple_of(start, 8), n), :] = value[:, t * LANES : (t + 1) * LANES]


def load_mode(wide_ref, m, slab, modes):
    re = strided(wide_ref, 2 * m, LAT_PAD, slab)
    im = strided(wide_ref, 2 * m + 1, LAT_PAD, slab)
    live = lax.axis_index("lat") * modes + m < KEPT
    value = jnp.concatenate([re, im], 0)
    return jnp.where(live, value, jnp.zeros_like(value)).astype(BF16)


def widen(recv_ref, wide_ref):
    shards, rows, slab, width = recv_ref.shape
    n = rows * slab

    def one(s, _):
        put_rows(wide_ref, s * n, recv_ref[s].astype(F32).reshape(n, width))
        return 0

    lax.fori_loop(0, shards, one, 0)
    if LAT % rows:
        first = LAT * slab
        last = (LAT // rows + 1) * n
        put_rows(wide_ref, first, jnp.zeros((last - first, width), F32))
    for s in range(-(-LAT // rows), shards):
        put_rows(wide_ref, s * n, jnp.zeros((n, width), F32))


def store_mode(out_s, m, value):
    put_rows(out_s, 2 * m * LAT_PAD, value)


def emit_slabs(out_s, out_ref):
    shards, rows, slab, _ = out_ref.shape

    def one(s, _):
        for r in range(rows):
            out_ref[s, r] = strided(out_s, s * rows + r, slab, LAT_PAD).astype(BF16)
        return 0

    lax.fori_loop(0, shards, one, 0)


def each_mode(modes, fn):
    few = next(n for n in (3, 2, 1) if modes % n == 0)

    def some(j, _):
        for u in range(few):
            fn(j * few + u)
        return 0

    lax.fori_loop(0, modes // few, some, 0)


def spread_blocks(w_ref, dense_s):
    _, blocks, n, _ = w_ref.shape
    dense_s[...] = jnp.zeros_like(dense_s)
    for p in range(2):
        for b in range(blocks):
            at = (p * blocks + b) * n
            dense_s[b * n : (b + 1) * n, at : at + n] = w_ref[p, b]


def pick_blocks(dense_ref, out_ref):
    _, blocks, n, lanes = out_ref.shape
    for p in range(2):
        for b in range(blocks):
            at = (p * blocks + b) * n
            block = dense_ref[b * n : (b + 1) * n, at : at + n]
            out_ref[p, b] = jnp.concatenate([block, jnp.zeros((n, lanes - n), F32)], 1)


def peers(shards, fn):
    def one(i, _):
        fn(i)
        return 0

    lax.fori_loop(1, shards, one, 0)


def emit_early(out_ref, early_s):
    rows = early_s.shape[1]
    for s in range(out_ref.shape[0]):
        early_s[s] = out_ref[s, :rows]


class Early:
    def __init__(self, src, dst, sems, rows, modes, slab, dp, me):
        self.src, self.dst, self.sems = src, dst, sems
        self.rows, self.modes, self.slab = rows, modes, slab
        self.dp, self.me, self.shards = dp, me, src.shape[0]

    def move(self, i, sender, receiver, act):
        count = self.src.shape[1]

        def piece(nr, ns):
            act(send(
                self.src.at[receiver, pl.ds(0, nr), pl.ds(0, ns)], self.dst.at[sender, pl.ds(0, nr), pl.ds(0, ns)],
                self.sems[0].at[i], self.sems[1].at[i], self.dp, receiver,
            ))

        live = row_sizes(receiver, count) if count == self.rows else [(receiver * self.rows < LAT, count)]
        each_size(live, slab_sizes(sender, self.modes, self.slab), piece)

    def own(self):
        return pltpu.make_async_copy(self.src.at[self.me], self.dst.at[self.me], self.sems[0].at[0])

    def start(self):
        self.own().start()
        peers(self.shards, lambda i: self.move(i, self.me, lax.rem(self.me + i, self.shards), lambda c: c.start()))

    def finish(self):
        self.own().wait()

        def one(i):
            self.move(i, self.me, lax.rem(self.me + i, self.shards), lambda c: c.wait_send())
            self.move(i, lax.rem(self.me + self.shards - i, self.shards), self.me, lambda c: c.wait_recv())

        peers(self.shards, one)


def spectral_forward_kernel(
    hops, x_ref, flt_ref, fa_ref, ia_ref, wi_ref, wo_ref, ng_ref, ns_ref, bi_ref, bo_ref,
    out_ref, freq_ref, hid_ref, gp_ref, t2_ref, early_ref,
    v_s, stage_s, recv_s, early_s, wide_s, out_s, wi_s, wo_s, go_send, go_recv, go_own, early_send, early_recv,
):
    g = pl.program_id(0)
    rows, lon, _ = x_ref.shape
    shards, _, slab, width = out_ref.shape
    modes = freq_ref.shape[0]
    h = LAT_PAD
    me = lax.axis_index("lat")
    dp = lax.axis_index("dp")
    early = Early(early_s, early_ref, (early_send, early_recv), rows, modes, slab, dp, me)

    hop = rows // hops

    def go(group, h, i, sender, receiver, act):
        def piece(nr, ns):
            part = (pl.ds(h * hop, nr), pl.ds(0, ns))
            act(send(
                stage_s.at[(group, receiver) + part], recv_s.at[(group, sender) + part],
                go_send.at[group, h, i], go_recv.at[group, h, i], dp, receiver,
            ))

        each_size([(sender * rows + h * hop < LAT, hop)], slab_sizes(receiver, modes, slab), piece)

    def own(group):
        return pltpu.make_async_copy(stage_s.at[group, me], recv_s.at[group, me], go_own.at[group])

    def to(i):
        return lax.rem(me + i, shards)

    def send_group(group, h):
        peers(shards, lambda i: go(group, h, i, me, to(i), lambda c: c.start()))

    @pl.when(g == 0)
    def _():
        def row(r, _):
            c, rs = center_scale(pad_rows(x_ref[r].astype(F32), COLS))
            first = (c * rs * vector(v_s, NORM_G) + vector(v_s, NORM_S)).astype(BF16)
            spec = dot(flt_ref[...], first).astype(BF16)
            for group in range(GROUPS):
                part = spec[:, group * width : (group + 1) * width]
                stage_s[group, :, r] = part.reshape(shards, slab, width)
            return 0

        put_vectors(v_s, ((NORM_G, ng_ref), (NORM_S, ns_ref)), ((INNER_B, bi_ref), (OUTER_B, bo_ref)))
        for h in range(hops):
            lax.fori_loop(h * hop, (h + 1) * hop, row, 0)
            if h == 0:
                greet(shards, me, dp)
            send_group(0, h)
        for group in range(GROUPS):
            own(group).start()
            if group:
                for h in range(hops):
                    send_group(group, h)

    spread_blocks(wi_ref, wi_s)
    spread_blocks(wo_ref, wo_s)
    if slab != 2 * modes:
        out_s[...] = jnp.zeros_like(out_s)
    for group in range(GROUPS):

        @pl.when(g == group)
        def _():
            own(group).wait()
            for h in range(hops):
                peers(shards, lambda i: go(group, h, i, lax.rem(me + shards - i, shards), me, lambda c: c.wait_recv()))
            widen(recv_s.at[group], wide_s)

    def mix(v, w_ref, bias):
        a = dot(v, w_ref[...])
        lanes = pl.ds(pl.multiple_of(g * width, LANES), width)
        re = a[:h, :width] - a[h:, width:] + v_s[bias : bias + 1, lanes]
        im = a[h:, :width] + a[:h, width:] + v_s[bias + 1 : bias + 2, lanes]
        return jnp.concatenate([re, im], 0)

    def one(m):
        fq = dot(fa_ref[...], load_mode(wide_s, m, slab, modes)).astype(BF16)
        freq_ref[m] = fq
        hid, gp = gelu_both(mix(fq, wi_s, INNER_B))
        hid = hid.astype(BF16)
        hid_ref[m] = hid
        gp_ref[m] = gp
        outer = mix(hid, wo_s, OUTER_B)
        t = jnp.tanh(outer * (1.0 / SHRINK))
        t2_ref[m] = t * t
        shrunk = (outer - SHRINK * t).astype(BF16)
        store_mode(out_s, m, dot(ia_ref[...], shrunk))

    each_mode(modes, one)
    emit_slabs(out_s, out_ref)

    @pl.when(g == 0)
    def _():
        emit_early(out_ref, early_s)
        early.start()

    @pl.when(g == GROUPS - 1)
    def _():
        early.finish()
        for group in range(GROUPS):
            for h in range(hops):
                peers(shards, lambda i: go(group, h, i, me, to(i), lambda c: c.wait_send()))


def group_specs(shards, rows, slab, modes, part):
    n = 2 * LAT_PAD
    slabs = pl.BlockSpec((shards, rows, slab, part), lambda g: (0, 0, 0, g))
    spec = pl.BlockSpec((modes, n, part), lambda g: (0, 0, g))
    pair = pl.BlockSpec((2, part), lambda g: (0, g))
    return slabs, spec, pair


def weight_spec(weight, lanes=None):
    _, blocks, n, _ = weight.shape
    return pl.BlockSpec((2, blocks // GROUPS, n, lanes or n), lambda g: (0, g, 0, 0))


def hops_of(rows):
    return 2 if rows % 4 == 0 else 1


def spectral_forward(x, tb, wi, wo, vectors, shards, slab, modes, collective_id):
    rows, lon, width = x.shape
    part = width // GROUPS
    n = 2 * LAT_PAD
    slabs, spec, _ = group_specs(shards, rows, slab, modes, part)
    hops = hops_of(rows)
    dma = pltpu.SemaphoreType.DMA
    early = (shards, rows // hops, slab, part)
    return pl.pallas_call(
        functools.partial(spectral_forward_kernel, hops),
        grid=(GROUPS,),
        in_specs=[full(x), full(tb["flt"]), full(tb["fa"]), full(tb["ia"]), weight_spec(wi), weight_spec(wo)]
        + [full(v) for v in vectors],
        out_specs=[slabs, spec, spec, spec, spec, pl.BlockSpec(memory_space=pl.ANY)],
        out_shape=[
            sds((shards, rows, slab, width), BF16),
            sds((modes, n, width), BF16),
            sds((modes, n, width), BF16),
            sds((modes, n, width), F32),
            sds((modes, n, width), F32),
            sds(early, BF16),
        ],
        scratch_shapes=[
            pltpu.VMEM((VECTOR_ROWS, width), F32),
            pltpu.VMEM((GROUPS, shards, rows, slab, part), BF16),
            pltpu.VMEM((GROUPS, shards, rows, slab, part), BF16),
            pltpu.VMEM(early, BF16),
            pltpu.VMEM((part // LANES, shards * rows * slab, LANES), F32),
            pltpu.VMEM((part // LANES, slab * LAT_PAD, LANES), F32),
            pltpu.VMEM((part, 2 * part), BF16),
            pltpu.VMEM((part, 2 * part), BF16),
            dma((GROUPS, hops, shards)), dma((GROUPS, hops, shards)), dma((GROUPS,)), dma((shards,)), dma((shards,)),
        ],
        compiler_params=params(collective_id=collective_id, has_side_effects=True),
        name="spectral_forward",
    )(x, tb["flt"], tb["fa"], tb["ia"], wi, wo, *vectors)


def spectral_backward_kernel(
    groups, plans, recv_ref, iat_ref, fat_ref, wo_ref, wi_ref, freq_ref, hid_ref, gp_ref, t2_ref, dw1_ref, dw2_ref,
    out_ref, dwo_ref, dbo_ref, dwi_ref, dbi_ref, part1_ref, part2_ref, early_ref,
    wide_s, out_s, wo_s, wi_s, dwo_s, dwi_s, acc1_s, acc2_s, recv1_s, recv2_s, early_s,
    load_sem, send_sems, recv_sems, early_send, early_recv,
):
    shards = recv_ref.shape[0]
    slab, width = recv_ref.shape[2:]
    modes = freq_ref.shape[0]
    h = LAT_PAD
    g = pl.program_id(0)
    me = lax.axis_index("lat")
    dp = lax.axis_index("dp")
    early = Early(early_s, early_ref, (early_send, early_recv), early_s.shape[1], modes, slab, dp, me)
    halving = Halving(plans, (acc1_s, acc2_s), (recv1_s, recv2_s), send_sems, recv_sems, dp, me)
    loads = [
        pltpu.make_async_copy(dw1_ref, acc1_s, load_sem.at[0]),
        pltpu.make_async_copy(dw2_ref, acc2_s, load_sem.at[1]),
    ]

    @pl.when(g == 0)
    def _():
        for copy in loads:
            copy.start()
        lat_peers = [(dp, lax.rem(me + i, shards)) for i in range(1, shards)]
        signal_all(lat_peers + [peer for peer in dp_halving_peers(groups, dp, me)])
        for copy in loads:
            copy.wait()
        halving.start(0)

    whole = GROUPS * modes
    when_due = [whole * n // 8 // 3 * 3 for n in (1, 4, 6, 7)]

    widen(recv_ref, wide_s)
    spread_blocks(wo_ref, wo_s)
    spread_blocks(wi_ref, wi_s)
    if slab != 2 * modes:
        out_s[...] = jnp.zeros_like(out_s)
    for ref in (dwo_s, dbo_ref, dwi_s, dbi_ref):
        ref[...] = jnp.zeros_like(ref)

    def lowered(grad):
        return grad[:h].astype(BF16), grad[h:].astype(BF16)

    def grads(ref, first, lows, dw_ref, db_ref):
        value = ref[pl.ds(first, len(lows))].reshape(len(lows) * 2 * h, width)
        both = [jnp.concatenate(low, 0) for low in lows]
        turned = [jnp.concatenate([im, -re], 0) for re, im in lows]
        grad = jnp.concatenate([jnp.concatenate(both, 0), jnp.concatenate(turned, 0)], 1)
        dw_ref[...] += dot_tn(value, grad)
        for part in range(2):
            total = sum(jnp.sum(low[part].astype(F32), 0, keepdims=True) for low in lows)
            db_ref[part : part + 1] += total
        return both

    def pull(v, w_ref):
        a = dot_nt(v, w_ref[:, :width])
        b = dot_nt(v, w_ref[:, width:])
        return jnp.concatenate([a[:h] + b[h:], a[h:] - b[:h]], 0)

    few = next(n for n in (3, 2, 1) if modes % n == 0)

    def some(j, _):
        first = j * few
        for stage, when in enumerate(when_due):
            pl.when(g * modes + first == when)(functools.partial(halving.tick, stage))
        lows = []
        for u in range(few):
            m = first + u
            merged = dot(iat_ref[...], load_mode(wide_s, m, slab, modes))
            lows.append(lowered(merged * t2_ref[m]))
        outer_grads = grads(hid_ref, first, lows, dwo_s, dbo_ref)
        lows = [lowered(pull(og, wo_s) * gp_ref[first + u]) for u, og in enumerate(outer_grads)]
        inner_grads = grads(freq_ref, first, lows, dwi_s, dbi_ref)
        for u, ig in enumerate(inner_grads):
            store_mode(out_s, first + u, dot(fat_ref[...], pull(ig, wi_s).astype(BF16)))
        return 0

    lax.fori_loop(0, modes // few, some, 0)
    pick_blocks(dwo_s, dwo_ref)
    pick_blocks(dwi_s, dwi_ref)
    emit_slabs(out_s, out_ref)

    @pl.when(g == 0)
    def _():
        emit_early(out_ref, early_s)
        early.start()

    @pl.when(g == GROUPS - 1)
    def _():
        for stage in range(len(when_due), halving.stages):
            halving.tick(stage)
        halving.keep((part1_ref, part2_ref))
        early.finish()


def spectral_backward(recv, tb, wo, wi, freq, hid, gp, t2, dw1, dw2, groups, plans, collective_id):
    shards, rows, slab, width = recv.shape
    modes = freq.shape[0]
    part = width // GROUPS
    slabs, spec, pair = group_specs(shards, rows, slab, modes, part)
    dw = sds(wo.shape[:3] + (LANES,), F32)
    grad = weight_spec(wo, LANES)
    db = sds((2, width), F32)
    any_ = pl.BlockSpec(memory_space=pl.ANY)
    whole = lambda n, w: pl.BlockSpec((n, w), lambda g: (0, 0))
    n1, n2 = (sum(n for k, _, _, n in plans if k == which) for which in range(2))
    stages = len(plans[0][2])
    dma = pltpu.SemaphoreType.DMA
    return pl.pallas_call(
        functools.partial(spectral_backward_kernel, groups, plans),
        grid=(GROUPS,),
        in_specs=[slabs, full(tb["iat"]), full(tb["fat"]), weight_spec(wo), weight_spec(wi), spec, spec, spec, spec]
        + [any_, any_],
        out_specs=[slabs, grad, pair, grad, pair, whole(n1, dw1.shape[1]), whole(n2, dw2.shape[1]), any_],
        out_shape=[
            sds(recv.shape, BF16), dw, db, dw, db,
            sds((n1, dw1.shape[1]), BF16), sds((n2, dw2.shape[1]), BF16),
            sds((shards, rows, slab, part), BF16),
        ],
        scratch_shapes=[
            pltpu.VMEM((part // LANES, shards * rows * slab, LANES), F32),
            pltpu.VMEM((part // LANES, slab * LAT_PAD, LANES), F32),
            pltpu.VMEM((part, 2 * part), BF16),
            pltpu.VMEM((part, 2 * part), BF16),
            pltpu.VMEM((part, 2 * part), F32),
            pltpu.VMEM((part, 2 * part), F32),
            pltpu.VMEM(dw1.shape, BF16),
            pltpu.VMEM(dw2.shape, BF16),
            pltpu.VMEM((sum(received(p) for k, _, p, _ in plans if k == 0), dw1.shape[1]), BF16),
            pltpu.VMEM((sum(received(p) for k, _, p, _ in plans if k == 1), dw2.shape[1]), BF16),
            pltpu.VMEM((shards, rows, slab, part), BF16),
            dma((2,)), dma((len(plans), stages)), dma((len(plans), stages)), dma((shards,)), dma((shards,)),
        ],
        compiler_params=params(collective_id=collective_id, has_side_effects=True),
        name="spectral_backward",
    )(recv, tb["iat"], tb["fat"], wo, wi, freq, hid, gp, t2, dw1, dw2)


def gather_row(r_ref, row, modes):
    shards, _, slab, width = r_ref.shape
    whole = KEPT // modes
    parts = [r_ref[:whole, row].astype(F32).reshape(whole * slab, width)]
    rest = (shards - whole) * slab
    if KEPT % modes:
        n = up8(2 * (KEPT % modes))
        parts.append(r_ref[whole, row].astype(F32)[:n])
        rest -= n
    if rest:
        parts.append(jnp.zeros((rest, width), F32))
    return jnp.concatenate(parts, 0).astype(BF16)


def feed_kernel(
    per, chunk, hops, modes, scale_ref, x_ref, c_ref, back_ref, early_ref, il_ref, ilt_ref, w1_ref, w2_ref,
    ng_ref, ns_ref, pg_ref, ps_ref, rb_ref, eb_ref,
    lo_ref, mg_ref, out_ref, dw1_ref, dw2_ref, deb_ref, drb_ref, dpg_ref, dps_ref,
    v_ref, slab_s, w1_s, w2_s, act_s, pre_s, sec_s, sect_s, up_s, mixed_s, xhat_s, rs_s, branch_s, grad_s,
    w_sem, dw_sem, early_sem, in_send, in_recv, in_own, out_send, out_recv, out_own,
):
    g = pl.program_id(0)
    steps = pl.num_programs(0)
    lon, width = x_ref.shape[1:]
    hidden = w1_s.shape[1]
    shards, rows, slab, _ = slab_s.shape
    hop = rows // hops
    every = steps // hops
    tall = per * COLS
    me = lax.axis_index("lat")
    dp = lax.axis_index("dp")

    def transfer(src, dst, sems, h, lanes, i, sender, receiver, row_owner, mode_owner, act):
        part = pl.ds(h * hop, hop)

        def piece(nr, ns):
            act(send(
                src.at[receiver, part, pl.ds(0, ns), lanes], dst.at[sender, part, pl.ds(0, ns), lanes],
                sems[0].at[h, i], sems[1].at[h, i], dp, receiver,
            ))

        live = row_owner * rows + h * hop < LAT
        each_size([(live, hop)], slab_sizes(mode_owner, modes, slab), piece)

    known = early_ref.shape[3]

    def fresh(h):
        return pl.ds(known, width - known) if h == 0 else pl.ds(0, width)

    def incoming(h, i, sender, receiver, act):
        transfer(
            back_ref, slab_s, (in_send, in_recv), h, fresh(h), i, sender, receiver, receiver, sender, act
        )

    def outgoing(h, i, sender, receiver, act):
        transfer(
            slab_s, out_ref, (out_send, out_recv), h, pl.ds(0, width), i, sender, receiver, sender, receiver, act
        )

    def own_in(h):
        part = pl.ds(h * hop, hop)
        return pltpu.make_async_copy(
            back_ref.at[me, part, :, fresh(h)], slab_s.at[me, part, :, fresh(h)], in_own.at[h]
        )

    early = pltpu.make_async_copy(early_ref, slab_s.at[:, pl.ds(0, hop), :, pl.ds(0, known)], early_sem)

    def own_out(h):
        part = pl.ds(h * hop, hop)
        return pltpu.make_async_copy(slab_s.at[me, part], out_ref.at[me, part], out_own.at[h])

    def to(i):
        return lax.rem(me + i, shards)

    def source(i):
        return lax.rem(me + shards - i, shards)

    def fetch(h):
        own_in(h).start()
        peers(shards, lambda i: incoming(h, i, me, to(i), lambda c: c.start()))

    weights = [
        pltpu.make_async_copy(w1_ref, w1_s, w_sem.at[0]),
        pltpu.make_async_copy(w2_ref, w2_s, w_sem.at[1]),
    ]

    @pl.when(g == 0)
    def _():
        for copy in weights:
            copy.start()
        early.start()
        greet(shards, me, dp)
        fetch(0)
        put_vectors(
            v_ref,
            (
                (NORM_G, ng_ref), (NORM_S, ns_ref), (POST_G, pg_ref), (POST_S, ps_ref), (REDUCE_B, rb_ref),
                (EXPAND_B, eb_ref),
            ),
            (),
        )
        for ref in (deb_ref, drb_ref, dpg_ref, dps_ref):
            ref[...] = jnp.zeros_like(ref)

    for h in range(hops):

        @pl.when(g == h * every)
        def _():
            if h == 0:
                early.wait()
            own_in(h).wait()
            peers(shards, lambda i: incoming(h, i, source(i), me, lambda c: c.wait_recv()))
            if h + 1 < hops:
                fetch(h + 1)

    at = pl.ds(0 if rows == per else pl.multiple_of(g * tall, tall), tall)
    for i in range(per):
        rows_i = pl.ds(i * COLS, COLS)
        x = pad_rows(x_ref[i].astype(F32), COLS)
        c, rs = center_scale(x)
        first = c * rs * vector(v_ref, NORM_G) + vector(v_ref, NORM_S)
        filtered = dot(il_ref[...], gather_row(slab_s, g * per + i, modes))
        live = me * rows + g * per + i < LAT
        mixed = jnp.where(live, filtered, jnp.zeros_like(filtered)) + first + x
        c, rs = center_scale(mixed)
        xhat = c * rs
        mixed_s[rows_i, :] = mixed
        xhat_s[rows_i, :] = xhat
        rs_s[rows_i, :] = jnp.broadcast_to(rs, (COLS, LANES))
        sec_s[rows_i, :] = (xhat * vector(v_ref, POST_G) + vector(v_ref, POST_S)).astype(BF16)
        up = (pad_rows(c_ref[i].astype(F32), COLS) * scale_ref[0, g * per + i]).astype(BF16)
        up_s[pl.ds(pl.multiple_of(g * tall + i * COLS, COLS), COLS), :] = up
        drb_ref[...] += jnp.sum(up.astype(F32), 0, keepdims=True)
    sect_s[:, at] = sec_s[...].T
    branch_s[...] = jnp.broadcast_to(vector(v_ref, REDUCE_B), branch_s.shape)
    grad_s[...] = jnp.zeros_like(grad_s)

    @pl.when(g == 0)
    def _():
        for copy in weights:
            copy.wait()

    def hidden_chunk(j, _):
        ds = pl.ds(pl.multiple_of(j * chunk, chunk), chunk)
        act, slope = gelu_both(dot(sec_s[...], w1_s[:, ds]) + v_ref[pl.ds(EXPAND_B + j, 1), :])
        act = act.astype(BF16)
        act_s[at, ds] = act
        pre = (dot_nt(up_s[at, :], w2_s[ds, :]) * slope).astype(BF16)
        pre_s[at, ds] = pre
        deb_ref[pl.ds(j, 1), :] += jnp.sum(pre.astype(F32), 0, keepdims=True)
        branch_s[...] += dot(act, w2_s[ds, :])
        grad_s[...] += dot_nt(pre, w1_s[:, ds])
        return 0

    lax.fori_loop(0, hidden // chunk, hidden_chunk, 0)
    for i in range(per):
        rows_i = pl.ds(i * COLS, COLS)
        grad = grad_s[rows_i, :]
        xhat = xhat_s[rows_i, :]
        up = pad_rows(c_ref[i].astype(F32), COLS) * scale_ref[0, g * per + i]
        mg = up + norm_back(grad, xhat, rs_s[rows_i, 0:1], vector(v_ref, POST_G))
        mg_ref[i] = mg[:lon]
        rg = dot(ilt_ref[...], mg.astype(BF16)).astype(BF16)
        slab_s[:, g * per + i] = rg.reshape(shards, slab, width)

    @pl.when(lax.rem(g, every) == every - 1)
    def _():
        h = g // every
        own_out(h).start()
        peers(shards, lambda i: outgoing(h, i, me, to(i), lambda c: c.start()))

    for i in range(per):
        rows_i = pl.ds(i * COLS, COLS)
        keep = scale_ref[1, g * per + i]
        lo_ref[i] = ((mixed_s[rows_i, :] + branch_s[rows_i, :]) * keep).astype(BF16)[:lon]
        grad = grad_s[rows_i, :]
        dpg_ref[...] += jnp.sum(grad * xhat_s[rows_i, :], 0, keepdims=True)
        dps_ref[...] += jnp.sum(grad, 0, keepdims=True)

    def gradients(j):
        ds = pl.ds(pl.multiple_of(j * chunk, chunk), chunk)
        side = dw1_ref.shape[1] // chunk
        place = (
            pl.ds(pl.multiple_of(j // side * width, width), width),
            pl.ds(pl.multiple_of(lax.rem(j, side) * chunk, chunk), chunk),
        )
        return (
            pltpu.make_async_copy(w1_s.at[:, ds], dw1_ref.at[place], dw_sem.at[0, j]),
            pltpu.make_async_copy(w2_s.at[ds, :], dw2_ref.at[ds, :], dw_sem.at[1, j]),
        )

    @pl.when(g == steps - 1)
    def _():
        def weight_chunk(j, _):
            ds = pl.ds(pl.multiple_of(j * chunk, chunk), chunk)
            w1_s[:, ds] = dot(sect_s[...], pre_s[:, ds]).astype(BF16)
            w2_s[ds, :] = dot_tn(act_s[:, ds], up_s[...]).astype(BF16)
            for copy in gradients(j):
                copy.start()
            return 0

        lax.fori_loop(0, hidden // chunk, weight_chunk, 0)

        for h in range(hops):
            own_out(h).wait()

            def wait_all(i):
                incoming(h, i, me, to(i), lambda c: c.wait_send())
                outgoing(h, i, me, to(i), lambda c: c.wait_send())
                outgoing(h, i, source(i), me, lambda c: c.wait_recv())

            peers(shards, wait_all)

        def finish(j, _):
            for copy in gradients(j):
                copy.wait()
            return 0

        lax.fori_loop(0, hidden // chunk, finish, 0)


def feed(scale, x, cot, back, early, tb, w1, w2, vectors, modes, collective_id):
    rows, lon, width = x.shape
    hidden = w1.shape[1]
    shards, _, slab, _ = back.shape
    per = next(n for n in (2, 3, 1) if rows % n == 0)
    steps = rows // per
    hops = hops_of(rows)
    chunk = width
    row = pl.BlockSpec((per, lon, width), lambda g: (g, 0, 0))
    any_ = pl.BlockSpec(memory_space=pl.ANY)
    vec = lambda n: pl.BlockSpec((n, width), lambda g: (0, 0))
    tall = per * COLS
    total = rows * COLS
    dma = pltpu.SemaphoreType.DMA
    return pl.pallas_call(
        functools.partial(feed_kernel, per, chunk, hops, modes),
        grid=(steps,),
        in_specs=[
            pl.BlockSpec(memory_space=pltpu.SMEM), row, row, any_, any_, full(tb["il"]), full(tb["ilt"]), any_, any_,
        ]
        + [full(v) for v in vectors],
        out_specs=[row, row, any_, any_, any_, vec(hidden // width), vec(1), vec(1), vec(1)],
        out_shape=[
            sds((rows, lon, width), BF16),
            sds((rows, lon, width), F32),
            sds(back.shape, BF16),
            sds((2 * width, hidden // 2), BF16),
            sds(w2.shape, BF16),
            sds((hidden // width, width), F32),
            sds((1, width), F32),
            sds((1, width), F32),
            sds((1, width), F32),
        ],
        scratch_shapes=[
            pltpu.VMEM((VECTOR_ROWS, width), F32),
            pltpu.VMEM(back.shape, BF16),
            pltpu.VMEM(w1.shape, BF16),
            pltpu.VMEM(w2.shape, BF16),
            pltpu.VMEM((total, hidden), BF16),
            pltpu.VMEM((total, hidden), BF16),
            pltpu.VMEM((tall, width), BF16),
            pltpu.VMEM((width, total), BF16),
            pltpu.VMEM((total, width), BF16),
            pltpu.VMEM((tall, width), F32),
            pltpu.VMEM((tall, width), F32),
            pltpu.VMEM((tall, LANES), F32),
            pltpu.VMEM((tall, width), F32),
            pltpu.VMEM((tall, width), F32),
            dma((2,)), dma((2, hidden // chunk)), dma,
            dma((hops, shards)), dma((hops, shards)), dma((hops,)),
            dma((hops, shards)), dma((hops, shards)), dma((hops,)),
        ],
        compiler_params=pltpu.CompilerParams(
            vmem_limit_bytes=63 * 2**20, collective_id=collective_id, has_side_effects=True
        ),
        name="feed",
    )(scale, x, cot, back, early, tb["il"], tb["ilt"], w1, w2, *vectors)


def leave_kernel(
    groups, hops, modes, plans, x_ref, back_ref, early_ref, mg_ref, fl_ref, ng_ref, *refs,
):
    weight_refs, line_refs, refs = refs[:2], refs[2:8], refs[8:]
    (
        part1_ref, part2_ref, out_ref, sums_ref, norm_ref, dw1_ref, dw2_ref,
        v_ref, slab_s, line_s, mine_s, from_dp, part_s, from_lat, all_s, norm_lat, norm_dp,
        in_send, in_recv, in_own, early_sem, wide_send, wide_recv, own_sem, small_sems,
    ) = refs
    g = pl.program_id(0)
    steps = pl.num_programs(0)
    lon = x_ref.shape[1]
    shards, rows, slab, _ = slab_s.shape
    n = from_lat.shape[1]
    hop = rows // hops
    me = lax.axis_index("lat")
    dp = lax.axis_index("dp")
    lat_peers = [lax.rem(me + i, shards) for i in range(1, shards)]
    dp_peers = [lax.rem(dp + i, groups) for i in range(1, groups)]

    known = early_ref.shape[3]
    fresh = pl.ds(known, slab_s.shape[3] - known)
    early = pltpu.make_async_copy(early_ref, slab_s.at[:, :, :, pl.ds(0, known)], early_sem)

    def incoming(h, i, sender, receiver, act):
        part = pl.ds(h * hop, hop)

        def piece(nr, ns):
            act(send(
                back_ref.at[receiver, part, pl.ds(0, ns), fresh], slab_s.at[sender, part, pl.ds(0, ns), fresh],
                in_send.at[h, i], in_recv.at[h, i], dp, receiver,
            ))

        live = receiver * rows + h * hop < LAT
        each_size([(live, hop)], slab_sizes(sender, modes, slab), piece)

    def own_in(h):
        part = pl.ds(h * hop, hop)
        return pltpu.make_async_copy(back_ref.at[me, part, :, fresh], slab_s.at[me, part, :, fresh], in_own.at[h])

    def fetch(h):
        own_in(h).start()
        peers(shards, lambda i: incoming(h, i, me, lax.rem(me + i, shards), lambda c: c.start()))

    def arrived(h):
        own_in(h).wait()
        peers(shards, lambda i: incoming(h, i, lax.rem(me + shards - i, shards), me, lambda c: c.wait_recv()))

    walks = [halving_walk(first, plan, dp, me) for _, first, plan, _ in plans]
    outs = (dw1_ref, dw2_ref)
    parts = (part1_ref, part2_ref)
    stages = len(plans[0][2])
    count = len(plans)

    def part(j):
        k, _, _, n = plans[j]
        at = sum(rest for which, _, _, rest in plans[:j] if which == k)
        return parts[k].at[pl.ds(at, n)]

    def own_part(j):
        k, _, _, n = plans[j]
        return pltpu.make_async_copy(part(j), outs[k].at[low_rows_at(walks[j][0][-1], n)], own_sem.at[j])

    def spread(j, stage):
        k, _, plan, _ = plans[j]
        _, _, n, halved = plan[stage]
        if not halved:
            return None
        where = low_rows_at(walks[j][0][stage + 1], n // 2)
        first = not any(later[3] for later in plan[stage + 1 :])
        return pltpu.make_async_remote_copy(
            src_ref=part(j) if first else outs[k].at[where], dst_ref=outs[k].at[where],
            send_sem=wide_send.at[j, stage], recv_sem=wide_recv.at[j, stage],
            device_id=walks[j][2][stage], device_id_type=MESH,
        )

    def spread_all(stage, act):
        for j in range(count):
            copy = spread(j, stage)
            if copy is not None:
                act(copy)

    def tick(i):
        stage = stages - 1 - i
        spread_all(stage, lambda c: c.wait())
        if i == 0:
            for j in range(count):
                own_part(j).wait()
        if stage:
            spread_all(stage - 1, lambda c: c.start())


    def remote(src, dst, stage, i, to):
        return pltpu.make_async_remote_copy(
            src_ref=src, dst_ref=dst, send_sem=small_sems.at[stage, 0, i], recv_sem=small_sems.at[stage, 1, i],
            device_id=to, device_id_type=MESH,
        )

    def over(peers_, axis):
        return [(i, p, (p, me) if axis == "dp" else (dp, p)) for i, p in enumerate(peers_)]

    block = shards * n
    mine = low_rows_at((dp * shards + me) * n, n)
    mine_dp = low_rows_at(dp * block, block)
    tiles = line_s.shape[1] // LANES

    def small(stage):
        if stage == 0:
            return [
                remote(mine_s.at[low_rows_at(p * block, block)], from_dp.at[i], 0, i, to)
                for i, p, to in over(dp_peers, "dp")
            ]
        if stage == 1:
            return [
                remote(part_s.at[low_rows_at(p * n, n)], from_lat.at[i], 1, i, to)
                for i, p, to in over(lat_peers, "lat")
            ]
        if stage == 2:
            return [remote(all_s.at[mine], all_s.at[mine], 2, i, to) for i, p, to in over(lat_peers, "lat")]
        if stage == 3:
            return [remote(all_s.at[mine_dp], all_s.at[mine_dp], 3, i, to) for i, p, to in over(dp_peers, "dp")]
        if stage == 4:
            return [remote(norm_lat.at[me], norm_lat.at[me], 4, i, to) for i, p, to in over(lat_peers, "lat")]
        return [remote(norm_dp.at[dp], norm_dp.at[dp], 5, i, to) for i, p, to in over(dp_peers, "dp")]

    def begin(stage):
        for copy in small(stage):
            copy.start()

    def end(stage):
        for copy in small(stage):
            copy.wait()
        if stage == 0:
            whole = mine_s[mine_dp, :].astype(F32) + jnp.sum(from_dp[...].astype(F32), 0)
            part_s[...] = whole.astype(BF16)
        if stage == 1:
            whole = part_s[low_rows_at(me * n, n), :].astype(F32) + jnp.sum(from_lat[...].astype(F32), 0)
            all_s[mine, :] = whole.astype(BF16)

    def small_tick(stage):
        end(stage)
        begin(stage + 1)

    @pl.when(g == 0)
    def _():
        early.start()
        for j in range(count):
            own_part(j).start()
        signal_all([(dp, p) for p in lat_peers] + [(p, me) for p in dp_peers])
        spread_all(stages - 1, lambda c: c.start())
        fetch(0)
        put_vectors(v_ref, ((NORM_G, ng_ref),), ())
        at = 0
        for ref in weight_refs:
            value = ref[...].reshape(-1, LANES)
            mine_s[at : at + value.shape[0], :] = value.astype(BF16)
            at += value.shape[0]
        lines = [
            ref[row : row + 1, t * LANES : (t + 1) * LANES]
            for ref in line_refs
            for row in range(ref.shape[0])
            for t in range(tiles)
        ]
        lines.append(jnp.zeros((mine_s.shape[0] - at - len(lines), LANES), F32))
        mine_s[at:, :] = jnp.concatenate(lines, 0).astype(BF16)
        begin(0)
        line_s[...] = jnp.zeros_like(line_s)
        tick(0)
        small_tick(0)
        early.wait()
        arrived(0)
        tick(1)
        small_tick(1)
        if hops > 1:
            fetch(1)

    for h in range(1, hops):
        pl.when(g == h * hop)(functools.partial(arrived, h))

    x = pad_rows(x_ref[0].astype(F32), COLS)
    c, rs = center_scale(x)
    xhat = c * rs
    mg = pad_rows(mg_ref[0], COLS)
    live = me * rows + g < LAT
    spectrum = dot(fl_ref[...], gather_row(slab_s, g, modes))
    grad = jnp.where(live, spectrum, jnp.zeros_like(spectrum)) + mg
    line_s[0:1] += jnp.sum(grad * xhat, 0, keepdims=True)
    line_s[1:2] += jnp.sum(grad, 0, keepdims=True)
    out_ref[...] = (mg + norm_back(grad, xhat, rs, vector(v_ref, NORM_G)))[:lon].reshape(out_ref.shape)

    @pl.when(g == hop - 1)
    def _():
        tick(2)
        small_tick(2)

    @pl.when(g == steps - 1)
    def _():
        norm_lat[me] = line_s[...]
        begin(4)
        for i in range(3, stages):
            tick(i)
        end(4)
        norm_dp[dp] = jnp.sum(norm_lat[...], 0)
        begin(5)
        end(3)
        sums_ref[...] = all_s[...].astype(F32)
        for h in range(hops):
            peers(shards, lambda i: incoming(h, i, me, lax.rem(me + i, shards), lambda c: c.wait_send()))
        end(5)
        norm_ref[...] = jnp.sum(norm_dp[...], 0)


def leave(x, back, early, mg, fl, gain, small, part1, part2, shapes, groups, plans, modes, collective_id):
    rows, lon, width = x.shape
    shards, _, slab, _ = back.shape
    hops = hops_of(rows)
    stages = len(plans[0][2])
    unit = LOW_ROWS * groups * shards
    total = -(-sum(v.size // LANES for v in small) // unit) * unit
    n = total // (groups * shards)
    row = pl.BlockSpec((1, lon, width), lambda r: (r, 0, 0))
    any_ = pl.BlockSpec(memory_space=pl.ANY)
    whole = lambda *shape: pl.BlockSpec(shape, lambda r: (0,) * len(shape))
    dma = pltpu.SemaphoreType.DMA
    return pl.pallas_call(
        functools.partial(leave_kernel, groups, hops, modes, plans),
        grid=(rows,),
        in_specs=[row, any_, any_, row, full(fl), full(gain)] + [full(v) for v in small] + [any_, any_],
        out_specs=[pl.BlockSpec((lon, 1, width), lambda r: (r, 0, 0)), whole(total, LANES), whole(2, width), any_, any_],
        out_shape=[sds((rows * lon, 1, width), F32), sds((total, LANES), F32), sds((2, width), F32)]
        + [sds(shape, BF16) for shape in shapes],
        scratch_shapes=[
            pltpu.VMEM((VECTOR_ROWS, width), F32),
            pltpu.VMEM(back.shape, BF16),
            pltpu.VMEM((2, width), F32),
            pltpu.VMEM((total, LANES), BF16),
            pltpu.VMEM((groups - 1, shards * n, LANES), BF16),
            pltpu.VMEM((shards * n, LANES), BF16),
            pltpu.VMEM((shards - 1, n, LANES), BF16),
            pltpu.VMEM((total, LANES), BF16),
            pltpu.VMEM((shards, 2, width), F32),
            pltpu.VMEM((groups, 2, width), F32),
            dma((hops, shards)), dma((hops, shards)), dma((hops,)), dma,
            dma((len(plans), stages)), dma((len(plans), stages)), dma((len(plans),)),
            dma((6, 2, max(groups, shards) - 1)),
        ],
        compiler_params=params(collective_id=collective_id, has_side_effects=True),
        name="leave",
    )(x, back, early, mg, fl, gain, *small, part1, part2)


def shards_fn(
    groups, shards, inputs, cotangent, storm_weight, norm_gain, norm_shift, inner_weight, inner_bias,
    outer_weight, outer_bias, post_gain, post_shift, expand_weight, expand_bias, reduce_weight, reduce_bias,
):
    _, rows, lon, width = inputs.shape
    modes = LON_PAD // shards
    slab = slab_rows(modes)
    tb = make_tables(shards, modes)
    row_ids = lax.axis_index("lat") * rows + jnp.arange(rows, dtype=jnp.int32)
    keep = (row_ids < LAT).astype(F32)
    scale = jnp.stack([keep * (storm_weight[0].astype(F32) / 64.0), keep])
    x = inputs[0]
    cot = cotangent[0]
    back, freq, hid, gp, t2, early = spectral_forward(
        x, tb, inner_weight, outer_weight, (norm_gain, norm_shift, inner_bias, outer_bias), shards, slab, modes, 0
    )
    (layer_out, mixed_grad, mode_grad, dw1, dw2, deb, drb, dpg, dps) = feed(
        scale, x, cot, back, early, tb, expand_weight, reduce_weight,
        (norm_gain, norm_shift, post_gain, post_shift, reduce_bias, expand_bias), modes, 1
    )
    plans = halving_plans(groups, shards, (dw1.shape[0], dw2.shape[0]))
    slab_grad, dwo, dbo, dwi, dbi, part1, part2, early = spectral_backward(
        mode_grad, tb, outer_weight, inner_weight, freq, hid, gp, t2, dw1, dw2, groups, plans, 2
    )
    small = (dwi, dwo, dbi, dbo, dpg, dps, deb, drb)
    input_grad, sums, norm, dw1, dw2 = leave(
        x, slab_grad, early, mixed_grad, tb["fl"], norm_gain, small, part1, part2,
        (dw1.shape, dw2.shape), groups, plans, modes, 3
    )
    dw1 = jnp.concatenate([dw1[:width], dw1[width:]], 1).astype(F32)
    dw2 = dw2.astype(F32)
    ends = np.cumsum([v.size // LANES for v in small])
    dwi, dwo, dbi, dbo, dpg, dps, deb, drb = [
        sums[e - v.size // LANES : e] for v, e in zip(small, ends)
    ]
    block = inner_weight.shape[-1]
    weight = lambda v: v.reshape(inner_weight.shape[:3] + (LANES,))[..., :block]
    line = lambda v: v.reshape(-1)
    return (
        layer_out[None], input_grad.reshape(1, rows, lon, width), norm[0], norm[1],
        weight(dwi), dbi.reshape(inner_bias.shape), weight(dwo), dbo.reshape(outer_bias.shape),
        line(dpg), line(dps), dw1, line(deb), dw2, line(drb),
    )


def solution(mesh):
    split = P("dp", "lat", None, None)
    return jax.shard_map(
        functools.partial(shards_fn, mesh.shape["dp"], mesh.shape["lat"]),
        mesh=mesh,
        in_specs=(split, split, P("dp")) + (P(),) * 12,
        out_specs=(split, split) + (P(),) * 12,
        check_vma=False,
    )
```

```python
import functools
import math

import jax
import jax.numpy as jnp
import ml_dtypes
import numpy as np
from jax import lax
from jax.experimental import pallas as pl
from jax.experimental.pallas import tpu as pltpu
from jax.sharding import PartitionSpec as P

BLOCKS = 8
LAT = 90
LON = 180
LAT_PAD = 96
LON_PAD = 96
KEPT = LON // 2 + 1
COLS = 192
GROUPS = 2
LANES = 128
LOW_ROWS = 16
NORM_G, NORM_S, POST_G, POST_S, REDUCE_B, INNER_B, OUTER_B, EXPAND_B = 0, 1, 2, 3, 4, 5, 7, 9

SHRINK = 0.01
EPS = 1e-6
SQRT_HALF = 0.7071067811865476
PDF_SCALE = 0.3989422804014327

F32 = jnp.float32
BF16 = jnp.bfloat16
MESH = pl.DeviceIdType.MESH
VMEM_LIMIT = 62 * 2**20


def base_tables():
    f = np.float32
    modes = np.arange(LON_PAD)
    columns = np.arange(LON)
    phases = (columns[:, None] * modes[None, :] % LON).astype(f) * f(2.0 * math.pi / LON)
    kept = (modes < LON // 2 + 1).astype(f)
    factor = np.where((modes == 0) | (modes == LON // 2), f(1), f(2)) * kept
    scale = f(1.0 / math.sqrt(LON))
    forward_lon = np.stack([np.cos(phases) * kept, -np.sin(phases) * kept], axis=1) * scale
    inverse_lon = np.stack([np.cos(phases) * factor, -np.sin(phases) * factor], axis=1) * scale
    rows = np.arange(LAT_PAD)
    angles = (rows[:, None] * rows[None, :] % LAT).astype(f) * f(2.0 * math.pi / LAT)
    inside = ((rows[:, None] < LAT) & (rows[None, :] < LAT)).astype(f) / f(math.sqrt(LAT))
    cs = np.cos(angles) * inside
    sn = np.sin(angles) * inside
    forward_lat = np.stack([np.stack([cs, sn], 1), np.stack([-sn, cs], 1)], 0)
    inverse_lat = np.stack([np.stack([cs, -sn], 1), np.stack([sn, cs], 1)], 0)
    return forward_lon, inverse_lon, forward_lat, inverse_lat


def slab_rows(modes):
    return -(-2 * modes // 8) * 8


def lon_table(table, shards, modes):
    slab = slab_rows(modes)
    out = np.zeros((COLS, shards, slab), np.float32)
    split = table.reshape(LON, 2, shards, modes).transpose(0, 2, 3, 1)
    out[:LON, :, : 2 * modes] = split.reshape(LON, shards, 2 * modes)
    return out.reshape(COLS, shards * slab)


def make_tables(shards, modes):
    forward_lon, inverse_lon, forward_lat, inverse_lat = base_tables()
    low = lambda t: jnp.asarray(np.ascontiguousarray(t).astype(ml_dtypes.bfloat16))
    n = 2 * LAT_PAD
    fl = lon_table(forward_lon, shards, modes)
    il = lon_table(inverse_lon, shards, modes)
    fa = forward_lat.reshape(n, n)
    ia = inverse_lat.reshape(n, n)
    return dict(
        fl=low(fl), flt=low(fl.T), il=low(il), ilt=low(il.T),
        fa=low(fa), fat=low(fa.T), ia=low(ia), iat=low(ia.T),
    )


def dot(a, b):
    return jnp.dot(a, b, preferred_element_type=F32)


def dot_nt(a, b):
    return lax.dot_general(a, b, (((1,), (1,)), ((), ())), preferred_element_type=F32)


def dot_tn(a, b):
    return lax.dot_general(a, b, (((0,), (0,)), ((), ())), preferred_element_type=F32)


def gelu_both(v):
    cdf = 0.5 * (1.0 + lax.erf(v * SQRT_HALF))
    pdf = jnp.exp(-0.5 * v * v) * PDF_SCALE
    return v * cdf, cdf + v * pdf


def center_scale(v):
    inv = 1.0 / v.shape[-1]
    c = v - jnp.sum(v, -1, keepdims=True) * inv
    return c, lax.rsqrt(jnp.sum(c * c, -1, keepdims=True) * inv + EPS)


def pad_rows(v, n):
    return jnp.concatenate([v, jnp.zeros((n - v.shape[0], v.shape[1]), v.dtype)], 0)


def norm_back(grad, xhat, rs, gain):
    inv = 1.0 / grad.shape[-1]
    dx = grad * gain
    m1 = jnp.sum(dx, -1, keepdims=True) * inv
    m2 = jnp.sum(dx * xhat, -1, keepdims=True) * inv
    return rs * (dx - m1 - xhat * m2)


def full(a):
    return pl.BlockSpec(a.shape, lambda *_: (0,) * a.ndim, pipeline_mode=pl.Buffered(1))


def sds(shape, dtype):
    return jax.ShapeDtypeStruct(shape, dtype)


def params(**kw):
    return pltpu.CompilerParams(vmem_limit_bytes=VMEM_LIMIT, **kw)


def vector(v_ref, row):
    return v_ref[row : row + 1, :]


VECTOR_ROWS = 16


def put_vectors(v_s, flat, blocked):
    width = v_s.shape[1]
    for row, ref in flat:
        for i in range(ref.shape[0] // width):
            v_s[row + i : row + i + 1, :] = ref[i * width : (i + 1) * width].reshape(1, width)
    for row, ref in blocked:
        _, blocks, n = ref.shape
        for p in range(2):
            for b in range(blocks):
                v_s[row + p : row + p + 1, b * n : (b + 1) * n] = ref[p, b : b + 1, :]


def up8(n):
    return -(-n // 8) * 8


def slab_sizes(index, modes, slab):
    sizes = [(index < KEPT // modes, slab)]
    if KEPT % modes:
        sizes.append((index == KEPT // modes, up8(2 * (KEPT % modes))))
    return sizes


def row_sizes(index, rows):
    sizes = [(index < LAT // rows, rows)]
    if LAT % rows:
        sizes.append((index == LAT // rows, LAT % rows))
    return sizes


def each_size(row_options, slab_options, fn):
    for row_ok, nr in row_options:
        for slab_ok, ns in slab_options:
            pl.when(row_ok & slab_ok)(functools.partial(fn, nr, ns))


def greet(shards, me, dp):
    barrier = pltpu.get_barrier_semaphore()

    def one(i, _):
        peer = lax.rem(me + i, shards)
        pl.semaphore_signal(barrier, inc=1, device_id=(dp, peer), device_id_type=MESH)
        return 0

    lax.fori_loop(1, shards, one, 0)
    pl.semaphore_wait(barrier, shards - 1)


def send(src, dst, send_sem, recv_sem, dp, peer):
    return pltpu.make_async_remote_copy(
        src_ref=src, dst_ref=dst, send_sem=send_sem, recv_sem=recv_sem,
        device_id=(dp, peer), device_id_type=MESH,
    )


def halving_plan(groups, shards, n, turn):
    dp_bits = [("dp", b) for b in range(groups.bit_length() - 1)]
    lat_bits = [("lat", b) for b in range(shards.bit_length() - 1)]
    middle = dp_bits[1:2] + lat_bits[:2]
    turn = turn % len(middle)
    order = dp_bits[:1] + middle[turn:] + middle[:turn] + dp_bits[2:] + lat_bits[2:]
    plan = []
    for axis, bit in order:
        halved = n % (2 * LOW_ROWS) == 0
        plan.append((axis, bit, n, halved))
        n = n // 2 if halved else n
    return plan, n


def halving_plans(groups, shards, sizes):
    return [
        (k, t * size // 3) + halving_plan(groups, shards, size // 3, t)
        for k, size in enumerate(sizes)
        for t in range(3)
    ]


def halving_walk(first, plan, dp, me):
    offsets, bits, peers = [first], [], []
    for axis, bit, n, halved in plan:
        index = dp if axis == "dp" else me
        b = lax.rem(index // 2**bit, 2)
        other = index + 2**bit * (1 - 2 * b)
        peers.append((other, me) if axis == "dp" else (dp, other))
        bits.append(b)
        offsets.append(offsets[-1] + b * (n // 2) if halved else offsets[-1])
    return offsets, bits, peers


def dp_halving_peers(groups, dp, me):
    bits = range(groups.bit_length() - 1)
    return [(dp + 2**bit * (1 - 2 * lax.rem(dp // 2**bit, 2)), me) for bit in bits]


def rows_at(start, n, unit=8):
    return pl.ds(pl.multiple_of(start, unit), n)


def low_rows_at(start, n):
    return rows_at(start, n, LOW_ROWS)


def signal_all(devices):
    barrier = pltpu.get_barrier_semaphore()
    for device in devices:
        pl.semaphore_signal(barrier, inc=1, device_id=device, device_id_type=MESH)
    pl.semaphore_wait(barrier, len(devices))


def received(plan):
    return sum(n // 2 if halved else n for _, _, n, halved in plan)


class Halving:
    def __init__(self, plans, accs, recvs, send_sems, recv_sems, dp, me):
        self.plans, self.accs, self.recvs = plans, accs, recvs
        self.send_sems, self.recv_sems = send_sems, recv_sems
        self.walks = [halving_walk(first, plan, dp, me) for _, first, plan, _ in plans]
        self.stages = len(plans[0][2])

    def base(self, j, stage):
        k, _, plan, _ = self.plans[j]
        before = sum(received(p) for which, _, p, _ in self.plans[:j] if which == k)
        return before + received(plan[:stage])

    def copy(self, j, stage):
        k = self.plans[j][0]
        _, _, n, halved = self.plans[j][2][stage]
        offsets, bits, peers = self.walks[j]
        count = n // 2 if halved else n
        start = offsets[stage] + (1 - bits[stage]) * count if halved else offsets[stage]
        return pltpu.make_async_remote_copy(
            src_ref=self.accs[k].at[low_rows_at(start, count)],
            dst_ref=self.recvs[k].at[pl.ds(self.base(j, stage), count)],
            send_sem=self.send_sems.at[j, stage], recv_sem=self.recv_sems.at[j, stage],
            device_id=peers[stage], device_id_type=MESH,
        )

    def start(self, stage):
        for j in range(len(self.plans)):
            self.copy(j, stage).start()

    def finish(self, stage):
        for j in range(len(self.plans)):
            self.copy(j, stage).wait()
            k = self.plans[j][0]
            _, _, n, halved = self.plans[j][2][stage]
            count = n // 2 if halved else n
            first = self.walks[j][0][stage + 1]
            base = self.base(j, stage)
            acc, recv = self.accs[k], self.recvs[k]
            most = 98304 // acc.shape[1]
            step = max(c for c in range(LOW_ROWS, most + 1, LOW_ROWS) if count % c == 0)

            def add(i, _):
                mine = low_rows_at(first + i * step, step)
                other = low_rows_at(base + i * step, step)
                acc[mine, :] = (acc[mine, :].astype(F32) + recv[other, :].astype(F32)).astype(BF16)
                return 0

            lax.fori_loop(0, count // step, add, 0)

    def tick(self, stage):
        self.finish(stage)
        if stage + 1 < self.stages:
            self.start(stage + 1)

    def keep(self, refs):
        at = [0] * len(refs)
        for j, (k, _, _, n) in enumerate(self.plans):
            refs[k][at[k] : at[k] + n, :] = self.accs[k][low_rows_at(self.walks[j][0][-1], n), :]
            at[k] += n


def strided(ref, start, count, stride):
    return jnp.concatenate([ref[t, pl.ds(start, count, stride=stride), :] for t in range(ref.shape[0])], 1)


def put_rows(ref, start, value):
    n = value.shape[0]
    for t in range(ref.shape[0]):
        ref[t, pl.ds(pl.multiple_of(start, 8), n), :] = value[:, t * LANES : (t + 1) * LANES]


def load_mode(wide_ref, m, slab, modes):
    re = strided(wide_ref, 2 * m, LAT_PAD, slab)
    im = strided(wide_ref, 2 * m + 1, LAT_PAD, slab)
    live = lax.axis_index("lat") * modes + m < KEPT
    value = jnp.concatenate([re, im], 0)
    return jnp.where(live, value, jnp.zeros_like(value)).astype(BF16)


def widen(recv_ref, wide_ref):
    shards, rows, slab, width = recv_ref.shape
    n = rows * slab

    def one(s, _):
        put_rows(wide_ref, s * n, recv_ref[s].astype(F32).reshape(n, width))
        return 0

    lax.fori_loop(0, shards, one, 0)
    if LAT % rows:
        first = LAT * slab
        last = (LAT // rows + 1) * n
        put_rows(wide_ref, first, jnp.zeros((last - first, width), F32))
    for s in range(-(-LAT // rows), shards):
        put_rows(wide_ref, s * n, jnp.zeros((n, width), F32))


def store_mode(out_s, m, value):
    put_rows(out_s, 2 * m * LAT_PAD, value)


def emit_slabs(out_s, out_ref):
    shards, rows, slab, _ = out_ref.shape

    def one(s, _):
        for r in range(rows):
            out_ref[s, r] = strided(out_s, s * rows + r, slab, LAT_PAD).astype(BF16)
        return 0

    lax.fori_loop(0, shards, one, 0)


def each_mode(modes, fn):
    few = next(n for n in (3, 2, 1) if modes % n == 0)

    def some(j, _):
        for u in range(few):
            fn(j * few + u)
        return 0

    lax.fori_loop(0, modes // few, some, 0)


def spread_blocks(w_ref, dense_s):
    _, blocks, n, _ = w_ref.shape
    dense_s[...] = jnp.zeros_like(dense_s)
    for p in range(2):
        for b in range(blocks):
            at = (p * blocks + b) * n
            dense_s[b * n : (b + 1) * n, at : at + n] = w_ref[p, b]


def pick_blocks(dense_ref, out_ref):
    _, blocks, n, lanes = out_ref.shape
    for p in range(2):
        for b in range(blocks):
            at = (p * blocks + b) * n
            block = dense_ref[b * n : (b + 1) * n, at : at + n]
            out_ref[p, b] = jnp.concatenate([block, jnp.zeros((n, lanes - n), F32)], 1)


def peers(shards, fn):
    def one(i, _):
        fn(i)
        return 0

    lax.fori_loop(1, shards, one, 0)


def emit_early(out_ref, early_s):
    rows = early_s.shape[1]
    for s in range(out_ref.shape[0]):
        early_s[s] = out_ref[s, :rows]


class Early:
    def __init__(self, src, dst, sems, rows, modes, slab, dp, me):
        self.src, self.dst, self.sems = src, dst, sems
        self.rows, self.modes, self.slab = rows, modes, slab
        self.dp, self.me, self.shards = dp, me, src.shape[0]

    def move(self, i, sender, receiver, act):
        count = self.src.shape[1]

        def piece(nr, ns):
            act(send(
                self.src.at[receiver, pl.ds(0, nr), pl.ds(0, ns)], self.dst.at[sender, pl.ds(0, nr), pl.ds(0, ns)],
                self.sems[0].at[i], self.sems[1].at[i], self.dp, receiver,
            ))

        live = row_sizes(receiver, count) if count == self.rows else [(receiver * self.rows < LAT, count)]
        each_size(live, slab_sizes(sender, self.modes, self.slab), piece)

    def own(self):
        return pltpu.make_async_copy(self.src.at[self.me], self.dst.at[self.me], self.sems[0].at[0])

    def start(self):
        self.own().start()
        peers(self.shards, lambda i: self.move(i, self.me, lax.rem(self.me + i, self.shards), lambda c: c.start()))

    def finish(self):
        self.own().wait()

        def one(i):
            self.move(i, self.me, lax.rem(self.me + i, self.shards), lambda c: c.wait_send())
            self.move(i, lax.rem(self.me + self.shards - i, self.shards), self.me, lambda c: c.wait_recv())

        peers(self.shards, one)


def spectral_forward_kernel(
    hops, x_ref, flt_ref, fa_ref, ia_ref, wi_ref, wo_ref, ng_ref, ns_ref, bi_ref, bo_ref,
    out_ref, freq_ref, hid_ref, gp_ref, t2_ref, early_ref,
    v_s, stage_s, recv_s, early_s, wide_s, out_s, wi_s, wo_s, go_send, go_recv, go_own, early_send, early_recv,
):
    g = pl.program_id(0)
    rows, lon, _ = x_ref.shape
    shards, _, slab, width = out_ref.shape
    modes = freq_ref.shape[0]
    h = LAT_PAD
    me = lax.axis_index("lat")
    dp = lax.axis_index("dp")
    early = Early(early_s, early_ref, (early_send, early_recv), rows, modes, slab, dp, me)

    hop = rows // hops

    def go(group, h, i, sender, receiver, act):
        def piece(nr, ns):
            part = (pl.ds(h * hop, nr), pl.ds(0, ns))
            act(send(
                stage_s.at[(group, receiver) + part], recv_s.at[(group, sender) + part],
                go_send.at[group, h, i], go_recv.at[group, h, i], dp, receiver,
            ))

        each_size([(sender * rows + h * hop < LAT, hop)], slab_sizes(receiver, modes, slab), piece)

    def own(group):
        return pltpu.make_async_copy(stage_s.at[group, me], recv_s.at[group, me], go_own.at[group])

    def to(i):
        return lax.rem(me + i, shards)

    def send_group(group, h):
        peers(shards, lambda i: go(group, h, i, me, to(i), lambda c: c.start()))

    @pl.when(g == 0)
    def _():
        def row(r, _):
            c, rs = center_scale(pad_rows(x_ref[r].astype(F32), COLS))
            first = (c * rs * vector(v_s, NORM_G) + vector(v_s, NORM_S)).astype(BF16)
            spec = dot(flt_ref[...], first).astype(BF16)
            for group in range(GROUPS):
                part = spec[:, group * width : (group + 1) * width]
                stage_s[group, :, r] = part.reshape(shards, slab, width)
            return 0

        put_vectors(v_s, ((NORM_G, ng_ref), (NORM_S, ns_ref)), ((INNER_B, bi_ref), (OUTER_B, bo_ref)))
        for h in range(hops):
            lax.fori_loop(h * hop, (h + 1) * hop, row, 0)
            if h == 0:
                greet(shards, me, dp)
            send_group(0, h)
        for group in range(GROUPS):
            own(group).start()
            if group:
                for h in range(hops):
                    send_group(group, h)

    spread_blocks(wi_ref, wi_s)
    spread_blocks(wo_ref, wo_s)
    if slab != 2 * modes:
        out_s[...] = jnp.zeros_like(out_s)
    for group in range(GROUPS):

        @pl.when(g == group)
        def _():
            own(group).wait()
            for h in range(hops):
                peers(shards, lambda i: go(group, h, i, lax.rem(me + shards - i, shards), me, lambda c: c.wait_recv()))
            widen(recv_s.at[group], wide_s)

    def mix(v, w_ref, bias):
        a = dot(v, w_ref[...])
        lanes = pl.ds(pl.multiple_of(g * width, LANES), width)
        re = a[:h, :width] - a[h:, width:] + v_s[bias : bias + 1, lanes]
        im = a[h:, :width] + a[:h, width:] + v_s[bias + 1 : bias + 2, lanes]
        return jnp.concatenate([re, im], 0)

    def one(m):
        fq = dot(fa_ref[...], load_mode(wide_s, m, slab, modes)).astype(BF16)
        freq_ref[m] = fq
        hid, gp = gelu_both(mix(fq, wi_s, INNER_B))
        hid = hid.astype(BF16)
        hid_ref[m] = hid
        gp_ref[m] = gp
        outer = mix(hid, wo_s, OUTER_B)
        t = jnp.tanh(outer * (1.0 / SHRINK))
        t2_ref[m] = t * t
        shrunk = (outer - SHRINK * t).astype(BF16)
        store_mode(out_s, m, dot(ia_ref[...], shrunk))

    each_mode(modes, one)
    emit_slabs(out_s, out_ref)

    @pl.when(g == 0)
    def _():
        emit_early(out_ref, early_s)
        early.start()

    @pl.when(g == GROUPS - 1)
    def _():
        early.finish()
        for group in range(GROUPS):
            for h in range(hops):
                peers(shards, lambda i: go(group, h, i, me, to(i), lambda c: c.wait_send()))


def group_specs(shards, rows, slab, modes, part):
    n = 2 * LAT_PAD
    slabs = pl.BlockSpec((shards, rows, slab, part), lambda g: (0, 0, 0, g))
    spec = pl.BlockSpec((modes, n, part), lambda g: (0, 0, g))
    pair = pl.BlockSpec((2, part), lambda g: (0, g))
    return slabs, spec, pair


def weight_spec(weight, lanes=None):
    _, blocks, n, _ = weight.shape
    return pl.BlockSpec((2, blocks // GROUPS, n, lanes or n), lambda g: (0, g, 0, 0))


def hops_of(rows):
    return 2 if rows % 4 == 0 else 1


def spectral_forward(x, tb, wi, wo, vectors, shards, slab, modes, collective_id):
    rows, lon, width = x.shape
    part = width // GROUPS
    n = 2 * LAT_PAD
    slabs, spec, _ = group_specs(shards, rows, slab, modes, part)
    hops = hops_of(rows)
    dma = pltpu.SemaphoreType.DMA
    early = (shards, rows // hops, slab, part)
    return pl.pallas_call(
        functools.partial(spectral_forward_kernel, hops),
        grid=(GROUPS,),
        in_specs=[full(x), full(tb["flt"]), full(tb["fa"]), full(tb["ia"]), weight_spec(wi), weight_spec(wo)]
        + [full(v) for v in vectors],
        out_specs=[slabs, spec, spec, spec, spec, pl.BlockSpec(memory_space=pl.ANY)],
        out_shape=[
            sds((shards, rows, slab, width), BF16),
            sds((modes, n, width), BF16),
            sds((modes, n, width), BF16),
            sds((modes, n, width), F32),
            sds((modes, n, width), F32),
            sds(early, BF16),
        ],
        scratch_shapes=[
            pltpu.VMEM((VECTOR_ROWS, width), F32),
            pltpu.VMEM((GROUPS, shards, rows, slab, part), BF16),
            pltpu.VMEM((GROUPS, shards, rows, slab, part), BF16),
            pltpu.VMEM(early, BF16),
            pltpu.VMEM((part // LANES, shards * rows * slab, LANES), F32),
            pltpu.VMEM((part // LANES, slab * LAT_PAD, LANES), F32),
            pltpu.VMEM((part, 2 * part), BF16),
            pltpu.VMEM((part, 2 * part), BF16),
            dma((GROUPS, hops, shards)), dma((GROUPS, hops, shards)), dma((GROUPS,)), dma((shards,)), dma((shards,)),
        ],
        compiler_params=params(collective_id=collective_id, has_side_effects=True),
        name="spectral_forward",
    )(x, tb["flt"], tb["fa"], tb["ia"], wi, wo, *vectors)


def spectral_backward_kernel(
    groups, plans, recv_ref, iat_ref, fat_ref, wo_ref, wi_ref, freq_ref, hid_ref, gp_ref, t2_ref, dw1_ref, dw2_ref,
    out_ref, dwo_ref, dbo_ref, dwi_ref, dbi_ref, part1_ref, part2_ref, early_ref,
    wide_s, out_s, wo_s, wi_s, dwo_s, dwi_s, acc1_s, acc2_s, recv1_s, recv2_s, early_s,
    load_sem, send_sems, recv_sems, early_send, early_recv,
):
    shards = recv_ref.shape[0]
    slab, width = recv_ref.shape[2:]
    modes = freq_ref.shape[0]
    h = LAT_PAD
    g = pl.program_id(0)
    me = lax.axis_index("lat")
    dp = lax.axis_index("dp")
    early = Early(early_s, early_ref, (early_send, early_recv), early_s.shape[1], modes, slab, dp, me)
    halving = Halving(plans, (acc1_s, acc2_s), (recv1_s, recv2_s), send_sems, recv_sems, dp, me)
    loads = [
        pltpu.make_async_copy(dw1_ref, acc1_s, load_sem.at[0]),
        pltpu.make_async_copy(dw2_ref, acc2_s, load_sem.at[1]),
    ]

    @pl.when(g == 0)
    def _():
        for copy in loads:
            copy.start()
        lat_peers = [(dp, lax.rem(me + i, shards)) for i in range(1, shards)]
        signal_all(lat_peers + [peer for peer in dp_halving_peers(groups, dp, me)])
        for copy in loads:
            copy.wait()
        halving.start(0)

    whole = GROUPS * modes
    when_due = [whole * n // 8 // 3 * 3 for n in (1, 4, 6, 7)]

    widen(recv_ref, wide_s)
    spread_blocks(wo_ref, wo_s)
    spread_blocks(wi_ref, wi_s)
    if slab != 2 * modes:
        out_s[...] = jnp.zeros_like(out_s)
    for ref in (dwo_s, dbo_ref, dwi_s, dbi_ref):
        ref[...] = jnp.zeros_like(ref)

    def lowered(grad):
        return grad[:h].astype(BF16), grad[h:].astype(BF16)

    def grads(ref, first, lows, dw_ref, db_ref):
        value = ref[pl.ds(first, len(lows))].reshape(len(lows) * 2 * h, width)
        both = [jnp.concatenate(low, 0) for low in lows]
        turned = [jnp.concatenate([im, -re], 0) for re, im in lows]
        grad = jnp.concatenate([jnp.concatenate(both, 0), jnp.concatenate(turned, 0)], 1)
        dw_ref[...] += dot_tn(value, grad)
        for part in range(2):
            total = sum(jnp.sum(low[part].astype(F32), 0, keepdims=True) for low in lows)
            db_ref[part : part + 1] += total
        return both

    def pull(v, w_ref):
        a = dot_nt(v, w_ref[:, :width])
        b = dot_nt(v, w_ref[:, width:])
        return jnp.concatenate([a[:h] + b[h:], a[h:] - b[:h]], 0)

    few = next(n for n in (3, 2, 1) if modes % n == 0)

    def some(j, _):
        first = j * few
        for stage, when in enumerate(when_due):
            pl.when(g * modes + first == when)(functools.partial(halving.tick, stage))
        lows = []
        for u in range(few):
            m = first + u
            merged = dot(iat_ref[...], load_mode(wide_s, m, slab, modes))
            lows.append(lowered(merged * t2_ref[m]))
        outer_grads = grads(hid_ref, first, lows, dwo_s, dbo_ref)
        lows = [lowered(pull(og, wo_s) * gp_ref[first + u]) for u, og in enumerate(outer_grads)]
        inner_grads = grads(freq_ref, first, lows, dwi_s, dbi_ref)
        for u, ig in enumerate(inner_grads):
            store_mode(out_s, first + u, dot(fat_ref[...], pull(ig, wi_s).astype(BF16)))
        return 0

    lax.fori_loop(0, modes // few, some, 0)
    pick_blocks(dwo_s, dwo_ref)
    pick_blocks(dwi_s, dwi_ref)
    emit_slabs(out_s, out_ref)

    @pl.when(g == 0)
    def _():
        emit_early(out_ref, early_s)
        early.start()

    @pl.when(g == GROUPS - 1)
    def _():
        for stage in range(len(when_due), halving.stages):
            halving.tick(stage)
        halving.keep((part1_ref, part2_ref))
        early.finish()


def spectral_backward(recv, tb, wo, wi, freq, hid, gp, t2, dw1, dw2, groups, plans, collective_id):
    shards, rows, slab, width = recv.shape
    modes = freq.shape[0]
    part = width // GROUPS
    slabs, spec, pair = group_specs(shards, rows, slab, modes, part)
    dw = sds(wo.shape[:3] + (LANES,), F32)
    grad = weight_spec(wo, LANES)
    db = sds((2, width), F32)
    any_ = pl.BlockSpec(memory_space=pl.ANY)
    whole = lambda n, w: pl.BlockSpec((n, w), lambda g: (0, 0))
    n1, n2 = (sum(n for k, _, _, n in plans if k == which) for which in range(2))
    stages = len(plans[0][2])
    dma = pltpu.SemaphoreType.DMA
    return pl.pallas_call(
        functools.partial(spectral_backward_kernel, groups, plans),
        grid=(GROUPS,),
        in_specs=[slabs, full(tb["iat"]), full(tb["fat"]), weight_spec(wo), weight_spec(wi), spec, spec, spec, spec]
        + [any_, any_],
        out_specs=[slabs, grad, pair, grad, pair, whole(n1, dw1.shape[1]), whole(n2, dw2.shape[1]), any_],
        out_shape=[
            sds(recv.shape, BF16), dw, db, dw, db,
            sds((n1, dw1.shape[1]), BF16), sds((n2, dw2.shape[1]), BF16),
            sds((shards, rows, slab, part), BF16),
        ],
        scratch_shapes=[
            pltpu.VMEM((part // LANES, shards * rows * slab, LANES), F32),
            pltpu.VMEM((part // LANES, slab * LAT_PAD, LANES), F32),
            pltpu.VMEM((part, 2 * part), BF16),
            pltpu.VMEM((part, 2 * part), BF16),
            pltpu.VMEM((part, 2 * part), F32),
            pltpu.VMEM((part, 2 * part), F32),
            pltpu.VMEM(dw1.shape, BF16),
            pltpu.VMEM(dw2.shape, BF16),
            pltpu.VMEM((sum(received(p) for k, _, p, _ in plans if k == 0), dw1.shape[1]), BF16),
            pltpu.VMEM((sum(received(p) for k, _, p, _ in plans if k == 1), dw2.shape[1]), BF16),
            pltpu.VMEM((shards, rows, slab, part), BF16),
            dma((2,)), dma((len(plans), stages)), dma((len(plans), stages)), dma((shards,)), dma((shards,)),
        ],
        compiler_params=params(collective_id=collective_id, has_side_effects=True),
        name="spectral_backward",
    )(recv, tb["iat"], tb["fat"], wo, wi, freq, hid, gp, t2, dw1, dw2)


def gather_row(r_ref, row, modes):
    shards, _, slab, width = r_ref.shape
    whole = KEPT // modes
    parts = [r_ref[:whole, row].astype(F32).reshape(whole * slab, width)]
    rest = (shards - whole) * slab
    if KEPT % modes:
        n = up8(2 * (KEPT % modes))
        parts.append(r_ref[whole, row].astype(F32)[:n])
        rest -= n
    if rest:
        parts.append(jnp.zeros((rest, width), F32))
    return jnp.concatenate(parts, 0).astype(BF16)


def feed_kernel(
    per, chunk, hops, modes, scale_ref, x_ref, c_ref, back_ref, early_ref, il_ref, ilt_ref, w1_ref, w2_ref,
    ng_ref, ns_ref, pg_ref, ps_ref, rb_ref, eb_ref,
    lo_ref, mg_ref, out_ref, dw1_ref, dw2_ref, deb_ref, drb_ref, dpg_ref, dps_ref,
    v_ref, slab_s, w1_s, w2_s, act_s, pre_s, sec_s, sect_s, up_s, mixed_s, xhat_s, rs_s, branch_s, grad_s,
    w_sem, dw_sem, early_sem, in_send, in_recv, in_own, out_send, out_recv, out_own,
):
    g = pl.program_id(0)
    steps = pl.num_programs(0)
    lon, width = x_ref.shape[1:]
    hidden = w1_s.shape[1]
    shards, rows, slab, _ = slab_s.shape
    hop = rows // hops
    every = steps // hops
    tall = per * COLS
    me = lax.axis_index("lat")
    dp = lax.axis_index("dp")

    def transfer(src, dst, sems, h, lanes, i, sender, receiver, row_owner, mode_owner, act):
        part = pl.ds(h * hop, hop)

        def piece(nr, ns):
            act(send(
                src.at[receiver, part, pl.ds(0, ns), lanes], dst.at[sender, part, pl.ds(0, ns), lanes],
                sems[0].at[h, i], sems[1].at[h, i], dp, receiver,
            ))

        live = row_owner * rows + h * hop < LAT
        each_size([(live, hop)], slab_sizes(mode_owner, modes, slab), piece)

    known = early_ref.shape[3]

    def fresh(h):
        return pl.ds(known, width - known) if h == 0 else pl.ds(0, width)

    def incoming(h, i, sender, receiver, act):
        transfer(
            back_ref, slab_s, (in_send, in_recv), h, fresh(h), i, sender, receiver, receiver, sender, act
        )

    def outgoing(h, i, sender, receiver, act):
        transfer(
            slab_s, out_ref, (out_send, out_recv), h, pl.ds(0, width), i, sender, receiver, sender, receiver, act
        )

    def own_in(h):
        part = pl.ds(h * hop, hop)
        return pltpu.make_async_copy(
            back_ref.at[me, part, :, fresh(h)], slab_s.at[me, part, :, fresh(h)], in_own.at[h]
        )

    early = pltpu.make_async_copy(early_ref, slab_s.at[:, pl.ds(0, hop), :, pl.ds(0, known)], early_sem)

    def own_out(h):
        part = pl.ds(h * hop, hop)
        return pltpu.make_async_copy(slab_s.at[me, part], out_ref.at[me, part], out_own.at[h])

    def to(i):
        return lax.rem(me + i, shards)

    def source(i):
        return lax.rem(me + shards - i, shards)

    def fetch(h):
        own_in(h).start()
        peers(shards, lambda i: incoming(h, i, me, to(i), lambda c: c.start()))

    weights = [
        pltpu.make_async_copy(w1_ref, w1_s, w_sem.at[0]),
        pltpu.make_async_copy(w2_ref, w2_s, w_sem.at[1]),
    ]

    @pl.when(g == 0)
    def _():
        for copy in weights:
            copy.start()
        early.start()
        greet(shards, me, dp)
        fetch(0)
        put_vectors(
            v_ref,
            (
                (NORM_G, ng_ref), (NORM_S, ns_ref), (POST_G, pg_ref), (POST_S, ps_ref), (REDUCE_B, rb_ref),
                (EXPAND_B, eb_ref),
            ),
            (),
        )
        for ref in (deb_ref, drb_ref, dpg_ref, dps_ref):
            ref[...] = jnp.zeros_like(ref)

    for h in range(hops):

        @pl.when(g == h * every)
        def _():
            if h == 0:
                early.wait()
            own_in(h).wait()
            peers(shards, lambda i: incoming(h, i, source(i), me, lambda c: c.wait_recv()))
            if h + 1 < hops:
                fetch(h + 1)

    at = pl.ds(0 if rows == per else pl.multiple_of(g * tall, tall), tall)
    for i in range(per):
        rows_i = pl.ds(i * COLS, COLS)
        x = pad_rows(x_ref[i].astype(F32), COLS)
        c, rs = center_scale(x)
        first = c * rs * vector(v_ref, NORM_G) + vector(v_ref, NORM_S)
        filtered = dot(il_ref[...], gather_row(slab_s, g * per + i, modes))
        live = me * rows + g * per + i < LAT
        mixed = jnp.where(live, filtered, jnp.zeros_like(filtered)) + first + x
        c, rs = center_scale(mixed)
        xhat = c * rs
        mixed_s[rows_i, :] = mixed
        xhat_s[rows_i, :] = xhat
        rs_s[rows_i, :] = jnp.broadcast_to(rs, (COLS, LANES))
        sec_s[rows_i, :] = (xhat * vector(v_ref, POST_G) + vector(v_ref, POST_S)).astype(BF16)
        up = (pad_rows(c_ref[i].astype(F32), COLS) * scale_ref[0, g * per + i]).astype(BF16)
        up_s[pl.ds(pl.multiple_of(g * tall + i * COLS, COLS), COLS), :] = up
        drb_ref[...] += jnp.sum(up.astype(F32), 0, keepdims=True)
    sect_s[:, at] = sec_s[...].T
    branch_s[...] = jnp.broadcast_to(vector(v_ref, REDUCE_B), branch_s.shape)
    grad_s[...] = jnp.zeros_like(grad_s)

    @pl.when(g == 0)
    def _():
        for copy in weights:
            copy.wait()

    def hidden_chunk(j, _):
        ds = pl.ds(pl.multiple_of(j * chunk, chunk), chunk)
        act, slope = gelu_both(dot(sec_s[...], w1_s[:, ds]) + v_ref[pl.ds(EXPAND_B + j, 1), :])
        act = act.astype(BF16)
        act_s[at, ds] = act
        pre = (dot_nt(up_s[at, :], w2_s[ds, :]) * slope).astype(BF16)
        pre_s[at, ds] = pre
        deb_ref[pl.ds(j, 1), :] += jnp.sum(pre.astype(F32), 0, keepdims=True)
        branch_s[...] += dot(act, w2_s[ds, :])
        grad_s[...] += dot_nt(pre, w1_s[:, ds])
        return 0

    lax.fori_loop(0, hidden // chunk, hidden_chunk, 0)
    for i in range(per):
        rows_i = pl.ds(i * COLS, COLS)
        grad = grad_s[rows_i, :]
        xhat = xhat_s[rows_i, :]
        up = pad_rows(c_ref[i].astype(F32), COLS) * scale_ref[0, g * per + i]
        mg = up + norm_back(grad, xhat, rs_s[rows_i, 0:1], vector(v_ref, POST_G))
        mg_ref[i] = mg[:lon]
        rg = dot(ilt_ref[...], mg.astype(BF16)).astype(BF16)
        slab_s[:, g * per + i] = rg.reshape(shards, slab, width)

    @pl.when(lax.rem(g, every) == every - 1)
    def _():
        h = g // every
        own_out(h).start()
        peers(shards, lambda i: outgoing(h, i, me, to(i), lambda c: c.start()))

    for i in range(per):
        rows_i = pl.ds(i * COLS, COLS)
        keep = scale_ref[1, g * per + i]
        lo_ref[i] = ((mixed_s[rows_i, :] + branch_s[rows_i, :]) * keep).astype(BF16)[:lon]
        grad = grad_s[rows_i, :]
        dpg_ref[...] += jnp.sum(grad * xhat_s[rows_i, :], 0, keepdims=True)
        dps_ref[...] += jnp.sum(grad, 0, keepdims=True)

    def gradients(j):
        ds = pl.ds(pl.multiple_of(j * chunk, chunk), chunk)
        side = dw1_ref.shape[1] // chunk
        place = (
            pl.ds(pl.multiple_of(j // side * width, width), width),
            pl.ds(pl.multiple_of(lax.rem(j, side) * chunk, chunk), chunk),
        )
        return (
            pltpu.make_async_copy(w1_s.at[:, ds], dw1_ref.at[place], dw_sem.at[0, j]),
            pltpu.make_async_copy(w2_s.at[ds, :], dw2_ref.at[ds, :], dw_sem.at[1, j]),
        )

    @pl.when(g == steps - 1)
    def _():
        def weight_chunk(j, _):
            ds = pl.ds(pl.multiple_of(j * chunk, chunk), chunk)
            w1_s[:, ds] = dot(sect_s[...], pre_s[:, ds]).astype(BF16)
            w2_s[ds, :] = dot_tn(act_s[:, ds], up_s[...]).astype(BF16)
            for copy in gradients(j):
                copy.start()
            return 0

        lax.fori_loop(0, hidden // chunk, weight_chunk, 0)

        for h in range(hops):
            own_out(h).wait()

            def wait_all(i):
                incoming(h, i, me, to(i), lambda c: c.wait_send())
                outgoing(h, i, me, to(i), lambda c: c.wait_send())
                outgoing(h, i, source(i), me, lambda c: c.wait_recv())

            peers(shards, wait_all)

        def finish(j, _):
            for copy in gradients(j):
                copy.wait()
            return 0

        lax.fori_loop(0, hidden // chunk, finish, 0)


def feed(scale, x, cot, back, early, tb, w1, w2, vectors, modes, collective_id):
    rows, lon, width = x.shape
    hidden = w1.shape[1]
    shards, _, slab, _ = back.shape
    per = next(n for n in (2, 3, 1) if rows % n == 0)
    steps = rows // per
    hops = hops_of(rows)
    chunk = width
    row = pl.BlockSpec((per, lon, width), lambda g: (g, 0, 0))
    any_ = pl.BlockSpec(memory_space=pl.ANY)
    vec = lambda n: pl.BlockSpec((n, width), lambda g: (0, 0))
    tall = per * COLS
    total = rows * COLS
    dma = pltpu.SemaphoreType.DMA
    return pl.pallas_call(
        functools.partial(feed_kernel, per, chunk, hops, modes),
        grid=(steps,),
        in_specs=[
            pl.BlockSpec(memory_space=pltpu.SMEM), row, row, any_, any_, full(tb["il"]), full(tb["ilt"]), any_, any_,
        ]
        + [full(v) for v in vectors],
        out_specs=[row, row, any_, any_, any_, vec(hidden // width), vec(1), vec(1), vec(1)],
        out_shape=[
            sds((rows, lon, width), BF16),
            sds((rows, lon, width), F32),
            sds(back.shape, BF16),
            sds((2 * width, hidden // 2), BF16),
            sds(w2.shape, BF16),
            sds((hidden // width, width), F32),
            sds((1, width), F32),
            sds((1, width), F32),
            sds((1, width), F32),
        ],
        scratch_shapes=[
            pltpu.VMEM((VECTOR_ROWS, width), F32),
            pltpu.VMEM(back.shape, BF16),
            pltpu.VMEM(w1.shape, BF16),
            pltpu.VMEM(w2.shape, BF16),
            pltpu.VMEM((total, hidden), BF16),
            pltpu.VMEM((total, hidden), BF16),
            pltpu.VMEM((tall, width), BF16),
            pltpu.VMEM((width, total), BF16),
            pltpu.VMEM((total, width), BF16),
            pltpu.VMEM((tall, width), F32),
            pltpu.VMEM((tall, width), F32),
            pltpu.VMEM((tall, LANES), F32),
            pltpu.VMEM((tall, width), F32),
            pltpu.VMEM((tall, width), F32),
            dma((2,)), dma((2, hidden // chunk)), dma,
            dma((hops, shards)), dma((hops, shards)), dma((hops,)),
            dma((hops, shards)), dma((hops, shards)), dma((hops,)),
        ],
        compiler_params=pltpu.CompilerParams(
            vmem_limit_bytes=63 * 2**20, collective_id=collective_id, has_side_effects=True
        ),
        name="feed",
    )(scale, x, cot, back, early, tb["il"], tb["ilt"], w1, w2, *vectors)


def leave_kernel(
    groups, hops, modes, plans, x_ref, back_ref, early_ref, mg_ref, fl_ref, ng_ref, *refs,
):
    weight_refs, line_refs, refs = refs[:2], refs[2:8], refs[8:]
    (
        part1_ref, part2_ref, out_ref, sum1_ref, sum2_ref, sums_ref, norm_ref, dw1_ref, dw2_ref,
        v_ref, slab_s, line_s, mine_s, from_dp, part_s, from_lat, all_s, norm_lat, norm_dp,
        in_send, in_recv, in_own, early_sem, wide_send, wide_recv, own_sem, small_sems,
    ) = refs
    g = pl.program_id(0)
    steps = pl.num_programs(0)
    lon = x_ref.shape[1]
    shards, rows, slab, _ = slab_s.shape
    n = from_lat.shape[1]
    hop = rows // hops
    me = lax.axis_index("lat")
    dp = lax.axis_index("dp")
    lat_peers = [lax.rem(me + i, shards) for i in range(1, shards)]
    dp_peers = [lax.rem(dp + i, groups) for i in range(1, groups)]

    known = early_ref.shape[3]
    fresh = pl.ds(known, slab_s.shape[3] - known)
    early = pltpu.make_async_copy(early_ref, slab_s.at[:, :, :, pl.ds(0, known)], early_sem)

    def incoming(h, i, sender, receiver, act):
        part = pl.ds(h * hop, hop)

        def piece(nr, ns):
            act(send(
                back_ref.at[receiver, part, pl.ds(0, ns), fresh], slab_s.at[sender, part, pl.ds(0, ns), fresh],
                in_send.at[h, i], in_recv.at[h, i], dp, receiver,
            ))

        live = receiver * rows + h * hop < LAT
        each_size([(live, hop)], slab_sizes(sender, modes, slab), piece)

    def own_in(h):
        part = pl.ds(h * hop, hop)
        return pltpu.make_async_copy(back_ref.at[me, part, :, fresh], slab_s.at[me, part, :, fresh], in_own.at[h])

    def fetch(h):
        own_in(h).start()
        peers(shards, lambda i: incoming(h, i, me, lax.rem(me + i, shards), lambda c: c.start()))

    def arrived(h):
        own_in(h).wait()
        peers(shards, lambda i: incoming(h, i, lax.rem(me + shards - i, shards), me, lambda c: c.wait_recv()))

    walks = [halving_walk(first, plan, dp, me) for _, first, plan, _ in plans]
    outs = (dw1_ref, dw2_ref)
    parts = (part1_ref, part2_ref)
    stages = len(plans[0][2])
    count = len(plans)

    def part(j):
        k, _, _, n = plans[j]
        at = sum(rest for which, _, _, rest in plans[:j] if which == k)
        return parts[k].at[pl.ds(at, n)]

    def own_part(j):
        k, _, _, n = plans[j]
        return pltpu.make_async_copy(part(j), outs[k].at[low_rows_at(walks[j][0][-1], n)], own_sem.at[j])

    def spread(j, stage):
        k, _, plan, _ = plans[j]
        _, _, n, halved = plan[stage]
        if not halved:
            return None
        where = low_rows_at(walks[j][0][stage + 1], n // 2)
        first = not any(later[3] for later in plan[stage + 1 :])
        return pltpu.make_async_remote_copy(
            src_ref=part(j) if first else outs[k].at[where], dst_ref=outs[k].at[where],
            send_sem=wide_send.at[j, stage], recv_sem=wide_recv.at[j, stage],
            device_id=walks[j][2][stage], device_id_type=MESH,
        )

    def spread_all(stage, act):
        for j in range(count):
            copy = spread(j, stage)
            if copy is not None:
                act(copy)

    def tick(i):
        stage = stages - 1 - i
        spread_all(stage, lambda c: c.wait())
        if i == 0:
            for j in range(count):
                own_part(j).wait()
        if stage:
            spread_all(stage - 1, lambda c: c.start())


    def remote(src, dst, stage, i, to):
        return pltpu.make_async_remote_copy(
            src_ref=src, dst_ref=dst, send_sem=small_sems.at[stage, 0, i], recv_sem=small_sems.at[stage, 1, i],
            device_id=to, device_id_type=MESH,
        )

    def over(peers_, axis):
        return [(i, p, (p, me) if axis == "dp" else (dp, p)) for i, p in enumerate(peers_)]

    block = shards * n
    mine = low_rows_at((dp * shards + me) * n, n)
    mine_dp = low_rows_at(dp * block, block)
    tiles = line_s.shape[1] // LANES

    def small(stage):
        if stage == 0:
            return [
                remote(mine_s.at[low_rows_at(p * block, block)], from_dp.at[i], 0, i, to)
                for i, p, to in over(dp_peers, "dp")
            ]
        if stage == 1:
            return [
                remote(part_s.at[low_rows_at(p * n, n)], from_lat.at[i], 1, i, to)
                for i, p, to in over(lat_peers, "lat")
            ]
        if stage == 2:
            return [remote(all_s.at[mine], all_s.at[mine], 2, i, to) for i, p, to in over(lat_peers, "lat")]
        if stage == 3:
            return [remote(all_s.at[mine_dp], all_s.at[mine_dp], 3, i, to) for i, p, to in over(dp_peers, "dp")]
        if stage == 4:
            return [remote(norm_lat.at[me], norm_lat.at[me], 4, i, to) for i, p, to in over(lat_peers, "lat")]
        return [remote(norm_dp.at[dp], norm_dp.at[dp], 5, i, to) for i, p, to in over(dp_peers, "dp")]

    def begin(stage):
        for copy in small(stage):
            copy.start()

    def end(stage):
        for copy in small(stage):
            copy.wait()
        if stage == 0:
            whole = mine_s[mine_dp, :].astype(F32) + jnp.sum(from_dp[...].astype(F32), 0)
            part_s[...] = whole.astype(BF16)
        if stage == 1:
            whole = part_s[low_rows_at(me * n, n), :].astype(F32) + jnp.sum(from_lat[...].astype(F32), 0)
            all_s[mine, :] = whole.astype(BF16)

    def small_tick(stage):
        end(stage)
        begin(stage + 1)

    @pl.when(g == 0)
    def _():
        early.start()
        for j in range(count):
            own_part(j).start()
        signal_all([(dp, p) for p in lat_peers] + [(p, me) for p in dp_peers])
        spread_all(stages - 1, lambda c: c.start())
        fetch(0)
        put_vectors(v_ref, ((NORM_G, ng_ref),), ())
        at = 0
        for ref in weight_refs:
            value = ref[...].reshape(-1, LANES)
            mine_s[at : at + value.shape[0], :] = value.astype(BF16)
            at += value.shape[0]
        lines = [
            ref[row : row + 1, t * LANES : (t + 1) * LANES]
            for ref in line_refs
            for row in range(ref.shape[0])
            for t in range(tiles)
        ]
        lines.append(jnp.zeros((mine_s.shape[0] - at - len(lines), LANES), F32))
        mine_s[at:, :] = jnp.concatenate(lines, 0).astype(BF16)
        begin(0)
        line_s[...] = jnp.zeros_like(line_s)
        tick(0)
        small_tick(0)
        early.wait()
        arrived(0)
        tick(1)
        small_tick(1)
        if hops > 1:
            fetch(1)

    for h in range(1, hops):
        pl.when(g == h * hop)(functools.partial(arrived, h))

    x = pad_rows(x_ref[0].astype(F32), COLS)
    c, rs = center_scale(x)
    xhat = c * rs
    mg = pad_rows(mg_ref[0], COLS)
    live = me * rows + g < LAT
    spectrum = dot(fl_ref[...], gather_row(slab_s, g, modes))
    grad = jnp.where(live, spectrum, jnp.zeros_like(spectrum)) + mg
    line_s[0:1] += jnp.sum(grad * xhat, 0, keepdims=True)
    line_s[1:2] += jnp.sum(grad, 0, keepdims=True)
    out_ref[...] = (mg + norm_back(grad, xhat, rs, vector(v_ref, NORM_G)))[:lon].reshape(out_ref.shape)

    @pl.when(g == hop - 1)
    def _():
        tick(2)
        small_tick(2)

    @pl.when(g == steps - 1)
    def _():
        norm_lat[me] = line_s[...]
        begin(4)
        for i in range(3, stages):
            tick(i)
        end(4)
        norm_dp[dp] = jnp.sum(norm_lat[...], 0)
        begin(5)
        end(3)
        at = 0
        for ref in (sum1_ref, sum2_ref):
            size = ref.shape[0] * ref.shape[1] * ref.shape[2]
            value = all_s[at : at + size, :].astype(F32)
            ref[...] = value.reshape(ref.shape[:3] + (LANES,))[..., : ref.shape[3]]
            at += size
        sums_ref[...] = all_s[at : at + sums_ref.shape[0], :].astype(F32)
        for h in range(hops):
            peers(shards, lambda i: incoming(h, i, me, lax.rem(me + i, shards), lambda c: c.wait_send()))
        end(5)
        norm_ref[...] = jnp.sum(norm_dp[...], 0)


def leave(x, back, early, mg, fl, gain, small, part1, part2, shapes, block, groups, plans, modes, collective_id):
    rows, lon, width = x.shape
    shards, _, slab, _ = back.shape
    hops = hops_of(rows)
    stages = len(plans[0][2])
    unit = LOW_ROWS * groups * shards
    total = -(-sum(v.size // LANES for v in small) // unit) * unit
    n = total // (groups * shards)
    lines = up8(sum(v.size // LANES for v in small[2:]))
    row = pl.BlockSpec((1, lon, width), lambda r: (r, 0, 0))
    any_ = pl.BlockSpec(memory_space=pl.ANY)
    whole = lambda *shape: pl.BlockSpec(shape, lambda r: (0,) * len(shape))
    dma = pltpu.SemaphoreType.DMA
    return pl.pallas_call(
        functools.partial(leave_kernel, groups, hops, modes, plans),
        grid=(rows,),
        in_specs=[row, any_, any_, row, full(fl), full(gain)] + [full(v) for v in small] + [any_, any_],
        out_specs=[pl.BlockSpec((lon, 1, width), lambda r: (r, 0, 0)), whole(*block), whole(*block), whole(lines, LANES), whole(2, width), any_, any_],
        out_shape=[sds((rows * lon, 1, width), F32), sds(block, F32), sds(block, F32)]
        + [sds((lines, LANES), F32), sds((2, width), F32)]
        + [sds(shape, BF16) for shape in shapes],
        scratch_shapes=[
            pltpu.VMEM((VECTOR_ROWS, width), F32),
            pltpu.VMEM(back.shape, BF16),
            pltpu.VMEM((2, width), F32),
            pltpu.VMEM((total, LANES), BF16),
            pltpu.VMEM((groups - 1, shards * n, LANES), BF16),
            pltpu.VMEM((shards * n, LANES), BF16),
            pltpu.VMEM((shards - 1, n, LANES), BF16),
            pltpu.VMEM((total, LANES), BF16),
            pltpu.VMEM((shards, 2, width), F32),
            pltpu.VMEM((groups, 2, width), F32),
            dma((hops, shards)), dma((hops, shards)), dma((hops,)), dma,
            dma((len(plans), stages)), dma((len(plans), stages)), dma((len(plans),)),
            dma((6, 2, max(groups, shards) - 1)),
        ],
        compiler_params=params(collective_id=collective_id, has_side_effects=True),
        name="leave",
    )(x, back, early, mg, fl, gain, *small, part1, part2)


def shards_fn(
    groups, shards, inputs, cotangent, storm_weight, norm_gain, norm_shift, inner_weight, inner_bias,
    outer_weight, outer_bias, post_gain, post_shift, expand_weight, expand_bias, reduce_weight, reduce_bias,
):
    _, rows, lon, width = inputs.shape
    modes = LON_PAD // shards
    slab = slab_rows(modes)
    tb = make_tables(shards, modes)
    row_ids = lax.axis_index("lat") * rows + jnp.arange(rows, dtype=jnp.int32)
    keep = (row_ids < LAT).astype(F32)
    scale = jnp.stack([keep * (storm_weight[0].astype(F32) / 64.0), keep])
    x = inputs[0]
    cot = cotangent[0]
    back, freq, hid, gp, t2, early = spectral_forward(
        x, tb, inner_weight, outer_weight, (norm_gain, norm_shift, inner_bias, outer_bias), shards, slab, modes, 0
    )
    (layer_out, mixed_grad, mode_grad, dw1, dw2, deb, drb, dpg, dps) = feed(
        scale, x, cot, back, early, tb, expand_weight, reduce_weight,
        (norm_gain, norm_shift, post_gain, post_shift, reduce_bias, expand_bias), modes, 1
    )
    plans = halving_plans(groups, shards, (dw1.shape[0], dw2.shape[0]))
    slab_grad, dwo, dbo, dwi, dbi, part1, part2, early = spectral_backward(
        mode_grad, tb, outer_weight, inner_weight, freq, hid, gp, t2, dw1, dw2, groups, plans, 2
    )
    small = (dwi, dwo, dbi, dbo, dpg, dps, deb, drb)
    input_grad, dwi, dwo, sums, norm, dw1, dw2 = leave(
        x, slab_grad, early, mixed_grad, tb["fl"], norm_gain, small, part1, part2,
        (dw1.shape, dw2.shape), inner_weight.shape, groups, plans, modes, 3
    )
    dw1 = jnp.concatenate([dw1[:width], dw1[width:]], 1).astype(F32)
    dw2 = dw2.astype(F32)
    small = small[2:]
    ends = np.cumsum([v.size // LANES for v in small])
    dbi, dbo, dpg, dps, deb, drb = [sums[e - v.size // LANES : e] for v, e in zip(small, ends)]
    line = lambda v: v.reshape(-1)
    return (
        layer_out[None], input_grad.reshape(1, rows, lon, width), norm[0], norm[1],
        dwi, dbi.reshape(inner_bias.shape), dwo, dbo.reshape(outer_bias.shape),
        line(dpg), line(dps), dw1, line(deb), dw2, line(drb),
    )


def solution(mesh):
    split = P("dp", "lat", None, None)
    return jax.shard_map(
        functools.partial(shards_fn, mesh.shape["dp"], mesh.shape["lat"]),
        mesh=mesh,
        in_specs=(split, split, P("dp")) + (P(),) * 12,
        out_specs=(split, split) + (P(),) * 12,
        check_vma=False,
    )
```
